32 devices in a mesh: parts: 2 (over y), row: 16 (over z, x, core).
Axes of the slice: x: 2, y: 2, z: 4, core: 2. Of those that a mesh axis runs over, the one named last changes fastest.
Arguments:
- traces: bfloat16 [256, 2, 12000], P(('parts', 'row')), parts along dimension 0, may hold values from -160 to 160
- valid_mask: int32 [256, 2], P(('parts', 'row')), parts along dimension 0, may hold values 0 or 1
- pair_table: int32 [32, 10], P(('parts', 'row')), parts along dimension 0, may hold values from 0 to 15, as said below
- stack_in: float32 [32, 10, 8, 8, 401], P(('parts', 'row')), parts along dimension 0, may hold values from -6 to 6
Outputs:
- stacks: float32 [32, 10, 8, 8, 401], P(('parts', 'row')), parts along dimension 0
The draws below stay inside these ranges and needn't reach their ends.
There are 2 independent parts, one for each index of `parts`. The reference program is written for one: setup_inputs(seed, part) draws one part's arguments, and reference() takes and returns one part's arrays. A program takes and returns all parts, laid end to end along the dimension named above; each array names one. Nothing has to cross between parts.
Inputs may be any that keep to these rules, and one draw needn't show every extreme that they name: `pair_table`: row i lists the panels (i + k) mod 16 for k = -1 to 8, each once, in an order that varies from row to row.
All inputs are finite; a program needn't handle non-finite values. No bound on the sum of `valid_mask` on one device may be relied on, other than what follows from the above.
Results may differ from the reference program's by a relative error of at most 0.0032.
Values may be sent and summed in bfloat16 or wider, within the bound.
No kernel may reach another device: no remote copies, remote signals or barrier semaphores. Data moves between devices by JAX's collectives and lax.ppermute only.
A program may use at most 128 MiB of HBM per device.

```python
import math
import jax
import jax.numpy as jnp
from jax import lax

CH_DEV = 8
SEGS = 2
SAMPLES = 12000
FLO = 6
BINS = 595
HALF = 40
LAGS = 401
CHANNELS = 128
OFFSETS = 10
N_ROW = 16


def draw_traces(key, part):
    base = jax.random.fold_in(key, 11)
    keys = jax.random.split(base, 5)
    noise = jax.random.truncated_normal(keys[0], -6.0, 6.0, (CHANNELS, SEGS, SAMPLES), jnp.float32)
    levels = jnp.exp(jax.random.uniform(keys[1], (CHANNELS, 1, 1), jnp.float32, 0.0, math.log(10.0)))
    tone_bins = jax.random.randint(keys[2], (CHANNELS, 4), FLO, FLO + BINS, dtype=jnp.int32)
    tone_sizes = jnp.exp(jax.random.uniform(keys[3], (CHANNELS, 4), jnp.float32, math.log(0.1), 0.0))
    tone_phase = jax.random.randint(keys[4], (CHANNELS, 4), 0, SAMPLES, dtype=jnp.int32)
    times = jnp.arange(SAMPLES, dtype=jnp.int32)
    signal = noise
    for number in range(4):
        index = (tone_bins[:, number, None] * times[None, :] + tone_phase[:, number, None]) % SAMPLES
        wave = tone_sizes[:, number, None] * jnp.sin(index.astype(jnp.float32) * (2.0 * math.pi / SAMPLES))
        signal = signal + wave[:, None, :]
    return (signal * levels).astype(jnp.bfloat16)


def draw_pair_table(key, part):
    base = jax.random.fold_in(key, 7)
    scores = jax.random.randint(base, (N_ROW, OFFSETS), 0, 1 << 20, dtype=jnp.int32) * OFFSETS
    scores = scores + jnp.arange(OFFSETS, dtype=jnp.int32)[None, :]
    order = jnp.argsort(scores, axis=1, stable=True).astype(jnp.int32)
    panels = jnp.arange(N_ROW, dtype=jnp.int32)[:, None]
    return ((panels + order - 1 + N_ROW) % N_ROW).astype(jnp.int32)


def set_ends(entries, key, least, largest):
    longest = entries.shape.index(max(entries.shape))
    spots = []
    for shift in (0, 1):
        where = [jax.random.randint(jax.random.fold_in(key, axis), (), 0, length) for axis, length in enumerate(entries.shape)]
        where[longest] = (where[longest] + shift) % entries.shape[longest]
        spots.append(tuple(where))
    return entries.at[spots[0]].set(least).at[spots[1]].set(largest)


def block_levels(own_key, dims, cuts, low, high):
    gain = 1.0
    for axis_at, shards_of in cuts:
        steps = jax.random.uniform(jax.random.fold_in(jax.random.fold_in(own_key, 6), axis_at), (shards_of,), jnp.float32, low / len(cuts), high / len(cuts))
        gain = gain * jnp.repeat(jnp.exp(steps), dims[axis_at] // shards_of).reshape((-1,) + (1,) * (len(dims) - 1 - axis_at))
    return gain


def normal_values(key, extent, width, limit, shards=(), kind=jnp.bfloat16):
    gain = block_levels(key, extent, shards, -0.22, 0.18) if shards else 1.0
    values = jax.random.normal(key, extent, jnp.float32) * width * gain
    return jnp.minimum(jnp.maximum(values, -limit), limit).astype(kind)


def setup_inputs(seed: int = 0, part: int = 0) -> dict:
    key_list = jax.random.split(jax.random.key(seed), 5)
    part_splits = jax.random.split(jax.random.fold_in(key_list[4], part), 5)
    return {
        "traces": draw_traces(jax.random.fold_in(jax.random.fold_in(key_list[4], part), 71), part),
        "valid_mask": set_ends((jax.random.randint(part_splits[1], (CHANNELS, SEGS), 0, 4) < 3).astype(jnp.int32), jax.random.fold_in(part_splits[1], 1), 0, 1),
        "pair_table": draw_pair_table(jax.random.fold_in(jax.random.fold_in(key_list[4], part), 71), part),
        "stack_in": normal_values(part_splits[3], (N_ROW, OFFSETS, CH_DEV, CH_DEV, LAGS), 1.0, 6.0, ((0, 16),), jnp.float32),
    }


epsilon = 1e-06

def spectra_of(rows, samples, first_bin, bins):
    length = samples // 8
    freq = first_bin + jnp.arange(bins, dtype=jnp.int32)

    def absorb(totals, block_index):
        first_row = block_index * length
        segment = lax.dynamic_slice_in_dim(rows, first_row, length, 1)
        times = first_row + jnp.arange(length, dtype=jnp.int32)
        angle = (times[:, None] * freq[None, :] % samples).astype(jnp.float32) * (2.0 * math.pi / samples)
        table = jnp.concatenate([jnp.cos(angle), -jnp.sin(angle)], axis=1).astype(jnp.bfloat16)
        return (totals + jnp.dot(segment, table, preferred_element_type=jnp.float32), None)
    start_total = jnp.zeros((rows.shape[0], 2 * bins), jnp.float32)
    totals, unused = lax.scan(absorb, start_total, jnp.arange(8, dtype=jnp.int32))
    return totals

def whiten_rows(traces, valid_mask, first_bin, bins, half_width):
    chans, minutes, samples = traces.shape
    spectrum = spectra_of(traces.reshape(chans * minutes, samples), samples, first_bin, bins)
    real_part = spectrum[:, :bins]
    imag_part = spectrum[:, bins:]
    power = real_part * real_part + imag_part * imag_part
    positions = jnp.arange(bins, dtype=jnp.int32)
    near = (jnp.abs(positions[:, None] - positions[None, :]) <= half_width).astype(jnp.float32)
    window = near / lax.optimization_barrier(jnp.sum(near, axis=0, keepdims=True))
    smooth = jnp.dot(power, window, precision=lax.Precision.HIGHEST)
    divisor = jnp.sqrt(smooth + epsilon)
    flags = valid_mask.reshape(-1, 1).astype(jnp.float32)
    whitened = spectrum * flags / jnp.concatenate([divisor, divisor], axis=1)
    return whitened.astype(jnp.bfloat16).reshape(chans, minutes, 2 * bins)

def lag_matrix(first_bin, bins, lags, samples):
    freq = first_bin + jnp.arange(bins, dtype=jnp.int32)
    shifts = jnp.arange(lags, dtype=jnp.int32) - (lags - 1) // 2
    angle = (freq[:, None] * shifts[None, :] % samples).astype(jnp.float32) * (2.0 * math.pi / samples)
    return jnp.concatenate([jnp.cos(angle), -jnp.sin(angle)], axis=0).astype(jnp.bfloat16)

def tile_corr(own_white, own_flags, partner_white, partner_flags, lag_table):
    bins = lag_table.shape[0] // 2
    own = own_white.astype(jnp.float32)
    partner = partner_white.astype(jnp.float32)
    shape = (partner.shape[0], own.shape[0], partner.shape[1], bins)
    real_sum = jnp.zeros(shape, jnp.float32)
    imag_sum = jnp.zeros(shape, jnp.float32)
    joint_sum = jnp.zeros(shape[:3], jnp.float32)
    for minute in range(own.shape[1]):
        own_real = own[:, minute, :bins][None, :, None, :]
        own_imag = own[:, minute, bins:][None, :, None, :]
        part_real = partner[:, :, minute, :bins][:, None, :, :]
        part_imag = partner[:, :, minute, bins:][:, None, :, :]
        real_sum = real_sum + (own_real * part_real + own_imag * part_imag)
        imag_sum = imag_sum + (own_imag * part_real - own_real * part_imag)
        own_valid = own_flags[:, minute].astype(jnp.float32)[None, :, None]
        part_valid = partner_flags[:, :, minute].astype(jnp.float32)[:, None, :]
        joint_sum = joint_sum + own_valid * part_valid
    inverse = 1.0 / jnp.maximum(joint_sum, 1.0)
    cross = (jnp.concatenate([real_sum, imag_sum], axis=-1) * inverse[..., None]).astype(jnp.bfloat16)
    corr = jnp.dot(cross.reshape(-1, 2 * bins), lag_table, preferred_element_type=jnp.float32) * (1.0 / math.sqrt(bins))
    return corr.reshape(shape[0], shape[1], shape[2], lag_table.shape[1])

def reference(traces, valid_mask, pair_table, stack_in):
    whitened = whiten_rows(traces, valid_mask, FLO, BINS, HALF)
    panels = whitened.reshape(N_ROW, CH_DEV, SEGS, 2 * BINS)
    panel_flags = valid_mask.reshape(N_ROW, CH_DEV, SEGS)
    lag_table = lag_matrix(FLO, BINS, LAGS, SAMPLES)

    def handle(panel_index):
        columns = pair_table[panel_index]
        partner = jnp.take(panels, columns, axis=0)
        partner_flags = jnp.take(panel_flags, columns, axis=0)
        corr = tile_corr(panels[panel_index], panel_flags[panel_index], partner, partner_flags, lag_table)
        return stack_in[panel_index] + corr
    return lax.map(handle, jnp.arange(N_ROW, dtype=jnp.int32))
```

```python
import math

import jax
import jax.numpy as jnp
import ml_dtypes
import numpy as np
from jax import lax
from jax.experimental import pallas as pl
from jax.experimental.pallas import tpu as pltpu
from jax.sharding import PartitionSpec as P

SAMPLES = 12000
FLO = 6
BINS = 595
HALF = 40
LAGS = 401
EPS = 1e-06

FOLD = SAMPLES // 10
LANES = 640
COLS = 512


def lane_bins():
    bins = np.full((LANES,), -1, np.int64)
    for group in range(5):
        for half in range(2):
            mine = [k for k in range(FLO, FLO + BINS) if k % 10 == group + 5 * half]
            start = group * 128 + half * 64
            bins[start : start + len(mine)] = mine
    return bins


BIN_OF = lane_bins()
USED = BIN_OF >= 0


def bf16(a):
    return np.asarray(a, np.float32).astype(ml_dtypes.bfloat16)


def fold_table():
    q = (np.arange(FOLD)[:, None] * BIN_OF[None, :]) % SAMPLES
    angle = 2.0 * np.pi * q / SAMPLES
    cos = np.where(USED, np.cos(angle), 0.0).reshape(FOLD, 5, 1, 128)
    sin = np.where(USED, -np.sin(angle), 0.0).reshape(FOLD, 5, 1, 128)
    table = np.concatenate([cos, sin], axis=2)
    order = [1, 4, 2, 3, 0]
    return bf16(table[:, order].reshape(FOLD, 5 * 256))


def near_table():
    gap = np.abs(BIN_OF[:, None] - BIN_OF[None, :])
    near = (gap <= HALF) & USED[:, None] & USED[None, :]
    count = np.maximum(near.sum(axis=0), 1)
    return bf16(near), (1.0 / count).astype(np.float32)[None, :]


def lag_table():
    tau = np.arange(LAGS) - (LAGS - 1) // 2
    q = (BIN_OF[:, None] * tau[None, :]) % SAMPLES
    angle = 2.0 * np.pi * q / SAMPLES
    table = np.zeros((2 * LANES, COLS), np.float64)
    table[:LANES, :LAGS] = np.where(USED[:, None], np.cos(angle), 0.0)
    table[LANES:, :LAGS] = np.where(USED[:, None], -np.sin(angle), 0.0)
    table[LANES - 1, COLS - 1] = 1.0
    return bf16(table)


C36, C72 = math.cos(math.pi / 5), math.cos(2 * math.pi / 5)
S36, S72 = math.sin(math.pi / 5), math.sin(2 * math.pi / 5)


def ten_point(s):
    e = [s[n] + s[n + 5] for n in range(5)]
    d = [s[n] - s[n + 5] for n in range(5)]
    e14, e23, f14, f23 = e[1] + e[4], e[2] + e[3], e[1] - e[4], e[2] - e[3]
    d14, d23, g14, g23 = d[1] + d[4], d[2] + d[3], d[1] - d[4], d[2] - d[3]
    y0 = e[0] + e14 + e23
    y2 = (e[0] + C72 * e14 - C36 * e23, -(S72 * f14 + S36 * f23))
    y4 = (e[0] - C36 * e14 + C72 * e23, -(S36 * f14 - S72 * f23))
    y1 = (d[0] + C36 * g14 + C72 * g23, -(S36 * d14 + S72 * d23))
    y3 = (d[0] - C72 * g14 - C36 * g23, -(S72 * d14 - S36 * d23))
    y5 = d[0] - g14 + g23
    return y0, y1, y2, y3, y4, y5


def hi_lo(y):
    hi = y.astype(jnp.bfloat16)
    return [hi, (y - hi.astype(jnp.float32)).astype(jnp.bfloat16)]


def whiten_kernel(x_ref, mask_ref, table_hbm, near_hbm, inv_ref, out_ref, table, near, sem):
    rows = x_ref.shape[0]
    parts = ((0, 512), (512, 512), (1024, 256))
    copies = [
        pltpu.make_async_copy(table_hbm.at[:, pl.ds(a, w)], table.at[:, pl.ds(a, w)], sem.at[i])
        for i, (a, w) in enumerate(parts)
    ] + [pltpu.make_async_copy(near_hbm, near, sem.at[3])]
    for c in copies:
        c.start()
    s = [x_ref[:, FOLD * n : FOLD * (n + 1)].astype(jnp.float32) for n in range(10)]
    y0, y1, y2, y3, y4, y5 = ten_point(s)
    lane = lax.broadcasted_iota(jnp.int32, (rows, 128), 1)
    lower = lane < 64
    real = [None] * 5
    imag = [None] * 5

    def product(ys, part):
        copies[part].wait()
        at, width = parts[part]
        left = jnp.concatenate([piece for y in ys for piece in hi_lo(y)], axis=0)
        full = jnp.dot(left, table[:, at : at + width], preferred_element_type=jnp.float32)
        return [
            full[2 * rows * i : 2 * rows * i + rows] + full[2 * rows * i + rows : 2 * rows * (i + 1)]
            for i in range(len(ys))
        ]

    for part, (ya, yb), groups in ((0, (y1, y4), (1, 4)), (1, (y2, y3), (2, 3))):
        pa, qa, pb, qb = product([ya[0], ya[1], yb[0], yb[1]], part)
        first, second = groups
        for group, at, (p0, q0, p1, q1) in ((first, 0, (pa, qa, pb, qb)), (second, 256, (pb, qb, pa, qa))):
            c, n = slice(at, at + 128), slice(at + 128, at + 256)
            real[group] = jnp.where(lower, p0[:, c] - q0[:, n], p1[:, c] + q1[:, n])
            imag[group] = jnp.where(lower, p0[:, n] + q0[:, c], p1[:, n] - q1[:, c])
    p0, p5 = product([y0, y5], 2)
    real[0] = jnp.where(lower, p0[:, :128], p5[:, :128])
    imag[0] = jnp.where(lower, p0[:, 128:], p5[:, 128:])
    re = jnp.concatenate(real, axis=1)
    im = jnp.concatenate(imag, axis=1)
    power = re * re + im * im
    hi, mid = hi_lo(power)
    low = (power - hi.astype(jnp.float32) - mid.astype(jnp.float32)).astype(jnp.bfloat16)
    copies[3].wait()
    sums = jnp.dot(jnp.concatenate([hi, mid, low], axis=0), near[...], preferred_element_type=jnp.float32)
    smooth = (sums[:rows] + sums[rows : 2 * rows] + sums[2 * rows :]) * inv_ref[...]
    chans = mask_ref.shape[1]
    mask = mask_ref[...].astype(jnp.float32)
    spread = jnp.concatenate(
        [jnp.broadcast_to(mask[i : i + 1], (chans, chans)) for i in range(mask_ref.shape[0])], axis=0
    )
    own = lax.broadcasted_iota(jnp.int32, (rows, chans), 0) % chans
    at = lax.broadcasted_iota(jnp.int32, (rows, chans), 1)
    flags = jnp.sum(jnp.where(own == at, spread, 0.0), axis=1, keepdims=True)
    factor = flags * lax.rsqrt(smooth + EPS)
    last = lax.broadcasted_iota(jnp.int32, (rows, LANES), 1) == LANES - 1
    out_ref[:, :LANES] = (re * factor).astype(jnp.bfloat16)
    out_ref[:, LANES:] = jnp.where(last, flags, im * factor).astype(jnp.bfloat16)


def whiten(traces, valid_mask):
    chans, minutes, samples = traces.shape
    rows = chans * minutes
    x = jnp.swapaxes(traces, 0, 1).reshape(rows, samples)
    near, inverse = near_table()
    vmem = pl.BlockSpec(memory_space=pltpu.VMEM)
    hbm = pl.BlockSpec(memory_space=pl.ANY)
    return pl.pallas_call(
        whiten_kernel,
        out_shape=jax.ShapeDtypeStruct((rows, 2 * LANES), jnp.bfloat16),
        in_specs=[vmem, vmem, hbm, hbm, vmem],
        out_specs=vmem,
        scratch_shapes=[
            pltpu.VMEM((FOLD, 5 * 256), jnp.bfloat16),
            pltpu.VMEM((LANES, LANES), jnp.bfloat16),
            pltpu.SemaphoreType.DMA((4,)),
        ],
        name="whiten",
    )(x, valid_mask.T, jnp.asarray(fold_table()), jnp.asarray(near), jnp.asarray(inverse))


def corr_kernel(slots_ref, own_ref, panels_ref, lag_ref, stack_ref, out_ref, cross):
    step = pl.program_id(0)
    count, chans = stack_ref.shape[0], stack_ref.shape[1]
    own = own_ref[...].astype(jnp.float32)
    minutes = own.shape[0] // chans
    for j in range(count):
        at = slots_ref[0, step * count + j]
        part = panels_ref[at].astype(jnp.float32)
        for a in range(0, chans, 2):
            both_re, both_im = [], []
            for channel in (a, a + 1):
                re = im = None
                for m in range(minutes):
                    row = m * chans + channel
                    o_re, o_im = own[row : row + 1, :LANES], own[row : row + 1, LANES:]
                    p_re = part[m * chans : (m + 1) * chans, :LANES]
                    p_im = part[m * chans : (m + 1) * chans, LANES:]
                    r = o_re * p_re + o_im * p_im
                    i = o_im * p_re - o_re * p_im
                    re = r if re is None else re + r
                    im = i if im is None else im + i
                both_re.append(re)
                both_im.append(im)
            rows = slice((j * chans + a) * chans, (j * chans + a + 2) * chans)
            cross[rows, :LANES] = jnp.concatenate(both_re, axis=0).astype(jnp.bfloat16)
            cross[rows, LANES:] = jnp.concatenate(both_im, axis=0).astype(jnp.bfloat16)
    full = jnp.dot(cross[...], lag_ref[...], preferred_element_type=jnp.float32)
    scale = (1.0 / math.sqrt(BINS)) / jnp.maximum(full[:, COLS - 1 :], 1.0)
    corr = (full * scale)[:, :LAGS].reshape(stack_ref.shape)
    out_ref[...] = stack_ref[...] + corr


def correlate(slots, own, panels, stack):
    offsets, chans = stack.shape[0], stack.shape[1]
    chunk = max(d for d in range(1, 7) if offsets % d == 0)
    rows, lanes = own.shape
    block = pl.BlockSpec((chunk, chans, chans, LAGS), lambda i, s: (i, 0, 0, 0))
    whole = pl.BlockSpec(memory_space=pltpu.VMEM)
    return pl.pallas_call(
        corr_kernel,
        out_shape=jax.ShapeDtypeStruct(stack.shape, jnp.float32),
        grid_spec=pltpu.PrefetchScalarGridSpec(
            num_scalar_prefetch=1,
            grid=(offsets // chunk,),
            in_specs=[whole, whole, whole, block],
            out_specs=block,
            scratch_shapes=[pltpu.VMEM((chunk * chans * chans, lanes), jnp.bfloat16)],
        ),
        name="correlate",
    )(slots, own, panels, jnp.asarray(lag_table()), stack)


def shards(traces, valid_mask, pair_table, stack_in):
    own = whiten(traces, valid_mask)
    panels = lax.all_gather(own, "row", axis=0)
    return correlate(pair_table, own, panels, stack_in[0])[None]


def solution(mesh):
    in_specs = (
        P(("parts", "row"), None, None),
        P(("parts", "row"), None),
        P(("parts", "row"), None),
        P(("parts", "row"), None, None, None, None),
    )
    out_specs = P(("parts", "row"), None, None, None, None)
    return jax.shard_map(shards, mesh=mesh, in_specs=in_specs, out_specs=out_specs, check_vma=False)
```

```python
import functools
import math

import jax
import jax.numpy as jnp
import ml_dtypes
import numpy as np
from jax import lax
from jax.experimental import pallas as pl
from jax.experimental.pallas import tpu as pltpu
from jax.sharding import PartitionSpec as P

SAMPLES = 12000
FLO = 6
BINS = 595
HALF = 40
LAGS = 401
EPS = 1e-06

FOLD = SAMPLES // 10
LANES = 640
COLS = 512


def lane_bins():
    bins = np.full((LANES,), -1, np.int64)
    for group in range(5):
        for half in range(2):
            mine = [k for k in range(FLO, FLO + BINS) if k % 10 == group + 5 * half]
            start = group * 128 + half * 64
            bins[start : start + len(mine)] = mine
    return bins


BIN_OF = lane_bins()
USED = BIN_OF >= 0


def bf16(a):
    return np.asarray(a, np.float32).astype(ml_dtypes.bfloat16)


def fold_table():
    q = (np.arange(FOLD)[:, None] * BIN_OF[None, :]) % SAMPLES
    angle = 2.0 * np.pi * q / SAMPLES
    cos = np.where(USED, np.cos(angle), 0.0).reshape(FOLD, 5, 1, 128)
    sin = np.where(USED, -np.sin(angle), 0.0).reshape(FOLD, 5, 1, 128)
    table = np.concatenate([cos, sin], axis=2)
    order = [1, 4, 2, 3, 0]
    return bf16(table[:, order].reshape(FOLD, 5 * 256))


def near_table():
    gap = np.abs(BIN_OF[:, None] - BIN_OF[None, :])
    near = (gap <= HALF) & USED[:, None] & USED[None, :]
    count = np.maximum(near.sum(axis=0), 1)
    return bf16(near), (1.0 / count).astype(np.float32)[None, :]


def lag_table():
    tau = np.arange(LAGS) - (LAGS - 1) // 2
    q = (BIN_OF[:, None] * tau[None, :]) % SAMPLES
    angle = 2.0 * np.pi * q / SAMPLES
    table = np.zeros((2 * LANES, COLS), np.float64)
    table[:LANES, :LAGS] = np.where(USED[:, None], np.cos(angle), 0.0)
    table[LANES:, :LAGS] = np.where(USED[:, None], -np.sin(angle), 0.0)
    table[LANES - 1, COLS - 1] = 1.0
    return bf16(table)


C36, C72 = math.cos(math.pi / 5), math.cos(2 * math.pi / 5)
S36, S72 = math.sin(math.pi / 5), math.sin(2 * math.pi / 5)


def ten_point(s):
    e = [s[n] + s[n + 5] for n in range(5)]
    d = [s[n] - s[n + 5] for n in range(5)]
    e14, e23, f14, f23 = e[1] + e[4], e[2] + e[3], e[1] - e[4], e[2] - e[3]
    d14, d23, g14, g23 = d[1] + d[4], d[2] + d[3], d[1] - d[4], d[2] - d[3]
    y0 = e[0] + e14 + e23
    y2 = (e[0] + C72 * e14 - C36 * e23, -(S72 * f14 + S36 * f23))
    y4 = (e[0] - C36 * e14 + C72 * e23, -(S36 * f14 - S72 * f23))
    y1 = (d[0] + C36 * g14 + C72 * g23, -(S36 * d14 + S72 * d23))
    y3 = (d[0] - C72 * g14 - C36 * g23, -(S72 * d14 - S36 * d23))
    y5 = d[0] - g14 + g23
    return y0, y1, y2, y3, y4, y5


def hi_lo(y):
    hi = y.astype(jnp.bfloat16)
    return [hi, (y - hi.astype(jnp.float32)).astype(jnp.bfloat16)]


def whiten_kernel(x_ref, mask_ref, table_hbm, near_hbm, inv_ref, out_ref, table, near, sem):
    rows = x_ref.shape[0]
    parts = ((0, 512), (512, 512), (1024, 256))
    copies = [
        pltpu.make_async_copy(table_hbm.at[:, pl.ds(a, w)], table.at[:, pl.ds(a, w)], sem.at[i])
        for i, (a, w) in enumerate(parts)
    ] + [pltpu.make_async_copy(near_hbm, near, sem.at[3])]
    for c in copies:
        c.start()
    s = [x_ref[:, FOLD * n : FOLD * (n + 1)].astype(jnp.float32) for n in range(10)]
    y0, y1, y2, y3, y4, y5 = ten_point(s)
    lane = lax.broadcasted_iota(jnp.int32, (rows, 128), 1)
    lower = lane < 64
    real = [None] * 5
    imag = [None] * 5

    def product(ys, part):
        copies[part].wait()
        at, width = parts[part]
        left = jnp.concatenate([piece for y in ys for piece in hi_lo(y)], axis=0)
        full = jnp.dot(left, table[:, at : at + width], preferred_element_type=jnp.float32)
        return [
            full[2 * rows * i : 2 * rows * i + rows] + full[2 * rows * i + rows : 2 * rows * (i + 1)]
            for i in range(len(ys))
        ]

    for part, (ya, yb), groups in ((0, (y1, y4), (1, 4)), (1, (y2, y3), (2, 3))):
        pa, qa, pb, qb = product([ya[0], ya[1], yb[0], yb[1]], part)
        first, second = groups
        for group, at, (p0, q0, p1, q1) in ((first, 0, (pa, qa, pb, qb)), (second, 256, (pb, qb, pa, qa))):
            c, n = slice(at, at + 128), slice(at + 128, at + 256)
            real[group] = jnp.where(lower, p0[:, c] - q0[:, n], p1[:, c] + q1[:, n])
            imag[group] = jnp.where(lower, p0[:, n] + q0[:, c], p1[:, n] - q1[:, c])
    p0, p5 = product([y0, y5], 2)
    real[0] = jnp.where(lower, p0[:, :128], p5[:, :128])
    imag[0] = jnp.where(lower, p0[:, 128:], p5[:, 128:])
    re = jnp.concatenate(real, axis=1)
    im = jnp.concatenate(imag, axis=1)
    power = re * re + im * im
    hi, mid = hi_lo(power)
    low = (power - hi.astype(jnp.float32) - mid.astype(jnp.float32)).astype(jnp.bfloat16)
    copies[3].wait()
    sums = jnp.dot(jnp.concatenate([hi, mid, low], axis=0), near[...], preferred_element_type=jnp.float32)
    smooth = (sums[:rows] + sums[rows : 2 * rows] + sums[2 * rows :]) * inv_ref[...]
    chans = mask_ref.shape[1]
    mask = mask_ref[...].astype(jnp.float32)
    spread = jnp.concatenate(
        [jnp.broadcast_to(mask[i : i + 1], (chans, chans)) for i in range(mask_ref.shape[0])], axis=0
    )
    own = lax.broadcasted_iota(jnp.int32, (rows, chans), 0) % chans
    at = lax.broadcasted_iota(jnp.int32, (rows, chans), 1)
    flags = jnp.sum(jnp.where(own == at, spread, 0.0), axis=1, keepdims=True)
    factor = flags * lax.rsqrt(smooth + EPS)
    last = lax.broadcasted_iota(jnp.int32, (rows, LANES), 1) == LANES - 1
    out_ref[:, :LANES] = (re * factor).astype(jnp.bfloat16)
    out_ref[:, LANES:] = jnp.where(last, flags, im * factor).astype(jnp.bfloat16)


def whiten(traces, valid_mask):
    chans, minutes, samples = traces.shape
    rows = chans * minutes
    x = jnp.swapaxes(traces, 0, 1).reshape(rows, samples)
    near, inverse = near_table()
    vmem = pl.BlockSpec(memory_space=pltpu.VMEM)
    hbm = pl.BlockSpec(memory_space=pl.ANY)
    return pl.pallas_call(
        whiten_kernel,
        out_shape=jax.ShapeDtypeStruct((rows, 2 * LANES), jnp.bfloat16),
        in_specs=[vmem, vmem, hbm, hbm, vmem],
        out_specs=vmem,
        scratch_shapes=[
            pltpu.VMEM((FOLD, 5 * 256), jnp.bfloat16),
            pltpu.VMEM((LANES, LANES), jnp.bfloat16),
            pltpu.SemaphoreType.DMA((4,)),
        ],
        name="whiten",
    )(x, valid_mask.T, jnp.asarray(fold_table()), jnp.asarray(near), jnp.asarray(inverse))


def corr_kernel(pick, slots_ref, own_ref, panels_ref, lag_ref, stack_ref, out_ref, cross):
    step = pl.program_id(0)
    count, chans = stack_ref.shape[0], stack_ref.shape[1]
    own = own_ref[...].astype(jnp.float32)
    minutes = own.shape[0] // chans
    for j in range(count):
        at = pick(slots_ref[0, step * count + j])
        part = panels_ref[at].astype(jnp.float32)
        for a in range(0, chans, 2):
            both_re, both_im = [], []
            for channel in (a, a + 1):
                re = im = None
                for m in range(minutes):
                    row = m * chans + channel
                    o_re, o_im = own[row : row + 1, :LANES], own[row : row + 1, LANES:]
                    p_re = part[m * chans : (m + 1) * chans, :LANES]
                    p_im = part[m * chans : (m + 1) * chans, LANES:]
                    r = o_re * p_re + o_im * p_im
                    i = o_im * p_re - o_re * p_im
                    re = r if re is None else re + r
                    im = i if im is None else im + i
                both_re.append(re)
                both_im.append(im)
            rows = slice((j * chans + a) * chans, (j * chans + a + 2) * chans)
            cross[rows, :LANES] = jnp.concatenate(both_re, axis=0).astype(jnp.bfloat16)
            cross[rows, LANES:] = jnp.concatenate(both_im, axis=0).astype(jnp.bfloat16)
    full = jnp.dot(cross[...], lag_ref[...], preferred_element_type=jnp.float32)
    scale = (1.0 / math.sqrt(BINS)) / jnp.maximum(full[:, COLS - 1 :], 1.0)
    corr = (full * scale)[:, :LAGS].reshape(stack_ref.shape)
    out_ref[...] = stack_ref[...] + corr


def correlate(pick, slots, own, panels, stack):
    offsets, chans = stack.shape[0], stack.shape[1]
    chunk = max(d for d in range(1, 7) if offsets % d == 0)
    rows, lanes = own.shape
    block = pl.BlockSpec((chunk, chans, chans, LAGS), lambda i, s: (i, 0, 0, 0))
    whole = pl.BlockSpec(memory_space=pltpu.VMEM)
    return pl.pallas_call(
        functools.partial(corr_kernel, pick),
        out_shape=jax.ShapeDtypeStruct(stack.shape, jnp.float32),
        grid_spec=pltpu.PrefetchScalarGridSpec(
            num_scalar_prefetch=1,
            grid=(offsets // chunk,),
            in_specs=[whole, whole, whole, block],
            out_specs=block,
            scratch_shapes=[pltpu.VMEM((chunk * chans * chans, lanes), jnp.bfloat16)],
        ),
        name="correlate",
    )(slots, own, panels, jnp.asarray(lag_table()), stack)


def share(own, panel_count, offsets):
    chips = panel_count // 2
    hops = (offsets + 1) // 2
    if panel_count % 2 or hops > 8 or hops + 2 > chips:
        return lax.all_gather(own, "row", axis=0), lambda j: j

    def fetch(far):
        shift = 2 * far
        return lax.ppermute(own, "row", [((i + shift) % panel_count, i) for i in range(panel_count)])

    mine = jnp.stack([own] + [fetch(far) for far in range(1, hops)] + [fetch(-1)])
    both = [[2 * c, 2 * c + 1] for c in range(chips)]
    panels = lax.all_gather(mine, "row", axis=0, tiled=True, axis_index_groups=both)

    def pick(j):
        base = (lax.axis_index("row") // 2) * 2
        ahead = lax.rem(j - base + panel_count, panel_count)
        far = ahead // 2
        place = jnp.where(far == chips - 1, hops, far)
        return lax.rem(ahead, 2) * (hops + 1) + place

    return panels, pick


def shards(traces, valid_mask, pair_table, stack_in):
    own = whiten(traces, valid_mask)
    panels, pick = share(own, lax.axis_size("row"), pair_table.shape[1])
    return correlate(pick, pair_table, own, panels, stack_in[0])[None]


def solution(mesh):
    in_specs = (
        P(("parts", "row"), None, None),
        P(("parts", "row"), None),
        P(("parts", "row"), None),
        P(("parts", "row"), None, None, None, None),
    )
    out_specs = P(("parts", "row"), None, None, None, None)
    return jax.shard_map(shards, mesh=mesh, in_specs=in_specs, out_specs=out_specs, check_vma=False)
```

```python
import functools
import math

import jax
import jax.numpy as jnp
import ml_dtypes
import numpy as np
from jax import lax
from jax.experimental import pallas as pl
from jax.experimental.pallas import tpu as pltpu
from jax.sharding import PartitionSpec as P

SAMPLES = 12000
FLO = 6
BINS = 595
HALF = 40
LAGS = 401
EPS = 1e-06
WHITEN_VMEM = 60 << 20
CORR_VMEM = 24 << 20

SPLIT = 20
FOLD = SAMPLES // SPLIT
LANES = 640
RUN = 32
COLS = 512


def bin_at(lane):
    residue = lane // 128 + 5 * (lane % 128 // RUN)
    return residue + SPLIT * (residue < FLO) + SPLIT * (lane % RUN)


BIN_OF = bin_at(np.arange(LANES))
USED = BIN_OF < FLO + BINS
GROUPS = ((1, 4), (2, 3), (0,))


def bf16(a):
    return np.asarray(a, np.float32).astype(ml_dtypes.bfloat16)


def fold_table():
    q = (np.arange(FOLD)[:, None] * BIN_OF[None, :]) % SAMPLES
    angle = 2.0 * np.pi * q / SAMPLES
    cos = np.where(USED, np.cos(angle), 0.0).reshape(FOLD, 5, 1, 128)
    sin = np.where(USED, -np.sin(angle), 0.0).reshape(FOLD, 5, 1, 128)
    table = np.concatenate([cos, sin], axis=2)
    order = [group for some in GROUPS for group in some]
    return bf16(table[:, order].reshape(FOLD, 5 * 256))


def lag_table():
    tau = np.arange(LAGS) - (LAGS - 1) // 2
    q = (BIN_OF[:, None] * tau[None, :]) % SAMPLES
    angle = 2.0 * np.pi * q / SAMPLES
    table = np.zeros((2 * LANES, COLS), np.float64)
    table[:LANES, :LAGS] = np.where(USED[:, None], np.cos(angle), 0.0)
    table[LANES:, :LAGS] = np.where(USED[:, None], -np.sin(angle), 0.0)
    table[LANES - 1, COLS - 1] = 1.0
    return bf16(table)


def cosine(n, of):
    return math.cos(2.0 * math.pi * n / of)


def sine(n, of):
    return math.sin(2.0 * math.pi * n / of)


def ten_point(s):
    e = [s[n] + s[n + 5] for n in range(5)]
    d = [s[n] - s[n + 5] for n in range(5)]
    c1, c2, s1, s2 = cosine(1, 10), cosine(2, 10), sine(1, 10), sine(2, 10)
    e14, e23, f14, f23 = e[1] + e[4], e[2] + e[3], e[1] - e[4], e[2] - e[3]
    d14, d23, g14, g23 = d[1] + d[4], d[2] + d[3], d[1] - d[4], d[2] - d[3]
    y0 = (e[0] + e14 + e23, None)
    y2 = (e[0] + c2 * e14 - c1 * e23, -(s2 * f14 + s1 * f23))
    y4 = (e[0] - c1 * e14 + c2 * e23, -(s1 * f14 - s2 * f23))
    y1 = (d[0] + c1 * g14 + c2 * g23, -(s1 * d14 + s2 * d23))
    y3 = (d[0] - c2 * g14 - c1 * g23, -(s2 * d14 - s1 * d23))
    y5 = (d[0] - g14 + g23, None)
    return [y0, y1, y2, y3, y4, y5]


def twenty_point(s):
    y = [None] * 11
    y[0::2] = ten_point([s[n] + s[n + 10] for n in range(10)])
    d = [s[n] - s[n + 10] for n in range(10)]
    g = [d[n] - d[10 - n] for n in range(1, 5)]
    h = [d[n] + d[10 - n] for n in range(1, 5)]
    for k in (1, 3, 5, 7, 9):
        real, imag = d[0], -sine(5 * k, 20) * d[5]
        for n in range(1, 5):
            real = real + cosine(n * k % 20, 20) * g[n - 1]
            imag = imag - sine(n * k % 20, 20) * h[n - 1]
        y[k] = (real, imag)
    return y


def hi_lo(y):
    hi = y.astype(jnp.bfloat16)
    return [hi, (y - hi.astype(jnp.float32)).astype(jnp.bfloat16)]


def whiten_kernel(x_hbm, mask_hbm, table_hbm, out_ref, x_buf, mask_buf, table, near, sem):
    chans, minutes, samples = x_buf.shape
    rows = chans * minutes
    starts = (0, 512, 1024, 1280)
    fetch_x = pltpu.make_async_copy(x_hbm, x_buf, sem.at[0])
    fetch_mask = pltpu.make_async_copy(mask_hbm, mask_buf, sem.at[1])
    fetch_table = [
        pltpu.make_async_copy(table_hbm.at[:, pl.ds(a, b - a)], table.at[:, pl.ds(a, b - a)], sem.at[2 + i])
        for i, (a, b) in enumerate(zip(starts, starts[1:]))
    ]
    for copy in [fetch_x, fetch_mask] + fetch_table:
        copy.start()

    down = bin_at(lax.broadcasted_iota(jnp.int32, (LANES, 128), 0))
    down = jnp.where(down < FLO + BINS, down, -SAMPLES)
    lanes = bin_at(lax.broadcasted_iota(jnp.int32, (8, LANES), 1))
    for group in range(5):
        across = jnp.broadcast_to(lanes[:1, group * 128 : (group + 1) * 128], (LANES, 128))
        close = (jnp.abs(down - across) <= HALF) & (across < FLO + BINS)
        near[:, group * 128 : (group + 1) * 128] = jnp.where(close, 1.0, 0.0).astype(jnp.bfloat16)
    bins = lanes[:1]
    count = jnp.minimum(bins + HALF, FLO + BINS - 1) - jnp.maximum(bins - HALF, FLO) + 1
    inverse = 1.0 / jnp.maximum(count, 1).astype(jnp.float32)

    fetch_x.wait()
    x = jnp.swapaxes(x_buf[...], 0, 1).reshape(rows, samples)
    y = twenty_point([x[:, FOLD * n : FOLD * (n + 1)].astype(jnp.float32) for n in range(SPLIT)])
    run = lax.broadcasted_iota(jnp.int32, (rows, 128), 1) // RUN
    for copy in [fetch_mask] + fetch_table:
        copy.wait()
    real = [None] * 5
    imag = [None] * 5
    for part, groups in enumerate(GROUPS):
        wanted = sorted({min(k, SPLIT - k) for g in groups for k in range(g, SPLIT, 5)})
        pieces = [(k, i) for k in wanted for i in range(2) if y[k][i] is not None]
        left = jnp.concatenate([p for k, i in pieces for p in hi_lo(y[k][i])], axis=0)
        at = starts[part]
        full = jnp.dot(left, table[:, at : starts[part + 1]], preferred_element_type=jnp.float32)
        got = {
            p: full[2 * rows * i : 2 * rows * i + rows] + full[2 * rows * i + rows : 2 * rows * (i + 1)]
            for i, p in enumerate(pieces)
        }
        for place, group in enumerate(groups):
            cos = slice(place * 256, place * 256 + 128)
            sin = slice(place * 256 + 128, place * 256 + 256)
            re = im = None
            for q in range(4):
                k = group + 5 * q
                same = min(k, SPLIT - k)
                a = got[(same, 0)]
                r, i = a[:, cos], a[:, sin]
                if (same, 1) in got:
                    b = got[(same, 1)] if k == same else -got[(same, 1)]
                    r, i = r - b[:, sin], i + b[:, cos]
                re = r if re is None else jnp.where(run == q, r, re)
                im = i if im is None else jnp.where(run == q, i, im)
            real[group], imag[group] = re, im
    re = jnp.concatenate(real, axis=1)
    im = jnp.concatenate(imag, axis=1)
    power = re * re + im * im
    hi, mid = hi_lo(power)
    low = (power - hi.astype(jnp.float32) - mid.astype(jnp.float32)).astype(jnp.bfloat16)
    sums = jnp.dot(jnp.concatenate([hi, mid, low], axis=0), near[...], preferred_element_type=jnp.float32)
    smooth = (sums[:rows] + sums[rows : 2 * rows] + sums[2 * rows :]) * inverse
    mask = mask_buf[...].astype(jnp.float32)
    spread = jnp.concatenate([jnp.broadcast_to(mask[m : m + 1], (chans, chans)) for m in range(minutes)], axis=0)
    own = lax.broadcasted_iota(jnp.int32, (rows, chans), 0) % chans
    other = lax.broadcasted_iota(jnp.int32, (rows, chans), 1)
    flags = jnp.sum(jnp.where(own == other, spread, 0.0), axis=1, keepdims=True)
    factor = flags * lax.rsqrt(smooth + EPS)
    last = lax.broadcasted_iota(jnp.int32, (rows, LANES), 1) == LANES - 1
    out_ref[:, :LANES] = (re * factor).astype(jnp.bfloat16)
    out_ref[:, LANES:] = jnp.where(last, flags, im * factor).astype(jnp.bfloat16)


def whiten(traces, valid_mask):
    chans, minutes, samples = traces.shape
    rows = chans * minutes
    anywhere = pl.BlockSpec(memory_space=pltpu.HBM)
    return pl.pallas_call(
        whiten_kernel,
        out_shape=jax.ShapeDtypeStruct((rows, 2 * LANES), jnp.bfloat16),
        in_specs=[anywhere] * 3,
        out_specs=pl.BlockSpec(memory_space=pltpu.VMEM),
        scratch_shapes=[
            pltpu.VMEM((chans, minutes, samples), jnp.bfloat16),
            pltpu.VMEM((minutes, chans), jnp.int32),
            pltpu.VMEM((FOLD, 5 * 256), jnp.bfloat16),
            pltpu.VMEM((LANES, LANES), jnp.bfloat16),
            pltpu.SemaphoreType.DMA((5,)),
        ],
        compiler_params=pltpu.CompilerParams(vmem_limit_bytes=WHITEN_VMEM),
        name="whiten",
    )(traces, valid_mask.T, jnp.asarray(fold_table()))


def corr_kernel(pick, slots_ref, panels_ref, lag_ref, stack_ref, out_ref, cross):
    step = pl.program_id(0)
    count, chans = out_ref.shape[0], out_ref.shape[1]
    own = panels_ref[pick(lax.axis_index("row"))].astype(jnp.float32)
    minutes = own.shape[0] // chans
    for j in range(count):
        part = panels_ref[pick(slots_ref[0, step * count + j])].astype(jnp.float32)
        for a in range(0, chans, 2):
            both_re, both_im = [], []
            for channel in (a, a + 1):
                re = im = None
                for m in range(minutes):
                    row = m * chans + channel
                    o_re, o_im = own[row : row + 1, :LANES], own[row : row + 1, LANES:]
                    p_re = part[m * chans : (m + 1) * chans, :LANES]
                    p_im = part[m * chans : (m + 1) * chans, LANES:]
                    r = o_re * p_re + o_im * p_im
                    i = o_im * p_re - o_re * p_im
                    re = r if re is None else re + r
                    im = i if im is None else im + i
                both_re.append(re)
                both_im.append(im)
            rows = slice((j * chans + a) * chans, (j * chans + a + 2) * chans)
            cross[rows, :LANES] = jnp.concatenate(both_re, axis=0).astype(jnp.bfloat16)
            cross[rows, LANES:] = jnp.concatenate(both_im, axis=0).astype(jnp.bfloat16)
    full = jnp.dot(cross[...], lag_ref[...], preferred_element_type=jnp.float32)
    scale = (1.0 / math.sqrt(BINS)) / jnp.maximum(full[:, COLS - 1 :], 1.0)
    corr = (full * scale)[:, :LAGS].reshape(out_ref.shape)
    out_ref[...] = stack_ref[pl.ds(step * count, count)] + corr


def correlate(pick, slots, panels, stack):
    offsets, chans = stack.shape[0], stack.shape[1]
    chunk = max(d for d in range(1, 7) if offsets % d == 0)
    whole = pl.BlockSpec(memory_space=pltpu.VMEM)
    return pl.pallas_call(
        functools.partial(corr_kernel, pick),
        out_shape=jax.ShapeDtypeStruct(stack.shape, jnp.float32),
        grid_spec=pltpu.PrefetchScalarGridSpec(
            num_scalar_prefetch=1,
            grid=(offsets // chunk,),
            in_specs=[whole, whole, whole],
            out_specs=pl.BlockSpec((chunk, chans, chans, LAGS), lambda i, s: (i, 0, 0, 0)),
            scratch_shapes=[pltpu.VMEM((chunk * chans * chans, panels.shape[2]), jnp.bfloat16)],
        ),
        compiler_params=pltpu.CompilerParams(vmem_limit_bytes=CORR_VMEM),
        name="correlate",
    )(slots, panels, jnp.asarray(lag_table()), stack)


def share(own, panel_count, offsets):
    chips = panel_count // 2
    hops = (offsets + 1) // 2
    if panel_count % 2 or hops > 8 or hops + 2 > chips:
        return lax.all_gather(own, "row", axis=0), lambda j: j

    def fetch(far):
        shift = 2 * far
        return lax.ppermute(own, "row", [((i + shift) % panel_count, i) for i in range(panel_count)])

    mine = jnp.stack([own] + [fetch(far) for far in range(1, hops)] + [fetch(-1)])
    both = [[2 * c, 2 * c + 1] for c in range(chips)]
    panels = lax.all_gather(mine, "row", axis=0, tiled=True, axis_index_groups=both)

    def pick(j):
        base = (lax.axis_index("row") // 2) * 2
        ahead = lax.rem(j - base + panel_count, panel_count)
        far = ahead // 2
        place = jnp.where(far == chips - 1, hops, far)
        return lax.rem(ahead, 2) * (hops + 1) + place

    return panels, pick


def shards(traces, valid_mask, pair_table, stack_in):
    own = whiten(traces, valid_mask)
    panels, pick = share(own, lax.axis_size("row"), pair_table.shape[1])
    return correlate(pick, pair_table, panels, stack_in[0])[None]


def solution(mesh):
    in_specs = (
        P(("parts", "row"), None, None),
        P(("parts", "row"), None),
        P(("parts", "row"), None),
        P(("parts", "row"), None, None, None, None),
    )
    out_specs = P(("parts", "row"), None, None, None, None)
    return jax.shard_map(shards, mesh=mesh, in_specs=in_specs, out_specs=out_specs, check_vma=False)
```

```python
import functools
import math

import jax
import jax.numpy as jnp
import ml_dtypes
import numpy as np
from jax import lax
from jax.experimental import pallas as pl
from jax.experimental.pallas import tpu as pltpu
from jax.sharding import PartitionSpec as P

SAMPLES = 12000
FLO = 6
BINS = 595
HALF = 40
LAGS = 401
EPS = 1e-06
WHITEN_VMEM = 60 << 20
CORR_VMEM = 24 << 20

SPLIT = 20
FOLD = SAMPLES // SPLIT
LANES = 640
RUN = 32
COLS = 512


def bin_at(lane):
    residue = lane // 128 + 5 * (lane % 128 // RUN)
    return residue + SPLIT * (residue < FLO) + SPLIT * (lane % RUN)


BIN_OF = bin_at(np.arange(LANES))
USED = BIN_OF < FLO + BINS
GROUPS = ((1, 4), (2, 3), (0,))


def bf16(a):
    return np.asarray(a, np.float32).astype(ml_dtypes.bfloat16)


def fold_table():
    q = (np.arange(FOLD)[:, None] * BIN_OF[None, :]) % SAMPLES
    angle = 2.0 * np.pi * q / SAMPLES
    cos = np.where(USED, np.cos(angle), 0.0).reshape(FOLD, 5, 1, 128)
    sin = np.where(USED, -np.sin(angle), 0.0).reshape(FOLD, 5, 1, 128)
    table = np.concatenate([cos, sin], axis=2)
    order = [group for some in GROUPS for group in some]
    return bf16(table[:, order].reshape(FOLD, 5 * 256))


def lag_table():
    tau = np.arange(LAGS) - (LAGS - 1) // 2
    q = (BIN_OF[:, None] * tau[None, :]) % SAMPLES
    angle = 2.0 * np.pi * q / SAMPLES
    table = np.zeros((2 * LANES, COLS), np.float64)
    table[:LANES, :LAGS] = np.where(USED[:, None], np.cos(angle), 0.0)
    table[LANES:, :LAGS] = np.where(USED[:, None], -np.sin(angle), 0.0)
    table[LANES - 1, COLS - 1] = 1.0
    return bf16(table)


def cosine(n, of):
    return math.cos(2.0 * math.pi * n / of)


def sine(n, of):
    return math.sin(2.0 * math.pi * n / of)


def ten_point(s):
    e = [s[n] + s[n + 5] for n in range(5)]
    d = [s[n] - s[n + 5] for n in range(5)]
    c1, c2, s1, s2 = cosine(1, 10), cosine(2, 10), sine(1, 10), sine(2, 10)
    e14, e23, f14, f23 = e[1] + e[4], e[2] + e[3], e[1] - e[4], e[2] - e[3]
    d14, d23, g14, g23 = d[1] + d[4], d[2] + d[3], d[1] - d[4], d[2] - d[3]
    y0 = (e[0] + e14 + e23, None)
    y2 = (e[0] + c2 * e14 - c1 * e23, -(s2 * f14 + s1 * f23))
    y4 = (e[0] - c1 * e14 + c2 * e23, -(s1 * f14 - s2 * f23))
    y1 = (d[0] + c1 * g14 + c2 * g23, -(s1 * d14 + s2 * d23))
    y3 = (d[0] - c2 * g14 - c1 * g23, -(s2 * d14 - s1 * d23))
    y5 = (d[0] - g14 + g23, None)
    return [y0, y1, y2, y3, y4, y5]


def twenty_point(s):
    y = [None] * 11
    y[0::2] = ten_point([s[n] + s[n + 10] for n in range(10)])
    d = [s[n] - s[n + 10] for n in range(10)]
    g = [d[n] - d[10 - n] for n in range(1, 5)]
    h = [d[n] + d[10 - n] for n in range(1, 5)]
    for k in (1, 3, 5, 7, 9):
        real, imag = d[0], -sine(5 * k, 20) * d[5]
        for n in range(1, 5):
            real = real + cosine(n * k % 20, 20) * g[n - 1]
            imag = imag - sine(n * k % 20, 20) * h[n - 1]
        y[k] = (real, imag)
    return y


def hi_lo(y):
    hi = y.astype(jnp.bfloat16)
    return [hi, (y - hi.astype(jnp.float32)).astype(jnp.bfloat16)]


def whiten_kernel(x_hbm, mask_hbm, table_hbm, out_ref, x_buf, mask_buf, table, near, sem):
    chans, minutes, samples = x_buf.shape
    rows = chans * minutes
    starts = (0, 512, 1024, 1280)
    fetch_x = pltpu.make_async_copy(x_hbm, x_buf, sem.at[0])
    fetch_mask = pltpu.make_async_copy(mask_hbm, mask_buf, sem.at[1])
    fetch_table = [
        pltpu.make_async_copy(table_hbm.at[:, pl.ds(a, b - a)], table.at[:, pl.ds(a, b - a)], sem.at[2 + i])
        for i, (a, b) in enumerate(zip(starts, starts[1:]))
    ]
    for copy in [fetch_x, fetch_mask] + fetch_table:
        copy.start()

    down = bin_at(lax.broadcasted_iota(jnp.int32, (LANES, 128), 0))
    down = jnp.where(down < FLO + BINS, down, -SAMPLES)
    lanes = bin_at(lax.broadcasted_iota(jnp.int32, (8, LANES), 1))
    for group in range(5):
        across = jnp.broadcast_to(lanes[:1, group * 128 : (group + 1) * 128], (LANES, 128))
        close = (jnp.abs(down - across) <= HALF) & (across < FLO + BINS)
        near[:, group * 128 : (group + 1) * 128] = jnp.where(close, 1.0, 0.0).astype(jnp.bfloat16)
    bins = lanes[:1]
    count = jnp.minimum(bins + HALF, FLO + BINS - 1) - jnp.maximum(bins - HALF, FLO) + 1
    inverse = 1.0 / jnp.maximum(count, 1).astype(jnp.float32)

    fetch_x.wait()
    x = jnp.swapaxes(x_buf[...], 0, 1).reshape(rows, samples)
    y = twenty_point([x[:, FOLD * n : FOLD * (n + 1)].astype(jnp.float32) for n in range(SPLIT)])
    run = lax.broadcasted_iota(jnp.int32, (rows, 128), 1) // RUN
    for copy in [fetch_mask] + fetch_table:
        copy.wait()
    real = [None] * 5
    imag = [None] * 5
    for part, groups in enumerate(GROUPS):
        wanted = sorted({min(k, SPLIT - k) for g in groups for k in range(g, SPLIT, 5)})
        pieces = [(k, i) for k in wanted for i in range(2) if y[k][i] is not None]
        left = jnp.concatenate([p for k, i in pieces for p in hi_lo(y[k][i])], axis=0)
        at = starts[part]
        full = jnp.dot(left, table[:, at : starts[part + 1]], preferred_element_type=jnp.float32)
        got = {
            p: full[2 * rows * i : 2 * rows * i + rows] + full[2 * rows * i + rows : 2 * rows * (i + 1)]
            for i, p in enumerate(pieces)
        }
        for place, group in enumerate(groups):
            cos = slice(place * 256, place * 256 + 128)
            sin = slice(place * 256 + 128, place * 256 + 256)
            re = im = None
            for q in range(4):
                k = group + 5 * q
                same = min(k, SPLIT - k)
                a = got[(same, 0)]
                r, i = a[:, cos], a[:, sin]
                if (same, 1) in got:
                    b = got[(same, 1)] if k == same else -got[(same, 1)]
                    r, i = r - b[:, sin], i + b[:, cos]
                re = r if re is None else jnp.where(run == q, r, re)
                im = i if im is None else jnp.where(run == q, i, im)
            real[group], imag[group] = re, im
    re = jnp.concatenate(real, axis=1)
    im = jnp.concatenate(imag, axis=1)
    power = re * re + im * im
    hi, mid = hi_lo(power)
    low = (power - hi.astype(jnp.float32) - mid.astype(jnp.float32)).astype(jnp.bfloat16)
    sums = jnp.dot(jnp.concatenate([hi, mid, low], axis=0), near[...], preferred_element_type=jnp.float32)
    smooth = (sums[:rows] + sums[rows : 2 * rows] + sums[2 * rows :]) * inverse
    mask = mask_buf[...].astype(jnp.float32)
    spread = jnp.concatenate([jnp.broadcast_to(mask[m : m + 1], (chans, chans)) for m in range(minutes)], axis=0)
    own = lax.broadcasted_iota(jnp.int32, (rows, chans), 0) % chans
    other = lax.broadcasted_iota(jnp.int32, (rows, chans), 1)
    flags = jnp.sum(jnp.where(own == other, spread, 0.0), axis=1, keepdims=True)
    factor = flags * lax.rsqrt(smooth + EPS)
    last = lax.broadcasted_iota(jnp.int32, (rows, LANES), 1) == LANES - 1
    out_ref[:, :LANES] = (re * factor).astype(jnp.bfloat16)
    out_ref[:, LANES:] = jnp.where(last, flags, im * factor).astype(jnp.bfloat16)


def whiten(traces, valid_mask):
    chans, minutes, samples = traces.shape
    rows = chans * minutes
    anywhere = pl.BlockSpec(memory_space=pltpu.HBM)
    return pl.pallas_call(
        whiten_kernel,
        out_shape=jax.ShapeDtypeStruct((rows, 2 * LANES), jnp.bfloat16),
        in_specs=[anywhere] * 3,
        out_specs=pl.BlockSpec(memory_space=pltpu.VMEM),
        scratch_shapes=[
            pltpu.VMEM((chans, minutes, samples), jnp.bfloat16),
            pltpu.VMEM((minutes, chans), jnp.int32),
            pltpu.VMEM((FOLD, 5 * 256), jnp.bfloat16),
            pltpu.VMEM((LANES, LANES), jnp.bfloat16),
            pltpu.SemaphoreType.DMA((5,)),
        ],
        compiler_params=pltpu.CompilerParams(vmem_limit_bytes=WHITEN_VMEM),
        name="whiten",
    )(traces, valid_mask.T, jnp.asarray(fold_table()))


def cross_tile(own, part, chans, cross, j):
    minutes = own.shape[0] // chans
    for a in range(0, chans, 2):
        both_re, both_im = [], []
        for channel in (a, a + 1):
            re = im = None
            for m in range(minutes):
                row = m * chans + channel
                o_re, o_im = own[row : row + 1, :LANES], own[row : row + 1, LANES:]
                p_re = part[m * chans : (m + 1) * chans, :LANES]
                p_im = part[m * chans : (m + 1) * chans, LANES:]
                r = o_re * p_re + o_im * p_im
                i = o_im * p_re - o_re * p_im
                re = r if re is None else re + r
                im = i if im is None else im + i
            both_re.append(re)
            both_im.append(im)
        rows = slice((j * chans + a) * chans, (j * chans + a + 2) * chans)
        cross[rows, :LANES] = jnp.concatenate(both_re, axis=0).astype(jnp.bfloat16)
        cross[rows, LANES:] = jnp.concatenate(both_im, axis=0).astype(jnp.bfloat16)


def lag_product(cross, table, shape):
    full = jnp.dot(cross, table, preferred_element_type=jnp.float32)
    scale = (1.0 / math.sqrt(BINS)) / jnp.maximum(full[:, COLS - 1 :], 1.0)
    return (full * scale)[:, :LAGS].reshape(shape)


def corr_kernel(pick, slots_ref, panels_ref, lag_ref, stack_ref, out_ref, cross):
    step = pl.program_id(0)
    count, chans = out_ref.shape[0], out_ref.shape[1]
    own = panels_ref[pick(lax.axis_index("row"))].astype(jnp.float32)
    for j in range(count):
        part = panels_ref[pick(slots_ref[0, step * count + j])].astype(jnp.float32)
        cross_tile(own, part, chans, cross, j)
    corr = lag_product(cross[...], lag_ref[...], out_ref.shape)
    out_ref[...] = stack_ref[pl.ds(step * count, count)] + corr


def correlate(pick, slots, panels, stack):
    offsets, chans = stack.shape[0], stack.shape[1]
    chunk = max(d for d in range(1, 7) if offsets % d == 0)
    whole = pl.BlockSpec(memory_space=pltpu.VMEM)
    return pl.pallas_call(
        functools.partial(corr_kernel, pick),
        out_shape=jax.ShapeDtypeStruct(stack.shape, jnp.float32),
        grid_spec=pltpu.PrefetchScalarGridSpec(
            num_scalar_prefetch=1,
            grid=(offsets // chunk,),
            in_specs=[whole, whole, whole],
            out_specs=pl.BlockSpec((chunk, chans, chans, LAGS), lambda i, s: (i, 0, 0, 0)),
            scratch_shapes=[pltpu.VMEM((chunk * chans * chans, panels.shape[2]), jnp.bfloat16)],
        ),
        compiler_params=pltpu.CompilerParams(vmem_limit_bytes=CORR_VMEM),
        name="correlate",
    )(slots, panels, jnp.asarray(lag_table()), stack)


def gather_all(own, slots, stack):
    panels = lax.all_gather(own, "row", axis=0)
    return correlate(lambda j: j, slots, panels, stack)


def place(panel_count):
    me = lax.axis_index("row")
    return me, me // 2, lax.rem(me, 2), lax.rem(me // 2, 2)


def first_hop(panel_count):
    me, chip, core, odd = place(panel_count)
    a = jnp.where(core == 0, chip + 1 - 2 * odd, chip + 2)
    b = jnp.where(core == 0, chip - 1 + 4 * odd, chip + 3 - 2 * odd)
    return a, b


def pair_panels(panel_count):
    me, chip, core, odd = place(panel_count)
    return [(0, 2 * chip, True), (1, 2 * chip + 1, True)]


def near_panels(panel_count):
    me, chip, core, odd = place(panel_count)
    a, b = first_hop(panel_count)
    return [(0, 2 * a, True), (1, 2 * a + 1, True), (2, 2 * b, True), (3, 2 * b + 1, True), (4, me + 8, True)]


def swapped_panels(panel_count):
    me, chip, core, odd = place(panel_count)
    low = 2 * odd * core
    found = []
    for t in range(2):
        ahead = jnp.where(core == 0, chip + 2, chip + 1 + 2 * odd)
        found.append((low + t, 2 * ahead + t, True))
    for t in range(2):
        ahead = 2 * (chip + 3 - 2 * odd) + t
        found.append((jnp.where(core == 0, 2 + t, 4), jnp.where(core == 0, ahead, 2 * chip + 8), (core == 0) | (t == 0)))
    return found


def tiles_kernel(panel_count, which, fresh, *refs):
    slots_ref, pair_ref, panels_ref, lag_ref, stack_ref = refs[:5]
    out_ref, cross, result, sem = refs[5 if fresh else 6 :]
    offsets, chans = stack_ref.shape[0], stack_ref.shape[1]
    me = lax.axis_index("row")
    own = pair_ref[lax.rem(me, 2)].astype(jnp.float32)
    found = which(panel_count)
    todo = []
    for j, (at, panel, wanted) in enumerate(found):
        panel = lax.rem(panel + panel_count, panel_count)
        valid = (lax.rem(panel - me + 1 + panel_count, panel_count) < offsets) & wanted
        slot = jnp.int32(0)
        for o in range(1, offsets):
            slot = jnp.where(slots_ref[0, o] == panel, o, slot)
        todo.append((at, slot, valid))
    copies = []
    for start in range(0, len(found), 2):
        some = todo[start : start + 2]
        for j, (at, slot, valid) in enumerate(some):
            cross_tile(own, panels_ref[at].astype(jnp.float32), chans, cross, start + j)
        rows = slice(start * chans * chans, (start + len(some)) * chans * chans)
        corr = lag_product(cross[rows], lag_ref[...], (len(some), chans, chans, LAGS))
        for j, (at, slot, valid) in enumerate(some):
            result[start + j] = stack_ref[slot] + corr[j]
            copies.append((valid, pltpu.make_async_copy(result.at[start + j], out_ref.at[slot], sem.at[start + j])))
            pl.when(valid)(copies[-1][1].start)
    for valid, copy in copies:
        pl.when(valid)(copy.wait)


def tiles(which, count, panel_count, slots, pair, panels, table, stack, out=None):
    offsets, chans = stack.shape[0], stack.shape[1]
    whole = pl.BlockSpec(memory_space=pltpu.VMEM)
    hbm = pl.BlockSpec(memory_space=pltpu.HBM)
    rows = count * chans * chans
    return pl.pallas_call(
        functools.partial(tiles_kernel, panel_count, which, out is None),
        out_shape=jax.ShapeDtypeStruct(stack.shape, jnp.float32),
        in_specs=[pl.BlockSpec(memory_space=pltpu.SMEM), whole, whole, whole, whole] + ([] if out is None else [hbm]),
        out_specs=hbm,
        scratch_shapes=[
            pltpu.VMEM((rows, 2 * LANES), jnp.bfloat16),
            pltpu.VMEM((count, chans, chans, LAGS), jnp.float32),
            pltpu.SemaphoreType.DMA((count,)),
        ],
        input_output_aliases={} if out is None else {5: 0},
        compiler_params=pltpu.CompilerParams(vmem_limit_bytes=CORR_VMEM),
        cost_estimate=pl.CostEstimate(flops=4 * rows * LANES * COLS, bytes_accessed=4 * rows * COLS, transcendentals=0),
        name=which.__name__,
    )(slots, pair, panels, table, stack, *([] if out is None else [out]))


def gather_near(own, slots, stack, panel_count):
    chips = panel_count // 2
    pair = lax.all_gather(own, "row", axis=0, axis_index_groups=[[2 * c, 2 * c + 1] for c in range(chips)])

    def fetch(array, even, odd):
        ahead = [even, odd]
        moves = []
        for i in range(panel_count):
            c = i // 2
            moves.append((2 * ((c + ahead[i % 2][c % 2]) % chips) + i % 2, i))
        return lax.ppermute(array, "row", moves)

    table = jnp.asarray(lag_table())
    near = fetch(pair, (1, -1), (2, 2))
    next_near = fetch(pair, (-1, 3), (3, 1))
    far = fetch(own, (4, 4), (4, 4))
    out = tiles(pair_panels, 2, panel_count, slots, pair, pair, table, stack)
    near, next_near, far, out = lax.optimization_barrier((near, next_near, far, out))
    five = jnp.concatenate([near, next_near, far[None]], axis=0)
    swapped = lax.ppermute(five, "row", [(i ^ 1, i) for i in range(panel_count)])
    out = tiles(near_panels, 5, panel_count, slots, pair, five, table, stack, out)
    return tiles(swapped_panels, 4, panel_count, slots, pair, swapped, table, stack, out)


def shards(traces, valid_mask, pair_table, stack_in):
    own = whiten(traces, valid_mask)
    panel_count = lax.axis_size("row")
    if pair_table.shape[1] == 10 and panel_count >= 12 and panel_count % 4 == 0:
        return gather_near(own, pair_table, stack_in[0], panel_count)[None]
    return gather_all(own, pair_table, stack_in[0])[None]


def solution(mesh):
    in_specs = (
        P(("parts", "row"), None, None),
        P(("parts", "row"), None),
        P(("parts", "row"), None),
        P(("parts", "row"), None, None, None, None),
    )
    out_specs = P(("parts", "row"), None, None, None, None)
    return jax.shard_map(shards, mesh=mesh, in_specs=in_specs, out_specs=out_specs, check_vma=False)
```

```python
import functools
import math

import jax
import jax.numpy as jnp
import ml_dtypes
import numpy as np
from jax import lax
from jax.experimental import pallas as pl
from jax.experimental.pallas import tpu as pltpu
from jax.sharding import PartitionSpec as P

SAMPLES = 12000
FLO = 6
BINS = 595
SEGS = 2
HALF = 40
LAGS = 401
EPS = 1e-06
WHITEN_VMEM = 60 << 20
CORR_VMEM = 24 << 20

SPLIT = 20
FOLD = SAMPLES // SPLIT
LANES = 640
RUN = 32
COLS = 512


def bin_at(lane):
    residue = lane // 128 + 5 * (lane % 128 // RUN)
    return residue + SPLIT * (residue < FLO) + SPLIT * (lane % RUN)


BIN_OF = bin_at(np.arange(LANES))
USED = BIN_OF < FLO + BINS
GROUPS = ((1, 4), (2, 3), (0,))


def bf16(a):
    return np.asarray(a, np.float32).astype(ml_dtypes.bfloat16)


def fold_table():
    q = (np.arange(FOLD)[:, None] * BIN_OF[None, :]) % SAMPLES
    angle = 2.0 * np.pi * q / SAMPLES
    cos = np.where(USED, np.cos(angle), 0.0).reshape(FOLD, 5, 1, 128)
    sin = np.where(USED, -np.sin(angle), 0.0).reshape(FOLD, 5, 1, 128)
    table = np.concatenate([cos, sin], axis=2)
    order = [group for some in GROUPS for group in some]
    return bf16(table[:, order].reshape(FOLD, 5 * 256))


def lag_table():
    tau = np.arange(LAGS) - (LAGS - 1) // 2
    q = (BIN_OF[:, None] * tau[None, :]) % SAMPLES
    angle = 2.0 * np.pi * q / SAMPLES
    table = np.zeros((2 * LANES, COLS), np.float64)
    table[:LANES, :LAGS] = np.where(USED[:, None], np.cos(angle), 0.0)
    table[LANES:, :LAGS] = np.where(USED[:, None], -np.sin(angle), 0.0)
    table[LANES - 1, COLS - 1] = 1.0
    return bf16(table)


def cosine(n, of):
    return math.cos(2.0 * math.pi * n / of)


def sine(n, of):
    return math.sin(2.0 * math.pi * n / of)


def ten_point(s):
    e = [s[n] + s[n + 5] for n in range(5)]
    d = [s[n] - s[n + 5] for n in range(5)]
    c1, c2, s1, s2 = cosine(1, 10), cosine(2, 10), sine(1, 10), sine(2, 10)
    e14, e23, f14, f23 = e[1] + e[4], e[2] + e[3], e[1] - e[4], e[2] - e[3]
    d14, d23, g14, g23 = d[1] + d[4], d[2] + d[3], d[1] - d[4], d[2] - d[3]
    y0 = (e[0] + e14 + e23, None)
    y2 = (e[0] + c2 * e14 - c1 * e23, -(s2 * f14 + s1 * f23))
    y4 = (e[0] - c1 * e14 + c2 * e23, -(s1 * f14 - s2 * f23))
    y1 = (d[0] + c1 * g14 + c2 * g23, -(s1 * d14 + s2 * d23))
    y3 = (d[0] - c2 * g14 - c1 * g23, -(s2 * d14 - s1 * d23))
    y5 = (d[0] - g14 + g23, None)
    return [y0, y1, y2, y3, y4, y5]


def twenty_point(s):
    y = [None] * 11
    y[0::2] = ten_point([s[n] + s[n + 10] for n in range(10)])
    d = [s[n] - s[n + 10] for n in range(10)]
    g = [d[n] - d[10 - n] for n in range(1, 5)]
    h = [d[n] + d[10 - n] for n in range(1, 5)]
    for k in (1, 3, 5, 7, 9):
        real, imag = d[0], -sine(5 * k, 20) * d[5]
        for n in range(1, 5):
            real = real + cosine(n * k % 20, 20) * g[n - 1]
            imag = imag - sine(n * k % 20, 20) * h[n - 1]
        y[k] = (real, imag)
    return y


def hi_lo(y):
    hi = y.astype(jnp.bfloat16)
    return [hi, (y - hi.astype(jnp.float32)).astype(jnp.bfloat16)]


def whiten_kernel(x_hbm, mask_hbm, table_hbm, out_ref, x_buf, mask_buf, table, near, sem):
    chans, minutes, samples = x_buf.shape
    rows = chans * minutes
    starts = (0, 512, 1024, 1280)
    fetch_x = pltpu.make_async_copy(x_hbm, x_buf, sem.at[0])
    fetch_mask = pltpu.make_async_copy(mask_hbm, mask_buf, sem.at[1])
    fetch_table = [
        pltpu.make_async_copy(table_hbm.at[:, pl.ds(a, b - a)], table.at[:, pl.ds(a, b - a)], sem.at[2 + i])
        for i, (a, b) in enumerate(zip(starts, starts[1:]))
    ]
    for copy in [fetch_x, fetch_mask] + fetch_table:
        copy.start()

    down = bin_at(lax.broadcasted_iota(jnp.int32, (LANES, 128), 0))
    down = jnp.where(down < FLO + BINS, down, -SAMPLES)
    lanes = bin_at(lax.broadcasted_iota(jnp.int32, (8, LANES), 1))
    for group in range(5):
        across = jnp.broadcast_to(lanes[:1, group * 128 : (group + 1) * 128], (LANES, 128))
        close = (jnp.abs(down - across) <= HALF) & (across < FLO + BINS)
        near[:, group * 128 : (group + 1) * 128] = jnp.where(close, 1.0, 0.0).astype(jnp.bfloat16)
    bins = lanes[:1]
    count = jnp.minimum(bins + HALF, FLO + BINS - 1) - jnp.maximum(bins - HALF, FLO) + 1
    inverse = 1.0 / jnp.maximum(count, 1).astype(jnp.float32)

    fetch_x.wait()
    x = jnp.swapaxes(x_buf[...], 0, 1).reshape(rows, samples)
    y = twenty_point([x[:, FOLD * n : FOLD * (n + 1)].astype(jnp.float32) for n in range(SPLIT)])
    run = lax.broadcasted_iota(jnp.int32, (rows, 128), 1) // RUN
    for copy in [fetch_mask] + fetch_table:
        copy.wait()
    real = [None] * 5
    imag = [None] * 5
    for part, groups in enumerate(GROUPS):
        wanted = sorted({min(k, SPLIT - k) for g in groups for k in range(g, SPLIT, 5)})
        pieces = [(k, i) for k in wanted for i in range(2) if y[k][i] is not None]
        left = jnp.concatenate([p for k, i in pieces for p in hi_lo(y[k][i])], axis=0)
        at = starts[part]
        full = jnp.dot(left, table[:, at : starts[part + 1]], preferred_element_type=jnp.float32)
        got = {
            p: full[2 * rows * i : 2 * rows * i + rows] + full[2 * rows * i + rows : 2 * rows * (i + 1)]
            for i, p in enumerate(pieces)
        }
        for place, group in enumerate(groups):
            cos = slice(place * 256, place * 256 + 128)
            sin = slice(place * 256 + 128, place * 256 + 256)
            re = im = None
            for q in range(4):
                k = group + 5 * q
                same = min(k, SPLIT - k)
                a = got[(same, 0)]
                r, i = a[:, cos], a[:, sin]
                if (same, 1) in got:
                    b = got[(same, 1)] if k == same else -got[(same, 1)]
                    r, i = r - b[:, sin], i + b[:, cos]
                re = r if re is None else jnp.where(run == q, r, re)
                im = i if im is None else jnp.where(run == q, i, im)
            real[group], imag[group] = re, im
    re = jnp.concatenate(real, axis=1)
    im = jnp.concatenate(imag, axis=1)
    power = re * re + im * im
    hi, mid = hi_lo(power)
    low = (power - hi.astype(jnp.float32) - mid.astype(jnp.float32)).astype(jnp.bfloat16)
    sums = jnp.dot(jnp.concatenate([hi, mid, low], axis=0), near[...], preferred_element_type=jnp.float32)
    smooth = (sums[:rows] + sums[rows : 2 * rows] + sums[2 * rows :]) * inverse
    mask = mask_buf[...].astype(jnp.float32)
    spread = jnp.concatenate([jnp.broadcast_to(mask[m : m + 1], (chans, chans)) for m in range(minutes)], axis=0)
    own = lax.broadcasted_iota(jnp.int32, (rows, chans), 0) % chans
    other = lax.broadcasted_iota(jnp.int32, (rows, chans), 1)
    flags = jnp.sum(jnp.where(own == other, spread, 0.0), axis=1, keepdims=True)
    factor = flags * lax.rsqrt(smooth + EPS)
    last = lax.broadcasted_iota(jnp.int32, (rows, LANES), 1) == LANES - 1
    out_ref[:, :LANES] = (re * factor).astype(jnp.bfloat16)
    out_ref[:, LANES:] = jnp.where(last, flags, im * factor).astype(jnp.bfloat16)


def whiten(traces, valid_mask):
    chans, minutes, samples = traces.shape
    rows = chans * minutes
    anywhere = pl.BlockSpec(memory_space=pltpu.HBM)
    return pl.pallas_call(
        whiten_kernel,
        out_shape=jax.ShapeDtypeStruct((rows, 2 * LANES), jnp.bfloat16),
        in_specs=[anywhere] * 3,
        out_specs=pl.BlockSpec(memory_space=pltpu.VMEM),
        scratch_shapes=[
            pltpu.VMEM((chans, minutes, samples), jnp.bfloat16),
            pltpu.VMEM((minutes, chans), jnp.int32),
            pltpu.VMEM((FOLD, 5 * 256), jnp.bfloat16),
            pltpu.VMEM((LANES, LANES), jnp.bfloat16),
            pltpu.SemaphoreType.DMA((5,)),
        ],
        compiler_params=pltpu.CompilerParams(vmem_limit_bytes=WHITEN_VMEM),
        name="whiten",
    )(traces, valid_mask.T, jnp.asarray(fold_table()))


def cross_tile(own, part, chans, cross, j):
    minutes = own.shape[0] // chans
    for a in range(0, chans, 2):
        both_re, both_im = [], []
        for channel in (a, a + 1):
            re = im = None
            for m in range(minutes):
                row = m * chans + channel
                o_re, o_im = own[row : row + 1, :LANES], own[row : row + 1, LANES:]
                p_re = part[m * chans : (m + 1) * chans, :LANES]
                p_im = part[m * chans : (m + 1) * chans, LANES:]
                r = o_re * p_re + o_im * p_im
                i = o_im * p_re - o_re * p_im
                re = r if re is None else re + r
                im = i if im is None else im + i
            both_re.append(re)
            both_im.append(im)
        rows = slice((j * chans + a) * chans, (j * chans + a + 2) * chans)
        cross[rows, :LANES] = jnp.concatenate(both_re, axis=0).astype(jnp.bfloat16)
        cross[rows, LANES:] = jnp.concatenate(both_im, axis=0).astype(jnp.bfloat16)


def lag_product(cross, table, shape):
    full = jnp.dot(cross, table, preferred_element_type=jnp.float32)
    scale = (1.0 / math.sqrt(BINS)) / jnp.maximum(full[:, COLS - 1 :], 1.0)
    return (full * scale)[:, :LAGS].reshape(shape)


def corr_kernel(pick, slots_ref, panels_ref, lag_ref, stack_ref, out_ref, cross):
    step = pl.program_id(0)
    count, chans = out_ref.shape[0], out_ref.shape[1]
    own = panels_ref[pick(lax.axis_index("row"))].astype(jnp.float32)
    for j in range(count):
        part = panels_ref[pick(slots_ref[0, step * count + j])].astype(jnp.float32)
        cross_tile(own, part, chans, cross, j)
    corr = lag_product(cross[...], lag_ref[...], out_ref.shape)
    out_ref[...] = stack_ref[pl.ds(step * count, count)] + corr


def correlate(pick, slots, panels, stack):
    offsets, chans = stack.shape[0], stack.shape[1]
    chunk = max(d for d in range(1, 7) if offsets % d == 0)
    whole = pl.BlockSpec(memory_space=pltpu.VMEM)
    return pl.pallas_call(
        functools.partial(corr_kernel, pick),
        out_shape=jax.ShapeDtypeStruct(stack.shape, jnp.float32),
        grid_spec=pltpu.PrefetchScalarGridSpec(
            num_scalar_prefetch=1,
            grid=(offsets // chunk,),
            in_specs=[whole, whole, whole],
            out_specs=pl.BlockSpec((chunk, chans, chans, LAGS), lambda i, s: (i, 0, 0, 0)),
            scratch_shapes=[pltpu.VMEM((chunk * chans * chans, panels.shape[2]), jnp.bfloat16)],
        ),
        compiler_params=pltpu.CompilerParams(vmem_limit_bytes=CORR_VMEM),
        name="correlate",
    )(slots, panels, jnp.asarray(lag_table()), stack)


def gather_all(own, slots, stack):
    panels = lax.all_gather(own, "row", axis=0)
    return correlate(lambda j: j, slots, panels, stack)


def place(panel_count):
    me = lax.axis_index("row")
    return me, me // 2, lax.rem(me, 2), lax.rem(me // 2, 2)


def first_hop(panel_count):
    me, chip, core, odd = place(panel_count)
    a = jnp.where(core == 0, chip + 1 - 2 * odd, chip + 2)
    b = jnp.where(core == 0, chip - 1 + 4 * odd, chip + 3 - 2 * odd)
    return a, b


def pair_panels(panel_count):
    me, chip, core, odd = place(panel_count)
    return [(0, 2 * chip, True), (1, 2 * chip + 1, True)]


def near_panels(panel_count):
    me, chip, core, odd = place(panel_count)
    a, b = first_hop(panel_count)
    return [(0, 2 * a, True), (1, 2 * a + 1, True), (2, 2 * b, True), (3, 2 * b + 1, True), (4, me + 8, True)]


def swapped_panels(panel_count):
    me, chip, core, odd = place(panel_count)
    low = 2 * odd * core
    found = []
    for t in range(2):
        ahead = jnp.where(core == 0, chip + 2, chip + 1 + 2 * odd)
        found.append((low + t, 2 * ahead + t, True))
    for t in range(2):
        ahead = 2 * (chip + 3 - 2 * odd) + t
        found.append((jnp.where(core == 0, 2 + t, 4), jnp.where(core == 0, ahead, 2 * chip + 8), (core == 0) | (t == 0)))
    return found


def products(which, panel_count, own, panels_ref, table, chans, cross, keep):
    found = which(panel_count)
    for start in range(0, len(found), 2):
        some = found[start : start + 2]
        for j, (at, panel, wanted) in enumerate(some):
            cross_tile(own, panels_ref[at].astype(jnp.float32), chans, cross, start + j)
        rows = slice(start * chans * chans, (start + len(some)) * chans * chans)
        full = jnp.dot(cross[rows], table, preferred_element_type=jnp.float32)
        scale = (1.0 / math.sqrt(BINS)) / jnp.maximum(full[:, COLS - 1 :], 1.0)
        keep(start, (full * scale).reshape(len(some), chans * chans, COLS))


def early_kernel(panel_count, which, pair_ref, panels_ref, table_ref, out_ref, cross):
    own = pair_ref[lax.rem(lax.axis_index("row"), 2)].astype(jnp.float32)

    def keep(start, corr):
        out_ref[start : start + corr.shape[0]] = corr

    products(which, panel_count, own, panels_ref, table_ref[...], own.shape[0] // SEGS, cross, keep)


def early(which, count, panel_count, chans, pair, panels, table):
    whole = pl.BlockSpec(memory_space=pltpu.VMEM)
    rows = count * chans * chans
    return pl.pallas_call(
        functools.partial(early_kernel, panel_count, which),
        out_shape=jax.ShapeDtypeStruct((count, chans * chans, COLS), jnp.float32),
        in_specs=[whole] * 3,
        out_specs=whole,
        scratch_shapes=[pltpu.VMEM((rows, 2 * LANES), jnp.bfloat16)],
        compiler_params=pltpu.CompilerParams(vmem_limit_bytes=CORR_VMEM),
        cost_estimate=pl.CostEstimate(flops=4 * rows * LANES * COLS, bytes_accessed=4 * rows * COLS, transcendentals=0),
        name=which.__name__,
    )(pair, panels, table)


def last_kernel(panel_count, lists, slots_ref, pair_ref, panels_ref, table_ref, stack_ref, *refs):
    done_refs = refs[: len(lists) - 1]
    out_ref, cross, result, sem = refs[len(lists) - 1 :]
    offsets, chans = stack_ref.shape[0], stack_ref.shape[1]
    me = lax.axis_index("row")
    copies = []

    def finish(found, corr):
        for j, (at, panel, wanted) in enumerate(found):
            panel = lax.rem(panel + panel_count, panel_count)
            valid = (lax.rem(panel - me + 1 + panel_count, panel_count) < offsets) & wanted
            slot = jnp.int32(0)
            for o in range(1, offsets):
                slot = jnp.where(slots_ref[0, o] == panel, o, slot)
            n = len(copies)
            result[n] = stack_ref[slot] + corr[j][:, :LAGS].reshape(chans, chans, LAGS)
            copy = pltpu.make_async_copy(result.at[n], out_ref.at[slot], sem.at[n])
            copies.append((valid, copy))
            pl.when(valid)(copy.start)

    for which, done in zip(lists, done_refs):
        finish(which(panel_count), done)
    own = pair_ref[lax.rem(me, 2)].astype(jnp.float32)
    found = lists[-1](panel_count)

    def keep(start, corr):
        finish(found[start : start + corr.shape[0]], corr)

    products(lists[-1], panel_count, own, panels_ref, table_ref[...], chans, cross, keep)
    for valid, copy in copies:
        pl.when(valid)(copy.wait)


def last(lists, counts, panel_count, slots, pair, panels, table, stack, *done):
    offsets, chans = stack.shape[0], stack.shape[1]
    whole = pl.BlockSpec(memory_space=pltpu.VMEM)
    rows = counts[-1] * chans * chans
    return pl.pallas_call(
        functools.partial(last_kernel, panel_count, lists),
        out_shape=jax.ShapeDtypeStruct(stack.shape, jnp.float32),
        in_specs=[pl.BlockSpec(memory_space=pltpu.SMEM)] + [whole] * (4 + len(done)),
        out_specs=pl.BlockSpec(memory_space=pltpu.HBM),
        scratch_shapes=[
            pltpu.VMEM((rows, 2 * LANES), jnp.bfloat16),
            pltpu.VMEM((sum(counts), chans, chans, LAGS), jnp.float32),
            pltpu.SemaphoreType.DMA((sum(counts),)),
        ],
        compiler_params=pltpu.CompilerParams(vmem_limit_bytes=CORR_VMEM),
        cost_estimate=pl.CostEstimate(flops=4 * rows * LANES * COLS, bytes_accessed=4 * rows * COLS, transcendentals=0),
        name=lists[-1].__name__,
    )(slots, pair, panels, table, stack, *done)


def gather_near(own, slots, stack, panel_count):
    chips = panel_count // 2
    pair = lax.all_gather(own, "row", axis=0, axis_index_groups=[[2 * c, 2 * c + 1] for c in range(chips)])

    def fetch(array, even, odd):
        ahead = [even, odd]
        moves = []
        for i in range(panel_count):
            c = i // 2
            moves.append((2 * ((c + ahead[i % 2][c % 2]) % chips) + i % 2, i))
        return lax.ppermute(array, "row", moves)

    table = jnp.asarray(lag_table())
    near = fetch(pair, (1, -1), (2, 2))
    next_near = fetch(pair, (-1, 3), (3, 1))
    far = fetch(own, (4, 4), (4, 4))
    chans = stack.shape[1]
    first = early(pair_panels, 2, panel_count, chans, pair, pair, table)
    near, next_near, far, first = lax.optimization_barrier((near, next_near, far, first))
    five = jnp.concatenate([near, next_near, far[None]], axis=0)
    swapped = lax.ppermute(five, "row", [(i ^ 1, i) for i in range(panel_count)])
    second = early(near_panels, 5, panel_count, chans, pair, five, table)
    lists = (pair_panels, near_panels, swapped_panels)
    return last(lists, (2, 5, 4), panel_count, slots, pair, swapped, table, stack, first, second)


def shards(traces, valid_mask, pair_table, stack_in):
    own = whiten(traces, valid_mask)
    panel_count = lax.axis_size("row")
    if pair_table.shape[1] == 10 and panel_count >= 12 and panel_count % 4 == 0:
        return gather_near(own, pair_table, stack_in[0], panel_count)[None]
    return gather_all(own, pair_table, stack_in[0])[None]


def solution(mesh):
    in_specs = (
        P(("parts", "row"), None, None),
        P(("parts", "row"), None),
        P(("parts", "row"), None),
        P(("parts", "row"), None, None, None, None),
    )
    out_specs = P(("parts", "row"), None, None, None, None)
    return jax.shard_map(shards, mesh=mesh, in_specs=in_specs, out_specs=out_specs, check_vma=False)
```

```python
import functools
import math

import jax
import jax.numpy as jnp
import ml_dtypes
import numpy as np
from jax import lax
from jax.experimental import pallas as pl
from jax.experimental.pallas import tpu as pltpu
from jax.sharding import PartitionSpec as P

SAMPLES = 12000
FLO = 6
BINS = 595
SEGS = 2
HALF = 40
LAGS = 401
EPS = 1e-06
WHITEN_VMEM = 60 << 20
CORR_VMEM = 24 << 20

SPLIT = 20
FOLD = SAMPLES // SPLIT
LANES = 640
RUN = 32
COLS = 512


def bin_at(lane):
    residue = lane // 128 + 5 * (lane % 128 // RUN)
    return residue + SPLIT * (residue < FLO) + SPLIT * (lane % RUN)


BIN_OF = bin_at(np.arange(LANES))
USED = BIN_OF < FLO + BINS
GROUPS = ((1, 4), (2, 3), (0,))


def bf16(a):
    return np.asarray(a, np.float32).astype(ml_dtypes.bfloat16)


def fold_table():
    q = (np.arange(FOLD)[:, None] * BIN_OF[None, :]) % SAMPLES
    angle = 2.0 * np.pi * q / SAMPLES
    cos = np.where(USED, np.cos(angle), 0.0).reshape(FOLD, 5, 1, 128)
    sin = np.where(USED, -np.sin(angle), 0.0).reshape(FOLD, 5, 1, 128)
    table = np.concatenate([cos, sin], axis=2)
    order = [group for some in GROUPS for group in some]
    return bf16(table[:, order].reshape(FOLD, 5 * 256))


def lag_table():
    tau = np.arange(LAGS) - (LAGS - 1) // 2
    q = (BIN_OF[:, None] * tau[None, :]) % SAMPLES
    angle = 2.0 * np.pi * q / SAMPLES
    table = np.zeros((2 * LANES, COLS), np.float64)
    table[:LANES, :LAGS] = np.where(USED[:, None], np.cos(angle), 0.0)
    table[LANES:, :LAGS] = np.where(USED[:, None], -np.sin(angle), 0.0)
    table[LANES - 1, COLS - 1] = 1.0
    return bf16(table)


def cosine(n, of):
    return math.cos(2.0 * math.pi * n / of)


def sine(n, of):
    return math.sin(2.0 * math.pi * n / of)


def ten_point(s):
    e = [s[n] + s[n + 5] for n in range(5)]
    d = [s[n] - s[n + 5] for n in range(5)]
    c1, c2, s1, s2 = cosine(1, 10), cosine(2, 10), sine(1, 10), sine(2, 10)
    e14, e23, f14, f23 = e[1] + e[4], e[2] + e[3], e[1] - e[4], e[2] - e[3]
    d14, d23, g14, g23 = d[1] + d[4], d[2] + d[3], d[1] - d[4], d[2] - d[3]
    y0 = (e[0] + e14 + e23, None)
    y2 = (e[0] + c2 * e14 - c1 * e23, -(s2 * f14 + s1 * f23))
    y4 = (e[0] - c1 * e14 + c2 * e23, -(s1 * f14 - s2 * f23))
    y1 = (d[0] + c1 * g14 + c2 * g23, -(s1 * d14 + s2 * d23))
    y3 = (d[0] - c2 * g14 - c1 * g23, -(s2 * d14 - s1 * d23))
    y5 = (d[0] - g14 + g23, None)
    return [y0, y1, y2, y3, y4, y5]


def twenty_point(s):
    y = [None] * 11
    y[0::2] = ten_point([s[n] + s[n + 10] for n in range(10)])
    d = [s[n] - s[n + 10] for n in range(10)]
    g = [d[n] - d[10 - n] for n in range(1, 5)]
    h = [d[n] + d[10 - n] for n in range(1, 5)]
    for k in (1, 3, 5, 7, 9):
        real, imag = d[0], -sine(5 * k, 20) * d[5]
        for n in range(1, 5):
            real = real + cosine(n * k % 20, 20) * g[n - 1]
            imag = imag - sine(n * k % 20, 20) * h[n - 1]
        y[k] = (real, imag)
    return y


def hi_lo(y):
    hi = y.astype(jnp.bfloat16)
    return [hi, (y - hi.astype(jnp.float32)).astype(jnp.bfloat16)]


def whiten_kernel(x_hbm, mask_hbm, table_hbm, out_ref, x_buf, mask_buf, table, near, sem):
    chans, minutes, samples = x_buf.shape
    rows = chans * minutes
    starts = (0, 512, 1024, 1280)
    fetch_x = pltpu.make_async_copy(x_hbm, x_buf, sem.at[0])
    fetch_mask = pltpu.make_async_copy(mask_hbm, mask_buf, sem.at[1])
    fetch_table = [
        pltpu.make_async_copy(table_hbm.at[:, pl.ds(a, b - a)], table.at[:, pl.ds(a, b - a)], sem.at[2 + i])
        for i, (a, b) in enumerate(zip(starts, starts[1:]))
    ]
    for copy in [fetch_x, fetch_mask] + fetch_table:
        copy.start()

    down = bin_at(lax.broadcasted_iota(jnp.int32, (LANES, 128), 0))
    down = jnp.where(down < FLO + BINS, down, -SAMPLES)
    lanes = bin_at(lax.broadcasted_iota(jnp.int32, (8, LANES), 1))
    for group in range(5):
        across = jnp.broadcast_to(lanes[:1, group * 128 : (group + 1) * 128], (LANES, 128))
        close = (jnp.abs(down - across) <= HALF) & (across < FLO + BINS)
        near[:, group * 128 : (group + 1) * 128] = jnp.where(close, 1.0, 0.0).astype(jnp.bfloat16)
    bins = lanes[:1]
    count = jnp.minimum(bins + HALF, FLO + BINS - 1) - jnp.maximum(bins - HALF, FLO) + 1
    inverse = 1.0 / jnp.maximum(count, 1).astype(jnp.float32)

    fetch_x.wait()
    x = jnp.swapaxes(x_buf[...], 0, 1).reshape(rows, samples)
    y = twenty_point([x[:, FOLD * n : FOLD * (n + 1)].astype(jnp.float32) for n in range(SPLIT)])
    run = lax.broadcasted_iota(jnp.int32, (rows, 128), 1) // RUN
    for copy in [fetch_mask] + fetch_table:
        copy.wait()
    real = [None] * 5
    imag = [None] * 5
    for part, groups in enumerate(GROUPS):
        wanted = sorted({min(k, SPLIT - k) for g in groups for k in range(g, SPLIT, 5)})
        pieces = [(k, i) for k in wanted for i in range(2) if y[k][i] is not None]
        left = jnp.concatenate([p for k, i in pieces for p in hi_lo(y[k][i])], axis=0)
        at = starts[part]
        full = jnp.dot(left, table[:, at : starts[part + 1]], preferred_element_type=jnp.float32)
        got = {
            p: full[2 * rows * i : 2 * rows * i + rows] + full[2 * rows * i + rows : 2 * rows * (i + 1)]
            for i, p in enumerate(pieces)
        }
        for place, group in enumerate(groups):
            cos = slice(place * 256, place * 256 + 128)
            sin = slice(place * 256 + 128, place * 256 + 256)
            re = im = None
            for q in range(4):
                k = group + 5 * q
                same = min(k, SPLIT - k)
                a = got[(same, 0)]
                r, i = a[:, cos], a[:, sin]
                if (same, 1) in got:
                    b = got[(same, 1)] if k == same else -got[(same, 1)]
                    r, i = r - b[:, sin], i + b[:, cos]
                re = r if re is None else jnp.where(run == q, r, re)
                im = i if im is None else jnp.where(run == q, i, im)
            real[group], imag[group] = re, im
    re = jnp.concatenate(real, axis=1)
    im = jnp.concatenate(imag, axis=1)
    power = re * re + im * im
    hi, mid = hi_lo(power)
    low = (power - hi.astype(jnp.float32) - mid.astype(jnp.float32)).astype(jnp.bfloat16)
    sums = jnp.dot(jnp.concatenate([hi, mid, low], axis=0), near[...], preferred_element_type=jnp.float32)
    smooth = (sums[:rows] + sums[rows : 2 * rows] + sums[2 * rows :]) * inverse
    mask = mask_buf[...].astype(jnp.float32)
    spread = jnp.concatenate([jnp.broadcast_to(mask[m : m + 1], (chans, chans)) for m in range(minutes)], axis=0)
    own = lax.broadcasted_iota(jnp.int32, (rows, chans), 0) % chans
    other = lax.broadcasted_iota(jnp.int32, (rows, chans), 1)
    flags = jnp.sum(jnp.where(own == other, spread, 0.0), axis=1, keepdims=True)
    factor = flags * lax.rsqrt(smooth + EPS)
    last = lax.broadcasted_iota(jnp.int32, (rows, LANES), 1) == LANES - 1
    out_ref[:, :LANES] = (re * factor).astype(jnp.bfloat16)
    out_ref[:, LANES:] = jnp.where(last, flags, im * factor).astype(jnp.bfloat16)


def whiten(traces, valid_mask):
    chans, minutes, samples = traces.shape
    rows = chans * minutes
    anywhere = pl.BlockSpec(memory_space=pltpu.HBM)
    return pl.pallas_call(
        whiten_kernel,
        out_shape=jax.ShapeDtypeStruct((rows, 2 * LANES), jnp.bfloat16),
        in_specs=[anywhere] * 3,
        out_specs=pl.BlockSpec(memory_space=pltpu.VMEM),
        scratch_shapes=[
            pltpu.VMEM((chans, minutes, samples), jnp.bfloat16),
            pltpu.VMEM((minutes, chans), jnp.int32),
            pltpu.VMEM((FOLD, 5 * 256), jnp.bfloat16),
            pltpu.VMEM((LANES, LANES), jnp.bfloat16),
            pltpu.SemaphoreType.DMA((5,)),
        ],
        compiler_params=pltpu.CompilerParams(vmem_limit_bytes=WHITEN_VMEM),
        name="whiten",
    )(traces, valid_mask.T, jnp.asarray(fold_table()))


def cross_tile(own, part, chans, cross, j):
    minutes = own.shape[0] // chans
    for a in range(0, chans, 2):
        both_re, both_im = [], []
        for channel in (a, a + 1):
            re = im = None
            for m in range(minutes):
                row = m * chans + channel
                o_re, o_im = own[row : row + 1, :LANES], own[row : row + 1, LANES:]
                p_re = part[m * chans : (m + 1) * chans, :LANES]
                p_im = part[m * chans : (m + 1) * chans, LANES:]
                r = o_re * p_re + o_im * p_im
                i = o_im * p_re - o_re * p_im
                re = r if re is None else re + r
                im = i if im is None else im + i
            both_re.append(re)
            both_im.append(im)
        rows = slice((j * chans + a) * chans, (j * chans + a + 2) * chans)
        cross[rows, :LANES] = jnp.concatenate(both_re, axis=0).astype(jnp.bfloat16)
        cross[rows, LANES:] = jnp.concatenate(both_im, axis=0).astype(jnp.bfloat16)


def lag_product(cross, table, shape):
    full = jnp.dot(cross, table, preferred_element_type=jnp.float32)
    scale = (1.0 / math.sqrt(BINS)) / jnp.maximum(full[:, COLS - 1 :], 1.0)
    return (full * scale)[:, :LAGS].reshape(shape)


def corr_kernel(pick, slots_ref, panels_ref, lag_ref, stack_ref, out_ref, cross):
    step = pl.program_id(0)
    count, chans = out_ref.shape[0], out_ref.shape[1]
    own = panels_ref[pick(lax.axis_index("row"))].astype(jnp.float32)
    for j in range(count):
        part = panels_ref[pick(slots_ref[0, step * count + j])].astype(jnp.float32)
        cross_tile(own, part, chans, cross, j)
    corr = lag_product(cross[...], lag_ref[...], out_ref.shape)
    out_ref[...] = stack_ref[pl.ds(step * count, count)] + corr


def correlate(pick, slots, panels, stack):
    offsets, chans = stack.shape[0], stack.shape[1]
    chunk = max(d for d in range(1, 7) if offsets % d == 0)
    whole = pl.BlockSpec(memory_space=pltpu.VMEM)
    return pl.pallas_call(
        functools.partial(corr_kernel, pick),
        out_shape=jax.ShapeDtypeStruct(stack.shape, jnp.float32),
        grid_spec=pltpu.PrefetchScalarGridSpec(
            num_scalar_prefetch=1,
            grid=(offsets // chunk,),
            in_specs=[whole, whole, whole],
            out_specs=pl.BlockSpec((chunk, chans, chans, LAGS), lambda i, s: (i, 0, 0, 0)),
            scratch_shapes=[pltpu.VMEM((chunk * chans * chans, panels.shape[2]), jnp.bfloat16)],
        ),
        compiler_params=pltpu.CompilerParams(vmem_limit_bytes=CORR_VMEM),
        name="correlate",
    )(slots, panels, jnp.asarray(lag_table()), stack)


def gather_all(own, slots, stack):
    panels = lax.all_gather(own, "row", axis=0)
    return correlate(lambda j: j, slots, panels, stack)


def place(panel_count):
    me = lax.axis_index("row")
    return me, me // 2, lax.rem(me, 2), lax.rem(me // 2, 2)


def first_hop(panel_count):
    me, chip, core, odd = place(panel_count)
    a = jnp.where(core == 0, chip + 1 - 2 * odd, chip + 2)
    b = jnp.where(core == 0, chip - 1 + 4 * odd, chip + 3 - 2 * odd)
    return a, b


def pair_panels(panel_count):
    me, chip, core, odd = place(panel_count)
    return [(0, me, True), (1, me + 1 - 2 * core, True)]


def near_panels(panel_count):
    me, chip, core, odd = place(panel_count)
    a, b = first_hop(panel_count)
    pairs = [(2 * i + t, 2 * c + (core if t == 0 else 1 - core), True) for i, c in enumerate((a, b)) for t in range(2)]
    return pairs + [(4, me + 8, True)]


def swapped_panels(panel_count):
    me, chip, core, odd = place(panel_count)
    found = []
    for t in range(2):
        ahead = jnp.where(core == 0, chip + 2, chip + 1 + 2 * odd)
        found.append((2 * odd * core + t, 2 * ahead + (1 - core if t == 0 else core), True))
    for t in range(2):
        ahead = 2 * (chip + 3 - 2 * odd) + 1 - t
        found.append((jnp.where(core == 0, 2 + t, 4), jnp.where(core == 0, ahead, 2 * chip + 8), (core == 0) | (t == 0)))
    return found


def products(which, panel_count, own, panels_ref, table, chans, cross, keep):
    found = which(panel_count)
    for start in range(0, len(found), 2):
        some = found[start : start + 2]
        for j, (at, panel, wanted) in enumerate(some):
            cross_tile(own, panels_ref[at].astype(jnp.float32), chans, cross, start + j)
        rows = slice(start * chans * chans, (start + len(some)) * chans * chans)
        full = jnp.dot(cross[rows], table, preferred_element_type=jnp.float32)
        scale = (1.0 / math.sqrt(BINS)) / jnp.maximum(full[:, COLS - 1 :], 1.0)
        keep(start, (full * scale).reshape(len(some), chans * chans, COLS))


def early_kernel(panel_count, which, pair_ref, panels_ref, table_ref, out_ref, cross):
    own = pair_ref[0].astype(jnp.float32)

    def keep(start, corr):
        out_ref[start : start + corr.shape[0]] = corr

    products(which, panel_count, own, panels_ref, table_ref[...], own.shape[0] // SEGS, cross, keep)


def early(which, count, panel_count, chans, pair, panels, table):
    whole = pl.BlockSpec(memory_space=pltpu.VMEM)
    rows = count * chans * chans
    return pl.pallas_call(
        functools.partial(early_kernel, panel_count, which),
        out_shape=jax.ShapeDtypeStruct((count, chans * chans, COLS), jnp.float32),
        in_specs=[whole] * 3,
        out_specs=whole,
        scratch_shapes=[pltpu.VMEM((rows, 2 * LANES), jnp.bfloat16)],
        compiler_params=pltpu.CompilerParams(vmem_limit_bytes=CORR_VMEM),
        cost_estimate=pl.CostEstimate(flops=4 * rows * LANES * COLS, bytes_accessed=4 * rows * COLS, transcendentals=0),
        name=which.__name__,
    )(pair, panels, table)


def last_kernel(panel_count, lists, slots_ref, pair_ref, panels_ref, table_ref, stack_ref, *refs):
    done_refs = refs[: len(lists) - 1]
    out_ref, cross, result, sem = refs[len(lists) - 1 :]
    offsets, chans = stack_ref.shape[0], stack_ref.shape[1]
    me = lax.axis_index("row")
    copies = []

    def finish(found, corr):
        for j, (at, panel, wanted) in enumerate(found):
            panel = lax.rem(panel + panel_count, panel_count)
            valid = (lax.rem(panel - me + 1 + panel_count, panel_count) < offsets) & wanted
            slot = jnp.int32(0)
            for o in range(1, offsets):
                slot = jnp.where(slots_ref[0, o] == panel, o, slot)
            n = len(copies)
            result[n] = stack_ref[slot] + corr[j][:, :LAGS].reshape(chans, chans, LAGS)
            copy = pltpu.make_async_copy(result.at[n], out_ref.at[slot], sem.at[n])
            copies.append((valid, copy))
            pl.when(valid)(copy.start)

    for which, done in zip(lists, done_refs):
        finish(which(panel_count), done)
    own = pair_ref[0].astype(jnp.float32)
    found = lists[-1](panel_count)

    def keep(start, corr):
        finish(found[start : start + corr.shape[0]], corr)

    products(lists[-1], panel_count, own, panels_ref, table_ref[...], chans, cross, keep)
    for valid, copy in copies:
        pl.when(valid)(copy.wait)


def last(lists, counts, panel_count, slots, pair, panels, table, stack, *done):
    offsets, chans = stack.shape[0], stack.shape[1]
    whole = pl.BlockSpec(memory_space=pltpu.VMEM)
    rows = counts[-1] * chans * chans
    return pl.pallas_call(
        functools.partial(last_kernel, panel_count, lists),
        out_shape=jax.ShapeDtypeStruct(stack.shape, jnp.float32),
        in_specs=[pl.BlockSpec(memory_space=pltpu.SMEM)] + [whole] * (4 + len(done)),
        out_specs=pl.BlockSpec(memory_space=pltpu.HBM),
        scratch_shapes=[
            pltpu.VMEM((rows, 2 * LANES), jnp.bfloat16),
            pltpu.VMEM((sum(counts), chans, chans, LAGS), jnp.float32),
            pltpu.SemaphoreType.DMA((sum(counts),)),
        ],
        compiler_params=pltpu.CompilerParams(vmem_limit_bytes=CORR_VMEM),
        cost_estimate=pl.CostEstimate(flops=4 * rows * LANES * COLS, bytes_accessed=4 * rows * COLS, transcendentals=0),
        name=lists[-1].__name__,
    )(slots, pair, panels, table, stack, *done)


def gather_near(own, slots, stack, panel_count):
    chips = panel_count // 2
    def swap(array):
        return lax.ppermute(array, "row", [(i ^ 1, i) for i in range(panel_count)])

    def fetch(array, even, odd):
        ahead = [even, odd]
        moves = []
        for i in range(panel_count):
            c = i // 2
            moves.append((2 * ((c + ahead[i % 2][c % 2]) % chips) + i % 2, i))
        return lax.ppermute(array, "row", moves)

    table = jnp.asarray(lag_table())
    twice = jnp.stack([own, own])
    pair, own = lax.optimization_barrier((lax.dynamic_update_slice(twice, swap(own)[None], (1, 0, 0)), own))
    near = fetch(pair, (1, -1), (2, 2))
    next_near = fetch(pair, (-1, 3), (3, 1))
    far = fetch(own, (4, 4), (4, 4))
    chans = stack.shape[1]
    first = early(pair_panels, 2, panel_count, chans, pair, pair, table)
    near, next_near, far, first = lax.optimization_barrier((near, next_near, far, first))
    five = jnp.concatenate([near, next_near, far[None]], axis=0)
    swapped = swap(five)
    second = early(near_panels, 5, panel_count, chans, pair, five, table)
    lists = (pair_panels, near_panels, swapped_panels)
    return last(lists, (2, 5, 4), panel_count, slots, pair, swapped, table, stack, first, second)


def shards(traces, valid_mask, pair_table, stack_in):
    own = whiten(traces, valid_mask)
    panel_count = lax.axis_size("row")
    if pair_table.shape[1] == 10 and panel_count >= 12 and panel_count % 4 == 0:
        return gather_near(own, pair_table, stack_in[0], panel_count)[None]
    return gather_all(own, pair_table, stack_in[0])[None]


def solution(mesh):
    in_specs = (
        P(("parts", "row"), None, None),
        P(("parts", "row"), None),
        P(("parts", "row"), None),
        P(("parts", "row"), None, None, None, None),
    )
    out_specs = P(("parts", "row"), None, None, None, None)
    return jax.shard_map(shards, mesh=mesh, in_specs=in_specs, out_specs=out_specs, check_vma=False)
```

```python
import functools
import math

import jax
import jax.numpy as jnp
import ml_dtypes
import numpy as np
from jax import lax
from jax.experimental import pallas as pl
from jax.experimental.pallas import tpu as pltpu
from jax.sharding import PartitionSpec as P

SAMPLES = 12000
FLO = 6
BINS = 595
SEGS = 2
HALF = 40
LAGS = 401
EPS = 1e-06
WHITEN_VMEM = 60 << 20
CORR_VMEM = 24 << 20

SPLIT = 20
FOLD = SAMPLES // SPLIT
LANES = 640
RUN = 32
COLS = 512


def bin_at(lane):
    residue = lane // 128 + 5 * (lane % 128 // RUN)
    return residue + SPLIT * (residue < FLO) + SPLIT * (lane % RUN)


BIN_OF = bin_at(np.arange(LANES))
USED = BIN_OF < FLO + BINS
GROUPS = ((1, 4), (2, 3), (0,))


def bf16(a):
    return np.asarray(a, np.float32).astype(ml_dtypes.bfloat16)


def fold_table():
    q = (np.arange(FOLD)[:, None] * BIN_OF[None, :]) % SAMPLES
    angle = 2.0 * np.pi * q / SAMPLES
    cos = np.where(USED, np.cos(angle), 0.0).reshape(FOLD, 5, 1, 128)
    sin = np.where(USED, -np.sin(angle), 0.0).reshape(FOLD, 5, 1, 128)
    table = np.concatenate([cos, sin], axis=2)
    order = [group for some in GROUPS for group in some]
    return bf16(table[:, order].reshape(FOLD, 5 * 256))


def lag_table():
    tau = np.arange(LAGS) - (LAGS - 1) // 2
    q = (BIN_OF[:, None] * tau[None, :]) % SAMPLES
    angle = 2.0 * np.pi * q / SAMPLES
    table = np.zeros((2 * LANES, COLS), np.float64)
    table[:LANES, :LAGS] = np.where(USED[:, None], np.cos(angle), 0.0)
    table[LANES:, :LAGS] = np.where(USED[:, None], -np.sin(angle), 0.0)
    table[LANES - 1, COLS - 1] = 1.0
    return bf16(table)


def cosine(n, of):
    return math.cos(2.0 * math.pi * n / of)


def sine(n, of):
    return math.sin(2.0 * math.pi * n / of)


def ten_point(s):
    e = [s[n] + s[n + 5] for n in range(5)]
    d = [s[n] - s[n + 5] for n in range(5)]
    c1, c2, s1, s2 = cosine(1, 10), cosine(2, 10), sine(1, 10), sine(2, 10)
    e14, e23, f14, f23 = e[1] + e[4], e[2] + e[3], e[1] - e[4], e[2] - e[3]
    d14, d23, g14, g23 = d[1] + d[4], d[2] + d[3], d[1] - d[4], d[2] - d[3]
    y0 = (e[0] + e14 + e23, None)
    y2 = (e[0] + c2 * e14 - c1 * e23, s2 * f14 + s1 * f23)
    y4 = (e[0] - c1 * e14 + c2 * e23, s1 * f14 - s2 * f23)
    y1 = (d[0] + c1 * g14 + c2 * g23, s1 * d14 + s2 * d23)
    y3 = (d[0] - c2 * g14 - c1 * g23, s2 * d14 - s1 * d23)
    y5 = (d[0] - g14 + g23, None)
    return [y0, y1, y2, y3, y4, y5]


def twenty_point(s):
    y = [None] * 11
    y[0::2] = ten_point([s[n] + s[n + 10] for n in range(10)])
    d = [s[n] - s[n + 10] for n in range(10)]
    g1, g2, g3, g4 = (d[n] - d[10 - n] for n in range(1, 5))
    h1, h2, h3, h4 = (d[n] + d[10 - n] for n in range(1, 5))
    for k, turn in ((1, d[5]), (3, -d[5])):
        even = d[0] + cosine(2 * k, 20) * g2 + cosine(4 * k, 20) * g4
        odd = cosine(k, 20) * g1 + cosine(3 * k, 20) * g3
        even_sin = sine(2 * k, 20) * h2 + sine(4 * k, 20) * h4
        odd_sin = sine(k, 20) * h1 + sine(3 * k, 20) * h3 + turn
        y[k] = (even + odd, odd_sin + even_sin)
        y[10 - k] = (even - odd, odd_sin - even_sin)
    y[5] = (d[0] - g2 + g4, h1 - h3 + d[5])
    return y


def hi_lo(y):
    hi = y.astype(jnp.bfloat16)
    return [hi, (y - hi.astype(jnp.float32)).astype(jnp.bfloat16)]


def whiten_kernel(x_hbm, mask_hbm, table_hbm, out_ref, x_buf, mask_buf, table, near, sem):
    chans, minutes, samples = x_buf.shape
    rows = chans * minutes
    starts = (0, 512, 1024, 1280)
    fetch_x = pltpu.make_async_copy(x_hbm, x_buf, sem.at[0])
    fetch_mask = pltpu.make_async_copy(mask_hbm, mask_buf, sem.at[1])
    fetch_table = [
        pltpu.make_async_copy(table_hbm.at[:, pl.ds(a, b - a)], table.at[:, pl.ds(a, b - a)], sem.at[2 + i])
        for i, (a, b) in enumerate(zip(starts, starts[1:]))
    ]
    for copy in [fetch_x, fetch_mask] + fetch_table:
        copy.start()

    down = bin_at(lax.broadcasted_iota(jnp.int32, (LANES, 128), 0))
    down = jnp.where(down < FLO + BINS, down, -SAMPLES)
    lanes = bin_at(lax.broadcasted_iota(jnp.int32, (8, LANES), 1))
    for group in range(5):
        across = jnp.broadcast_to(lanes[:1, group * 128 : (group + 1) * 128], (LANES, 128))
        close = (jnp.abs(down - across) <= HALF) & (across < FLO + BINS)
        near[:, group * 128 : (group + 1) * 128] = jnp.where(close, 1.0, 0.0).astype(jnp.bfloat16)
    bins = lanes[:1]
    count = jnp.minimum(bins + HALF, FLO + BINS - 1) - jnp.maximum(bins - HALF, FLO) + 1
    inverse = 1.0 / jnp.maximum(count, 1).astype(jnp.float32)

    fetch_x.wait()
    x = jnp.swapaxes(x_buf[...], 0, 1).reshape(rows, samples)
    y = twenty_point([x[:, FOLD * n : FOLD * (n + 1)].astype(jnp.float32) for n in range(SPLIT)])
    run = lax.broadcasted_iota(jnp.int32, (rows, 128), 1) // RUN
    for copy in [fetch_mask] + fetch_table:
        copy.wait()
    real = [None] * 5
    imag = [None] * 5
    for part, groups in enumerate(GROUPS):
        wanted = sorted({min(k, SPLIT - k) for g in groups for k in range(g, SPLIT, 5)})
        pieces = [(k, i) for k in wanted for i in range(2) if y[k][i] is not None]
        halves = [hi_lo(y[k][i]) for k, i in pieces]
        left = jnp.concatenate([half[j] for j in range(2) for half in halves], axis=0)
        at = starts[part]
        full = jnp.dot(left, table[:, at : starts[part + 1]], preferred_element_type=jnp.float32)
        got = {
            p: full[rows * i : rows * (i + 1)] + full[rows * (len(pieces) + i) : rows * (len(pieces) + i + 1)]
            for i, p in enumerate(pieces)
        }
        for place, group in enumerate(groups):
            cos = slice(place * 256, place * 256 + 128)
            sin = slice(place * 256 + 128, place * 256 + 256)
            re = im = None
            for q in range(4):
                k = group + 5 * q
                same = min(k, SPLIT - k)
                a = got[(same, 0)]
                r, i = a[:, cos], a[:, sin]
                if (same, 1) in got:
                    b = got[(same, 1)]
                    if k == same:
                        r, i = r + b[:, sin], i - b[:, cos]
                    else:
                        r, i = r - b[:, sin], i + b[:, cos]
                re = r if re is None else jnp.where(run == q, r, re)
                im = i if im is None else jnp.where(run == q, i, im)
            real[group], imag[group] = re, im
    re = jnp.concatenate(real, axis=1)
    im = jnp.concatenate(imag, axis=1)
    power = re * re + im * im
    hi, mid = hi_lo(power)
    low = (power - hi.astype(jnp.float32) - mid.astype(jnp.float32)).astype(jnp.bfloat16)
    sums = jnp.dot(jnp.concatenate([hi, mid, low], axis=0), near[...], preferred_element_type=jnp.float32)
    smooth = (sums[:rows] + sums[rows : 2 * rows] + sums[2 * rows :]) * inverse
    mask = mask_buf[...].astype(jnp.float32)
    spread = jnp.concatenate([jnp.broadcast_to(mask[m : m + 1], (chans, chans)) for m in range(minutes)], axis=0)
    own = lax.broadcasted_iota(jnp.int32, (rows, chans), 0) % chans
    other = lax.broadcasted_iota(jnp.int32, (rows, chans), 1)
    flags = jnp.sum(jnp.where(own == other, spread, 0.0), axis=1, keepdims=True)
    factor = flags * lax.rsqrt(smooth + EPS)
    last = lax.broadcasted_iota(jnp.int32, (rows, LANES), 1) == LANES - 1
    out_ref[:, :LANES] = (re * factor).astype(jnp.bfloat16)
    out_ref[:, LANES:] = jnp.where(last, flags, im * factor).astype(jnp.bfloat16)


def whiten(traces, valid_mask):
    chans, minutes, samples = traces.shape
    rows = chans * minutes
    anywhere = pl.BlockSpec(memory_space=pltpu.HBM)
    return pl.pallas_call(
        whiten_kernel,
        out_shape=jax.ShapeDtypeStruct((rows, 2 * LANES), jnp.bfloat16),
        in_specs=[anywhere] * 3,
        out_specs=pl.BlockSpec(memory_space=pltpu.VMEM),
        scratch_shapes=[
            pltpu.VMEM((chans, minutes, samples), jnp.bfloat16),
            pltpu.VMEM((minutes, chans), jnp.int32),
            pltpu.VMEM((FOLD, 5 * 256), jnp.bfloat16),
            pltpu.VMEM((LANES, LANES), jnp.bfloat16),
            pltpu.SemaphoreType.DMA((5,)),
        ],
        compiler_params=pltpu.CompilerParams(vmem_limit_bytes=WHITEN_VMEM),
        name="whiten",
    )(traces, valid_mask.T, jnp.asarray(fold_table()))


def cross_tile(own, part, chans, cross, j):
    minutes = own.shape[0] // chans
    for a in range(0, chans, 2):
        both_re, both_im = [], []
        for channel in (a, a + 1):
            re = im = None
            for m in range(minutes):
                row = m * chans + channel
                o_re, o_im = own[row : row + 1, :LANES], own[row : row + 1, LANES:]
                p_re = part[m * chans : (m + 1) * chans, :LANES]
                p_im = part[m * chans : (m + 1) * chans, LANES:]
                r = o_re * p_re + o_im * p_im
                i = o_im * p_re - o_re * p_im
                re = r if re is None else re + r
                im = i if im is None else im + i
            both_re.append(re)
            both_im.append(im)
        rows = slice((j * chans + a) * chans, (j * chans + a + 2) * chans)
        cross[rows, :LANES] = jnp.concatenate(both_re, axis=0).astype(jnp.bfloat16)
        cross[rows, LANES:] = jnp.concatenate(both_im, axis=0).astype(jnp.bfloat16)


def lag_product(cross, table, shape):
    full = jnp.dot(cross, table, preferred_element_type=jnp.float32)
    scale = (1.0 / math.sqrt(BINS)) / jnp.maximum(full[:, COLS - 1 :], 1.0)
    return (full * scale)[:, :LAGS].reshape(shape)


def corr_kernel(pick, slots_ref, panels_ref, lag_ref, stack_ref, out_ref, cross):
    step = pl.program_id(0)
    count, chans = out_ref.shape[0], out_ref.shape[1]
    own = panels_ref[pick(lax.axis_index("row"))].astype(jnp.float32)
    for j in range(count):
        part = panels_ref[pick(slots_ref[0, step * count + j])].astype(jnp.float32)
        cross_tile(own, part, chans, cross, j)
    corr = lag_product(cross[...], lag_ref[...], out_ref.shape)
    out_ref[...] = stack_ref[pl.ds(step * count, count)] + corr


def correlate(pick, slots, panels, stack):
    offsets, chans = stack.shape[0], stack.shape[1]
    chunk = max(d for d in range(1, 7) if offsets % d == 0)
    whole = pl.BlockSpec(memory_space=pltpu.VMEM)
    return pl.pallas_call(
        functools.partial(corr_kernel, pick),
        out_shape=jax.ShapeDtypeStruct(stack.shape, jnp.float32),
        grid_spec=pltpu.PrefetchScalarGridSpec(
            num_scalar_prefetch=1,
            grid=(offsets // chunk,),
            in_specs=[whole, whole, whole],
            out_specs=pl.BlockSpec((chunk, chans, chans, LAGS), lambda i, s: (i, 0, 0, 0)),
            scratch_shapes=[pltpu.VMEM((chunk * chans * chans, panels.shape[2]), jnp.bfloat16)],
        ),
        compiler_params=pltpu.CompilerParams(vmem_limit_bytes=CORR_VMEM),
        name="correlate",
    )(slots, panels, jnp.asarray(lag_table()), stack)


def gather_all(own, slots, stack):
    panels = lax.all_gather(own, "row", axis=0)
    return correlate(lambda j: j, slots, panels, stack)


def place(panel_count):
    me = lax.axis_index("row")
    return me, me // 2, lax.rem(me, 2), lax.rem(me // 2, 2)


def first_hop(panel_count):
    me, chip, core, odd = place(panel_count)
    a = jnp.where(core == 0, chip + 1 - 2 * odd, chip + 2)
    b = jnp.where(core == 0, chip - 1 + 4 * odd, chip + 3 - 2 * odd)
    return a, b


def pair_panels(panel_count):
    me, chip, core, odd = place(panel_count)
    return [(0, me, True), (1, me + 1 - 2 * core, True)]


def near_panels(panel_count):
    me, chip, core, odd = place(panel_count)
    a, b = first_hop(panel_count)
    pairs = [(2 * i + t, 2 * c + (core if t == 0 else 1 - core), True) for i, c in enumerate((a, b)) for t in range(2)]
    return pairs + [(4, me + 8, True)]


def swapped_panels(panel_count):
    me, chip, core, odd = place(panel_count)
    found = []
    for t in range(2):
        ahead = jnp.where(core == 0, chip + 2, chip + 1 + 2 * odd)
        found.append((2 * odd * core + t, 2 * ahead + (1 - core if t == 0 else core), True))
    for t in range(2):
        ahead = 2 * (chip + 3 - 2 * odd) + 1 - t
        found.append((jnp.where(core == 0, 2 + t, 4), jnp.where(core == 0, ahead, 2 * chip + 8), (core == 0) | (t == 0)))
    return found


def products(which, panel_count, own, panels_ref, table, chans, cross, keep):
    found = which(panel_count)
    for start in range(0, len(found), 2):
        some = found[start : start + 2]
        for j, (at, panel, wanted) in enumerate(some):
            cross_tile(own, panels_ref[at].astype(jnp.float32), chans, cross, start + j)
        rows = slice(start * chans * chans, (start + len(some)) * chans * chans)
        full = jnp.dot(cross[rows], table, preferred_element_type=jnp.float32)
        scale = (1.0 / math.sqrt(BINS)) / jnp.maximum(full[:, COLS - 1 :], 1.0)
        keep(start, (full * scale).reshape(len(some), chans * chans, COLS))


def early_kernel(panel_count, which, pair_ref, panels_ref, table_ref, out_ref, cross):
    own = pair_ref[0].astype(jnp.float32)

    def keep(start, corr):
        out_ref[start : start + corr.shape[0]] = corr

    products(which, panel_count, own, panels_ref, table_ref[...], own.shape[0] // SEGS, cross, keep)


def early(which, count, panel_count, chans, pair, panels, table):
    whole = pl.BlockSpec(memory_space=pltpu.VMEM)
    rows = count * chans * chans
    return pl.pallas_call(
        functools.partial(early_kernel, panel_count, which),
        out_shape=jax.ShapeDtypeStruct((count, chans * chans, COLS), jnp.float32),
        in_specs=[whole] * 3,
        out_specs=whole,
        scratch_shapes=[pltpu.VMEM((rows, 2 * LANES), jnp.bfloat16)],
        compiler_params=pltpu.CompilerParams(vmem_limit_bytes=CORR_VMEM),
        cost_estimate=pl.CostEstimate(flops=4 * rows * LANES * COLS, bytes_accessed=4 * rows * COLS, transcendentals=0),
        name=which.__name__,
    )(pair, panels, table)


def last_kernel(panel_count, lists, slots_any, pair_ref, panels_ref, table_ref, stack_ref, *refs):
    done_refs = refs[: len(lists) - 1]
    out_ref, slots_ref, cross, result, sem = refs[len(lists) - 1 :]
    offsets, chans = stack_ref.shape[0], stack_ref.shape[1]
    fetch_slots = pltpu.make_async_copy(slots_any, slots_ref, sem.at[sem.shape[0] - 1])
    fetch_slots.start()
    me = lax.axis_index("row")
    own = pair_ref[0].astype(jnp.float32)
    copies = []

    def finish(found, corr):
        for j, (at, panel, wanted) in enumerate(found):
            panel = lax.rem(panel + panel_count, panel_count)
            valid = (lax.rem(panel - me + 1 + panel_count, panel_count) < offsets) & wanted
            slot = jnp.int32(0)
            for o in range(1, offsets):
                slot = jnp.where(slots_ref[0, o] == panel, o, slot)
            n = len(copies)
            result[n] = stack_ref[slot] + corr[j][:, :LAGS].reshape(chans, chans, LAGS)
            copy = pltpu.make_async_copy(result.at[n], out_ref.at[slot], sem.at[n])
            copies.append((valid, copy))
            pl.when(valid)(copy.start)

    found = lists[-1](panel_count)

    def keep(start, corr):
        if start == 0:
            fetch_slots.wait()
            for which, done in zip(lists, done_refs):
                finish(which(panel_count), done)
        finish(found[start : start + corr.shape[0]], corr)

    products(lists[-1], panel_count, own, panels_ref, table_ref[...], chans, cross, keep)
    for valid, copy in copies:
        pl.when(valid)(copy.wait)


def last(lists, counts, panel_count, slots, pair, panels, table, stack, *done):
    offsets, chans = stack.shape[0], stack.shape[1]
    whole = pl.BlockSpec(memory_space=pltpu.VMEM)
    rows = counts[-1] * chans * chans
    return pl.pallas_call(
        functools.partial(last_kernel, panel_count, lists),
        out_shape=jax.ShapeDtypeStruct(stack.shape, jnp.float32),
        in_specs=[pl.BlockSpec(memory_space=pl.ANY)] + [whole] * (4 + len(done)),
        out_specs=pl.BlockSpec(memory_space=pltpu.HBM),
        scratch_shapes=[
            pltpu.SMEM(slots.shape, jnp.int32),
            pltpu.VMEM((rows, 2 * LANES), jnp.bfloat16),
            pltpu.VMEM((sum(counts), chans, chans, LAGS), jnp.float32),
            pltpu.SemaphoreType.DMA((sum(counts) + 1,)),
        ],
        compiler_params=pltpu.CompilerParams(vmem_limit_bytes=CORR_VMEM),
        cost_estimate=pl.CostEstimate(flops=4 * rows * LANES * COLS, bytes_accessed=4 * rows * COLS, transcendentals=0),
        name=lists[-1].__name__,
    )(slots, pair, panels, table, stack, *done)


def gather_near(own, slots, stack, panel_count):
    chips = panel_count // 2
    def swap(array):
        return lax.ppermute(array, "row", [(i ^ 1, i) for i in range(panel_count)])

    def fetch(array, even, odd):
        ahead = [even, odd]
        moves = []
        for i in range(panel_count):
            c = i // 2
            moves.append((2 * ((c + ahead[i % 2][c % 2]) % chips) + i % 2, i))
        return lax.ppermute(array, "row", moves)

    table = jnp.asarray(lag_table())
    twice = jnp.stack([own, own])
    pair, own = lax.optimization_barrier((lax.dynamic_update_slice(twice, swap(own)[None], (1, 0, 0)), own))
    near = fetch(pair, (1, -1), (2, 2))
    next_near = fetch(pair, (-1, 3), (3, 1))
    far = fetch(own, (4, 4), (4, 4))
    chans = stack.shape[1]
    first = early(pair_panels, 2, panel_count, chans, pair, pair, table)
    near, next_near, far, first = lax.optimization_barrier((near, next_near, far, first))
    five = jnp.concatenate([near, next_near, far[None]], axis=0)
    swapped = swap(five)
    second = early(near_panels, 5, panel_count, chans, pair, five, table)
    lists = (pair_panels, near_panels, swapped_panels)
    return last(lists, (2, 5, 4), panel_count, slots, pair, swapped, table, stack, first, second)


def shards(traces, valid_mask, pair_table, stack_in):
    own = whiten(traces, valid_mask)
    panel_count = lax.axis_size("row")
    if pair_table.shape[1] == 10 and panel_count >= 12 and panel_count % 4 == 0:
        return gather_near(own, pair_table, stack_in[0], panel_count)[None]
    return gather_all(own, pair_table, stack_in[0])[None]


def solution(mesh):
    in_specs = (
        P(("parts", "row"), None, None),
        P(("parts", "row"), None),
        P(("parts", "row"), None),
        P(("parts", "row"), None, None, None, None),
    )
    out_specs = P(("parts", "row"), None, None, None, None)
    return jax.shard_map(shards, mesh=mesh, in_specs=in_specs, out_specs=out_specs, check_vma=False)
```

```python
import functools
import math

import jax
import jax.numpy as jnp
import ml_dtypes
import numpy as np
from jax import lax
from jax.experimental import pallas as pl
from jax.experimental.pallas import tpu as pltpu
from jax.sharding import PartitionSpec as P

SAMPLES = 12000
FLO = 6
BINS = 595
SEGS = 2
HALF = 40
LAGS = 401
EPS = 1e-06
WHITEN_VMEM = 60 << 20
CORR_VMEM = 24 << 20

SPLIT = 20
FOLD = SAMPLES // SPLIT
LANES = 640
RUN = 32
COLS = 512


def bin_at(lane):
    residue = lane // 128 + 5 * (lane % 128 // RUN)
    return residue + SPLIT * (residue < FLO) + SPLIT * (lane % RUN)


BIN_OF = bin_at(np.arange(LANES))
USED = BIN_OF < FLO + BINS
GROUPS = ((1, 4), (2, 3), (0,))


def bf16(a):
    return np.asarray(a, np.float32).astype(ml_dtypes.bfloat16)


def fold_table():
    q = (np.arange(FOLD)[:, None] * BIN_OF[None, :]) % SAMPLES
    angle = 2.0 * np.pi * q / SAMPLES
    cos = np.where(USED, np.cos(angle), 0.0).reshape(FOLD, 5, 1, 128)
    sin = np.where(USED, -np.sin(angle), 0.0).reshape(FOLD, 5, 1, 128)
    table = np.concatenate([cos, sin], axis=2)
    order = [group for some in GROUPS for group in some]
    return bf16(table[:, order].reshape(FOLD, 5 * 256))


def lag_table():
    tau = np.arange(LAGS) - (LAGS - 1) // 2
    q = (BIN_OF[:, None] * tau[None, :]) % SAMPLES
    angle = 2.0 * np.pi * q / SAMPLES
    table = np.zeros((2 * LANES, COLS), np.float64)
    table[:LANES, :LAGS] = np.where(USED[:, None], np.cos(angle), 0.0)
    table[LANES:, :LAGS] = np.where(USED[:, None], -np.sin(angle), 0.0)
    table[LANES - 1, COLS - 1] = 1.0
    return bf16(table)


def cosine(n, of):
    return math.cos(2.0 * math.pi * n / of)


def sine(n, of):
    return math.sin(2.0 * math.pi * n / of)


def ten_point(s):
    e = [s[n] + s[n + 5] for n in range(5)]
    d = [s[n] - s[n + 5] for n in range(5)]
    c1, c2, s1, s2 = cosine(1, 10), cosine(2, 10), sine(1, 10), sine(2, 10)
    e14, e23, f14, f23 = e[1] + e[4], e[2] + e[3], e[1] - e[4], e[2] - e[3]
    d14, d23, g14, g23 = d[1] + d[4], d[2] + d[3], d[1] - d[4], d[2] - d[3]
    y0 = (e[0] + e14 + e23, None)
    y2 = (e[0] + c2 * e14 - c1 * e23, s2 * f14 + s1 * f23)
    y4 = (e[0] - c1 * e14 + c2 * e23, s1 * f14 - s2 * f23)
    y1 = (d[0] + c1 * g14 + c2 * g23, s1 * d14 + s2 * d23)
    y3 = (d[0] - c2 * g14 - c1 * g23, s2 * d14 - s1 * d23)
    y5 = (d[0] - g14 + g23, None)
    return [y0, y1, y2, y3, y4, y5]


def twenty_point(s):
    y = [None] * 11
    y[0::2] = ten_point([s[n] + s[n + 10] for n in range(10)])
    d = [s[n] - s[n + 10] for n in range(10)]
    g1, g2, g3, g4 = (d[n] - d[10 - n] for n in range(1, 5))
    h1, h2, h3, h4 = (d[n] + d[10 - n] for n in range(1, 5))
    for k, turn in ((1, d[5]), (3, -d[5])):
        even = d[0] + cosine(2 * k, 20) * g2 + cosine(4 * k, 20) * g4
        odd = cosine(k, 20) * g1 + cosine(3 * k, 20) * g3
        even_sin = sine(2 * k, 20) * h2 + sine(4 * k, 20) * h4
        odd_sin = sine(k, 20) * h1 + sine(3 * k, 20) * h3 + turn
        y[k] = (even + odd, odd_sin + even_sin)
        y[10 - k] = (even - odd, odd_sin - even_sin)
    y[5] = (d[0] - g2 + g4, h1 - h3 + d[5])
    return y


def hi_lo(y):
    hi = y.astype(jnp.bfloat16)
    return [hi, (y - hi.astype(jnp.float32)).astype(jnp.bfloat16)]


def whiten_kernel(x_hbm, mask_hbm, table_hbm, out_ref, x_buf, mask_buf, table, near, sem):
    chans, minutes, samples = x_buf.shape
    rows = chans * minutes
    starts = (0, 512, 1024, 1280)
    fetch_x = pltpu.make_async_copy(x_hbm, x_buf, sem.at[0])
    fetch_mask = pltpu.make_async_copy(mask_hbm, mask_buf, sem.at[1])
    fetch_table = [
        pltpu.make_async_copy(table_hbm.at[:, pl.ds(a, b - a)], table.at[:, pl.ds(a, b - a)], sem.at[2 + i])
        for i, (a, b) in enumerate(zip(starts, starts[1:]))
    ]
    for copy in [fetch_x, fetch_mask] + fetch_table:
        copy.start()

    down = bin_at(lax.broadcasted_iota(jnp.int32, (LANES, 128), 0))
    down = jnp.where(down < FLO + BINS, down, -SAMPLES)
    lanes = bin_at(lax.broadcasted_iota(jnp.int32, (8, LANES), 1))
    for group in range(5):
        across = jnp.broadcast_to(lanes[:1, group * 128 : (group + 1) * 128], (LANES, 128))
        close = (jnp.abs(down - across) <= HALF) & (across < FLO + BINS)
        near[:, group * 128 : (group + 1) * 128] = jnp.where(close, 1.0, 0.0).astype(jnp.bfloat16)
    bins = lanes[:1]
    count = jnp.minimum(bins + HALF, FLO + BINS - 1) - jnp.maximum(bins - HALF, FLO) + 1
    inverse = 1.0 / jnp.maximum(count, 1).astype(jnp.float32)

    fetch_x.wait()
    x = jnp.swapaxes(x_buf[...], 0, 1).reshape(rows, samples)
    y = twenty_point([x[:, FOLD * n : FOLD * (n + 1)].astype(jnp.float32) for n in range(SPLIT)])
    run = lax.broadcasted_iota(jnp.int32, (rows, 128), 1) // RUN
    for copy in [fetch_mask] + fetch_table:
        copy.wait()
    real = [None] * 5
    imag = [None] * 5
    for part, groups in enumerate(GROUPS):
        wanted = sorted({min(k, SPLIT - k) for g in groups for k in range(g, SPLIT, 5)})
        pieces = [(k, i) for k in wanted for i in range(2) if y[k][i] is not None]
        halves = [hi_lo(y[k][i]) for k, i in pieces]
        left = jnp.concatenate([half[j] for j in range(2) for half in halves], axis=0)
        at = starts[part]
        full = jnp.dot(left, table[:, at : starts[part + 1]], preferred_element_type=jnp.float32)
        got = {
            p: full[rows * i : rows * (i + 1)] + full[rows * (len(pieces) + i) : rows * (len(pieces) + i + 1)]
            for i, p in enumerate(pieces)
        }
        for place, group in enumerate(groups):
            cos = slice(place * 256, place * 256 + 128)
            sin = slice(place * 256 + 128, place * 256 + 256)
            re = im = None
            for q in range(4):
                k = group + 5 * q
                same = min(k, SPLIT - k)
                a = got[(same, 0)]
                r, i = a[:, cos], a[:, sin]
                if (same, 1) in got:
                    b = got[(same, 1)]
                    if k == same:
                        r, i = r + b[:, sin], i - b[:, cos]
                    else:
                        r, i = r - b[:, sin], i + b[:, cos]
                re = r if re is None else jnp.where(run == q, r, re)
                im = i if im is None else jnp.where(run == q, i, im)
            real[group], imag[group] = re, im
    re = jnp.concatenate(real, axis=1)
    im = jnp.concatenate(imag, axis=1)
    power = re * re + im * im
    hi, mid = hi_lo(power)
    low = (power - hi.astype(jnp.float32) - mid.astype(jnp.float32)).astype(jnp.bfloat16)
    sums = jnp.dot(jnp.concatenate([hi, mid, low], axis=0), near[...], preferred_element_type=jnp.float32)
    smooth = (sums[:rows] + sums[rows : 2 * rows] + sums[2 * rows :]) * inverse
    mask = mask_buf[...].astype(jnp.float32)
    spread = jnp.concatenate([jnp.broadcast_to(mask[m : m + 1], (chans, chans)) for m in range(minutes)], axis=0)
    own = lax.broadcasted_iota(jnp.int32, (rows, chans), 0) % chans
    other = lax.broadcasted_iota(jnp.int32, (rows, chans), 1)
    flags = jnp.sum(jnp.where(own == other, spread, 0.0), axis=1, keepdims=True)
    factor = flags * lax.rsqrt(smooth + EPS)
    last = lax.broadcasted_iota(jnp.int32, (rows, LANES), 1) == LANES - 1
    out_ref[:, :LANES] = (re * factor).astype(jnp.bfloat16)
    out_ref[:, LANES:] = jnp.where(last, flags, im * factor).astype(jnp.bfloat16)


def whiten(traces, valid_mask):
    chans, minutes, samples = traces.shape
    rows = chans * minutes
    anywhere = pl.BlockSpec(memory_space=pltpu.HBM)
    return pl.pallas_call(
        whiten_kernel,
        out_shape=jax.ShapeDtypeStruct((rows, 2 * LANES), jnp.bfloat16),
        in_specs=[anywhere] * 3,
        out_specs=pl.BlockSpec(memory_space=pltpu.VMEM),
        scratch_shapes=[
            pltpu.VMEM((chans, minutes, samples), jnp.bfloat16),
            pltpu.VMEM((minutes, chans), jnp.int32),
            pltpu.VMEM((FOLD, 5 * 256), jnp.bfloat16),
            pltpu.VMEM((LANES, LANES), jnp.bfloat16),
            pltpu.SemaphoreType.DMA((5,)),
        ],
        compiler_params=pltpu.CompilerParams(vmem_limit_bytes=WHITEN_VMEM),
        name="whiten",
    )(traces, valid_mask.T, jnp.asarray(fold_table()))


def cross_tile(own, part, chans, cross, j):
    minutes = own.shape[0] // chans
    for a in range(0, chans, 2):
        both_re, both_im = [], []
        for channel in (a, a + 1):
            re = im = None
            for m in range(minutes):
                row = m * chans + channel
                o_re, o_im = own[row : row + 1, :LANES], own[row : row + 1, LANES:]
                p_re = part[m * chans : (m + 1) * chans, :LANES]
                p_im = part[m * chans : (m + 1) * chans, LANES:]
                r = o_re * p_re + o_im * p_im
                i = o_im * p_re - o_re * p_im
                re = r if re is None else re + r
                im = i if im is None else im + i
            both_re.append(re)
            both_im.append(im)
        rows = slice((j * chans + a) * chans, (j * chans + a + 2) * chans)
        cross[rows, :LANES] = jnp.concatenate(both_re, axis=0).astype(jnp.bfloat16)
        cross[rows, LANES:] = jnp.concatenate(both_im, axis=0).astype(jnp.bfloat16)


def lag_product(cross, table, shape):
    full = jnp.dot(cross, table, preferred_element_type=jnp.float32)
    scale = (1.0 / math.sqrt(BINS)) / jnp.maximum(full[:, COLS - 1 :], 1.0)
    return (full * scale)[:, :LAGS].reshape(shape)


def corr_kernel(pick, slots_ref, panels_ref, lag_ref, stack_ref, out_ref, cross):
    step = pl.program_id(0)
    count, chans = out_ref.shape[0], out_ref.shape[1]
    own = panels_ref[pick(lax.axis_index("row"))].astype(jnp.float32)
    for j in range(count):
        part = panels_ref[pick(slots_ref[0, step * count + j])].astype(jnp.float32)
        cross_tile(own, part, chans, cross, j)
    corr = lag_product(cross[...], lag_ref[...], out_ref.shape)
    out_ref[...] = stack_ref[pl.ds(step * count, count)] + corr


def correlate(pick, slots, panels, stack):
    offsets, chans = stack.shape[0], stack.shape[1]
    chunk = max(d for d in range(1, 7) if offsets % d == 0)
    whole = pl.BlockSpec(memory_space=pltpu.VMEM)
    return pl.pallas_call(
        functools.partial(corr_kernel, pick),
        out_shape=jax.ShapeDtypeStruct(stack.shape, jnp.float32),
        grid_spec=pltpu.PrefetchScalarGridSpec(
            num_scalar_prefetch=1,
            grid=(offsets // chunk,),
            in_specs=[whole, whole, whole],
            out_specs=pl.BlockSpec((chunk, chans, chans, LAGS), lambda i, s: (i, 0, 0, 0)),
            scratch_shapes=[pltpu.VMEM((chunk * chans * chans, panels.shape[2]), jnp.bfloat16)],
        ),
        compiler_params=pltpu.CompilerParams(vmem_limit_bytes=CORR_VMEM),
        name="correlate",
    )(slots, panels, jnp.asarray(lag_table()), stack)


def gather_all(own, slots, stack):
    panels = lax.all_gather(own, "row", axis=0)
    return correlate(lambda j: j, slots, panels, stack)


def place(panel_count):
    me = lax.axis_index("row")
    return me, me // 2, lax.rem(me, 2), lax.rem(me // 2, 2)


def first_hop(panel_count):
    me, chip, core, odd = place(panel_count)
    a = jnp.where(core == 0, chip + 1 - 2 * odd, chip + 2)
    b = jnp.where(core == 0, chip - 1 + 4 * odd, chip + 3 - 2 * odd)
    return a, b


def pair_panels(panel_count):
    me, chip, core, odd = place(panel_count)
    return [(0, me, True), (1, me + 1 - 2 * core, True)]


def near_panels(panel_count):
    me, chip, core, odd = place(panel_count)
    a, b = first_hop(panel_count)
    pairs = [(2 * i + t, 2 * c + (core if t == 0 else 1 - core), True) for i, c in enumerate((a, b)) for t in range(2)]
    for i, here in ((0, odd == 1), (2, odd == 0)):
        pairs[i] = (i, pairs[i][1], (core == 1) | jnp.logical_not(here))
    return pairs + [(4, me + 8, True)]


def swapped_panels(panel_count):
    me, chip, core, odd = place(panel_count)
    found = []
    for t in range(2):
        ahead = jnp.where(core == 0, chip + 2, chip + 1 + 2 * odd)
        found.append((2 * odd * core + t, 2 * ahead + (1 - core if t == 0 else core), True))
    for t in range(2):
        ahead = 2 * (chip + 3 - 2 * odd) + 1 - t
        wanted = True if t == 0 else core == 0
        found.append((jnp.where(core == 0, 2 + t, 4), jnp.where(core == 0, ahead, 2 * chip + 8), wanted))
    return found


def products(which, panel_count, own, panels_ref, table, chans, cross, keep):
    found = which(panel_count)
    for start in range(0, len(found), 2):
        some = found[start : start + 2]
        for j, (at, panel, wanted) in enumerate(some):
            cross_tile(own, panels_ref[at].astype(jnp.float32), chans, cross, start + j)
        rows = slice(start * chans * chans, (start + len(some)) * chans * chans)
        full = jnp.dot(cross[rows], table, preferred_element_type=jnp.float32)
        scale = (1.0 / math.sqrt(BINS)) / jnp.maximum(full[:, COLS - 1 :], 1.0)
        keep(start, (full * scale).reshape(len(some), chans * chans, COLS))


def early_kernel(panel_count, which, pair_ref, panels_ref, table_ref, out_ref, cross):
    own = pair_ref[0].astype(jnp.float32)

    def keep(start, corr):
        out_ref[start : start + corr.shape[0]] = corr

    products(which, panel_count, own, panels_ref, table_ref[...], own.shape[0] // SEGS, cross, keep)


def early(which, count, panel_count, chans, pair, panels, table):
    whole = pl.BlockSpec(memory_space=pltpu.VMEM)
    rows = count * chans * chans
    return pl.pallas_call(
        functools.partial(early_kernel, panel_count, which),
        out_shape=jax.ShapeDtypeStruct((count, chans * chans, COLS), jnp.float32),
        in_specs=[whole] * 3,
        out_specs=whole,
        scratch_shapes=[pltpu.VMEM((rows, 2 * LANES), jnp.bfloat16)],
        compiler_params=pltpu.CompilerParams(vmem_limit_bytes=CORR_VMEM),
        cost_estimate=pl.CostEstimate(flops=4 * rows * LANES * COLS, bytes_accessed=4 * rows * COLS, transcendentals=0),
        name=which.__name__,
    )(pair, panels, table)


def last_kernel(panel_count, lists, slots_any, pair_ref, panels_ref, table_ref, stack_ref, *refs):
    done_refs = refs[: len(lists) - 1]
    out_ref, slots_ref, cross, result, sem = refs[len(lists) - 1 :]
    offsets, chans = stack_ref.shape[0], stack_ref.shape[1]
    fetch_slots = pltpu.make_async_copy(slots_any, slots_ref, sem.at[sem.shape[0] - 1])
    fetch_slots.start()
    own = pair_ref[0].astype(jnp.float32)
    copies = []

    def only(wanted, act):
        if wanted is True:
            act()
        else:
            pl.when(wanted)(act)

    def finish(found, corr):
        for j, (at, panel, wanted) in enumerate(found):
            panel = lax.rem(panel + panel_count, panel_count)
            slot = jnp.int32(0)
            for o in range(1, offsets):
                slot = jnp.where(slots_ref[0, o] == panel, o, slot)
            n = len(copies)
            result[n] = stack_ref[slot] + corr[j][:, :LAGS].reshape(chans, chans, LAGS)
            copy = pltpu.make_async_copy(result.at[n], out_ref.at[slot], sem.at[n])
            copies.append((wanted, copy))
            only(wanted, copy.start)

    found = lists[-1](panel_count)

    def keep(start, corr):
        if start == 0:
            fetch_slots.wait()
            for which, done in zip(lists, done_refs):
                finish(which(panel_count), done)
        finish(found[start : start + corr.shape[0]], corr)

    products(lists[-1], panel_count, own, panels_ref, table_ref[...], chans, cross, keep)
    for wanted, copy in copies:
        only(wanted, copy.wait)


def last(lists, counts, panel_count, slots, pair, panels, table, stack, *done):
    offsets, chans = stack.shape[0], stack.shape[1]
    whole = pl.BlockSpec(memory_space=pltpu.VMEM)
    rows = counts[-1] * chans * chans
    return pl.pallas_call(
        functools.partial(last_kernel, panel_count, lists),
        out_shape=jax.ShapeDtypeStruct(stack.shape, jnp.float32),
        in_specs=[whole] * (5 + len(done)),
        out_specs=pl.BlockSpec(memory_space=pltpu.HBM),
        scratch_shapes=[
            pltpu.SMEM(slots.shape, jnp.int32),
            pltpu.VMEM((rows, 2 * LANES), jnp.bfloat16),
            pltpu.VMEM((sum(counts), chans, chans, LAGS), jnp.float32),
            pltpu.SemaphoreType.DMA((sum(counts) + 1,)),
        ],
        compiler_params=pltpu.CompilerParams(vmem_limit_bytes=CORR_VMEM),
        cost_estimate=pl.CostEstimate(flops=4 * rows * LANES * COLS, bytes_accessed=4 * rows * COLS, transcendentals=0),
        name=lists[-1].__name__,
    )(slots, pair, panels, table, stack, *done)


def gather_near(own, slots, stack, panel_count):
    chips = panel_count // 2
    def swap(array):
        return lax.ppermute(array, "row", [(i ^ 1, i) for i in range(panel_count)])

    def fetch(array, even, odd):
        ahead = [even, odd]
        moves = []
        for i in range(panel_count):
            c = i // 2
            moves.append((2 * ((c + ahead[i % 2][c % 2]) % chips) + i % 2, i))
        return lax.ppermute(array, "row", moves)

    table = jnp.asarray(lag_table())
    twice = jnp.stack([own, own])
    pair = lax.optimization_barrier(lax.dynamic_update_slice(twice, swap(own)[None], (1, 0, 0)))
    near = fetch(pair, (1, -1), (2, 2))
    next_near = fetch(pair, (-1, 3), (3, 1))
    far = fetch(pair[0], (4, 4), (4, 4))
    chans = stack.shape[1]
    first = early(pair_panels, 2, panel_count, chans, pair, pair, table)
    near, next_near, far, first = lax.optimization_barrier((near, next_near, far, first))
    five = jnp.concatenate([near, next_near, far[None]], axis=0)
    swapped = swap(five)
    second = early(near_panels, 5, panel_count, chans, pair, five, table)
    lists = (pair_panels, near_panels, swapped_panels)
    return last(lists, (2, 5, 4), panel_count, slots, pair, swapped, table, stack, first, second)


def shards(traces, valid_mask, pair_table, stack_in):
    own = whiten(traces, valid_mask)
    panel_count = lax.axis_size("row")
    if pair_table.shape[1] == 10 and panel_count >= 12 and panel_count % 4 == 0:
        return gather_near(own, pair_table, stack_in[0], panel_count)[None]
    return gather_all(own, pair_table, stack_in[0])[None]


def solution(mesh):
    in_specs = (
        P(("parts", "row"), None, None),
        P(("parts", "row"), None),
        P(("parts", "row"), None),
        P(("parts", "row"), None, None, None, None),
    )
    out_specs = P(("parts", "row"), None, None, None, None)
    return jax.shard_map(shards, mesh=mesh, in_specs=in_specs, out_specs=out_specs, check_vma=False)
```

```python
import functools
import math

import jax
import jax.numpy as jnp
import ml_dtypes
import numpy as np
from jax import lax
from jax.experimental import pallas as pl
from jax.experimental.pallas import tpu as pltpu
from jax.sharding import PartitionSpec as P

SAMPLES = 12000
FLO = 6
BINS = 595
SEGS = 2
HALF = 40
LAGS = 401
EPS = 1e-06
WHITEN_VMEM = 60 << 20
CORR_VMEM = 24 << 20

SPLIT = 20
FOLD = SAMPLES // SPLIT
LANES = 640
RUN = 32
COLS = 512


def bin_at(lane):
    residue = lane // 128 + 5 * (lane % 128 // RUN)
    return residue + SPLIT * (residue < FLO) + SPLIT * (lane % RUN)


BIN_OF = bin_at(np.arange(LANES))
USED = BIN_OF < FLO + BINS
GROUPS = ((1, 4), (2, 3), (0,))


def bf16(a):
    return np.asarray(a, np.float32).astype(ml_dtypes.bfloat16)


def fold_table():
    q = (np.arange(FOLD)[:, None] * BIN_OF[None, :]) % SAMPLES
    angle = 2.0 * np.pi * q / SAMPLES
    cos = np.where(USED, np.cos(angle), 0.0).reshape(FOLD, 5, 1, 128)
    sin = np.where(USED, -np.sin(angle), 0.0).reshape(FOLD, 5, 1, 128)
    table = np.concatenate([cos, sin], axis=2)
    order = [group for some in GROUPS for group in some]
    return bf16(table[:, order].reshape(FOLD, 5 * 256))


def lag_table():
    tau = np.arange(LAGS) - (LAGS - 1) // 2
    q = (BIN_OF[:, None] * tau[None, :]) % SAMPLES
    angle = 2.0 * np.pi * q / SAMPLES
    table = np.zeros((2 * LANES, COLS), np.float64)
    table[:LANES, :LAGS] = np.where(USED[:, None], np.cos(angle), 0.0)
    table[LANES:, :LAGS] = np.where(USED[:, None], -np.sin(angle), 0.0)
    table[LANES - 1, COLS - 1] = 1.0
    return bf16(table)


def cosine(n, of):
    return math.cos(2.0 * math.pi * n / of)


def sine(n, of):
    return math.sin(2.0 * math.pi * n / of)


def ten_point(s):
    e = [s[n] + s[n + 5] for n in range(5)]
    d = [s[n] - s[n + 5] for n in range(5)]
    c1, c2, s1, s2 = cosine(1, 10), cosine(2, 10), sine(1, 10), sine(2, 10)
    e14, e23, f14, f23 = e[1] + e[4], e[2] + e[3], e[1] - e[4], e[2] - e[3]
    d14, d23, g14, g23 = d[1] + d[4], d[2] + d[3], d[1] - d[4], d[2] - d[3]
    y0 = (e[0] + e14 + e23, None)
    y2 = (e[0] + c2 * e14 - c1 * e23, s2 * f14 + s1 * f23)
    y4 = (e[0] - c1 * e14 + c2 * e23, s1 * f14 - s2 * f23)
    y1 = (d[0] + c1 * g14 + c2 * g23, s1 * d14 + s2 * d23)
    y3 = (d[0] - c2 * g14 - c1 * g23, s2 * d14 - s1 * d23)
    y5 = (d[0] - g14 + g23, None)
    return [y0, y1, y2, y3, y4, y5]


def twenty_point(s):
    y = [None] * 11
    y[0::2] = ten_point([s[n] + s[n + 10] for n in range(10)])
    d = [s[n] - s[n + 10] for n in range(10)]
    g1, g2, g3, g4 = (d[n] - d[10 - n] for n in range(1, 5))
    h1, h2, h3, h4 = (d[n] + d[10 - n] for n in range(1, 5))
    for k, turn in ((1, d[5]), (3, -d[5])):
        even = d[0] + cosine(2 * k, 20) * g2 + cosine(4 * k, 20) * g4
        odd = cosine(k, 20) * g1 + cosine(3 * k, 20) * g3
        even_sin = sine(2 * k, 20) * h2 + sine(4 * k, 20) * h4
        odd_sin = sine(k, 20) * h1 + sine(3 * k, 20) * h3 + turn
        y[k] = (even + odd, odd_sin + even_sin)
        y[10 - k] = (even - odd, odd_sin - even_sin)
    y[5] = (d[0] - g2 + g4, h1 - h3 + d[5])
    return y


def hi_lo(y):
    hi = y.astype(jnp.bfloat16)
    return [hi, (y - hi.astype(jnp.float32)).astype(jnp.bfloat16)]


def whiten_kernel(x_hbm, mask_hbm, table_hbm, out_ref, x_buf, mask_buf, table, near, sem):
    chans, minutes, samples = x_buf.shape
    rows = chans * minutes
    starts = (0, 512, 1024, 1280)
    fetch_x = pltpu.make_async_copy(x_hbm, x_buf, sem.at[0])
    fetch_mask = pltpu.make_async_copy(mask_hbm, mask_buf, sem.at[1])
    fetch_table = [
        pltpu.make_async_copy(table_hbm.at[:, pl.ds(a, b - a)], table.at[:, pl.ds(a, b - a)], sem.at[2 + i])
        for i, (a, b) in enumerate(zip(starts, starts[1:]))
    ]
    for copy in [fetch_x, fetch_mask] + fetch_table:
        copy.start()

    down = bin_at(lax.broadcasted_iota(jnp.int32, (LANES, 128), 0))
    down = jnp.where(down < FLO + BINS, down, -SAMPLES)
    lanes = bin_at(lax.broadcasted_iota(jnp.int32, (8, LANES), 1))
    for group in range(5):
        across = jnp.broadcast_to(lanes[:1, group * 128 : (group + 1) * 128], (LANES, 128))
        close = (jnp.abs(down - across) <= HALF) & (across < FLO + BINS)
        near[:, group * 128 : (group + 1) * 128] = jnp.where(close, 1.0, 0.0).astype(jnp.bfloat16)
    bins = lanes[:1]
    count = jnp.minimum(bins + HALF, FLO + BINS - 1) - jnp.maximum(bins - HALF, FLO) + 1
    inverse = 1.0 / jnp.maximum(count, 1).astype(jnp.float32)

    fetch_x.wait()
    x = jnp.swapaxes(x_buf[...], 0, 1).reshape(rows, samples)
    y = twenty_point([x[:, FOLD * n : FOLD * (n + 1)].astype(jnp.float32) for n in range(SPLIT)])
    run = lax.broadcasted_iota(jnp.int32, (rows, 128), 1) // RUN
    for copy in [fetch_mask] + fetch_table:
        copy.wait()
    real = [None] * 5
    imag = [None] * 5
    for part, groups in enumerate(GROUPS):
        wanted = sorted({min(k, SPLIT - k) for g in groups for k in range(g, SPLIT, 5)})
        pieces = [(k, i) for k in wanted for i in range(2) if y[k][i] is not None]
        halves = [hi_lo(y[k][i]) for k, i in pieces]
        left = jnp.concatenate([half[j] for j in range(2) for half in halves], axis=0)
        at = starts[part]
        full = jnp.dot(left, table[:, at : starts[part + 1]], preferred_element_type=jnp.float32)
        got = {
            p: full[rows * i : rows * (i + 1)] + full[rows * (len(pieces) + i) : rows * (len(pieces) + i + 1)]
            for i, p in enumerate(pieces)
        }
        for place, group in enumerate(groups):
            cos = slice(place * 256, place * 256 + 128)
            sin = slice(place * 256 + 128, place * 256 + 256)
            re = im = None
            for q in range(4):
                k = group + 5 * q
                same = min(k, SPLIT - k)
                a = got[(same, 0)]
                r, i = a[:, cos], a[:, sin]
                if (same, 1) in got:
                    b = got[(same, 1)]
                    if k == same:
                        r, i = r + b[:, sin], i - b[:, cos]
                    else:
                        r, i = r - b[:, sin], i + b[:, cos]
                re = r if re is None else jnp.where(run == q, r, re)
                im = i if im is None else jnp.where(run == q, i, im)
            real[group], imag[group] = re, im
    re = jnp.concatenate(real, axis=1)
    im = jnp.concatenate(imag, axis=1)
    power = re * re + im * im
    hi, mid = hi_lo(power)
    low = (power - hi.astype(jnp.float32) - mid.astype(jnp.float32)).astype(jnp.bfloat16)
    sums = jnp.dot(jnp.concatenate([hi, mid, low], axis=0), near[...], preferred_element_type=jnp.float32)
    smooth = (sums[:rows] + sums[rows : 2 * rows] + sums[2 * rows :]) * inverse
    mask = mask_buf[...].astype(jnp.float32)
    spread = jnp.concatenate([jnp.broadcast_to(mask[m : m + 1], (chans, chans)) for m in range(minutes)], axis=0)
    own = lax.broadcasted_iota(jnp.int32, (rows, chans), 0) % chans
    other = lax.broadcasted_iota(jnp.int32, (rows, chans), 1)
    flags = jnp.sum(jnp.where(own == other, spread, 0.0), axis=1, keepdims=True)
    factor = flags * lax.rsqrt(smooth + EPS)
    last = lax.broadcasted_iota(jnp.int32, (rows, LANES), 1) == LANES - 1
    out_ref[:, :LANES] = (re * factor).astype(jnp.bfloat16)
    out_ref[:, LANES:] = jnp.where(last, flags, im * factor).astype(jnp.bfloat16)


def whiten(traces, valid_mask):
    chans, minutes, samples = traces.shape
    rows = chans * minutes
    anywhere = pl.BlockSpec(memory_space=pltpu.HBM)
    return pl.pallas_call(
        whiten_kernel,
        out_shape=pltpu.VMEM((rows, 2 * LANES), jnp.bfloat16),
        in_specs=[anywhere] * 3,
        out_specs=pl.BlockSpec(memory_space=pltpu.VMEM),
        scratch_shapes=[
            pltpu.VMEM((chans, minutes, samples), jnp.bfloat16),
            pltpu.VMEM((minutes, chans), jnp.int32),
            pltpu.VMEM((FOLD, 5 * 256), jnp.bfloat16),
            pltpu.VMEM((LANES, LANES), jnp.bfloat16),
            pltpu.SemaphoreType.DMA((5,)),
        ],
        compiler_params=pltpu.CompilerParams(vmem_limit_bytes=WHITEN_VMEM),
        name="whiten",
    )(traces, valid_mask.T, jnp.asarray(fold_table()))


def cross_tile(own, part, chans, cross, j):
    minutes = own.shape[0] // chans
    for a in range(0, chans, 2):
        both_re, both_im = [], []
        for channel in (a, a + 1):
            re = im = None
            for m in range(minutes):
                row = m * chans + channel
                o_re, o_im = own[row : row + 1, :LANES], own[row : row + 1, LANES:]
                p_re = part[m * chans : (m + 1) * chans, :LANES]
                p_im = part[m * chans : (m + 1) * chans, LANES:]
                r = o_re * p_re + o_im * p_im
                i = o_im * p_re - o_re * p_im
                re = r if re is None else re + r
                im = i if im is None else im + i
            both_re.append(re)
            both_im.append(im)
        rows = slice((j * chans + a) * chans, (j * chans + a + 2) * chans)
        cross[rows, :LANES] = jnp.concatenate(both_re, axis=0).astype(jnp.bfloat16)
        cross[rows, LANES:] = jnp.concatenate(both_im, axis=0).astype(jnp.bfloat16)


def lag_product(cross, table, shape):
    full = jnp.dot(cross, table, preferred_element_type=jnp.float32)
    scale = (1.0 / math.sqrt(BINS)) / jnp.maximum(full[:, COLS - 1 :], 1.0)
    return (full * scale)[:, :LAGS].reshape(shape)


def corr_kernel(pick, slots_ref, panels_ref, lag_ref, stack_ref, out_ref, cross):
    step = pl.program_id(0)
    count, chans = out_ref.shape[0], out_ref.shape[1]
    own = panels_ref[pick(lax.axis_index("row"))].astype(jnp.float32)
    for j in range(count):
        part = panels_ref[pick(slots_ref[0, step * count + j])].astype(jnp.float32)
        cross_tile(own, part, chans, cross, j)
    corr = lag_product(cross[...], lag_ref[...], out_ref.shape)
    out_ref[...] = stack_ref[pl.ds(step * count, count)] + corr


def correlate(pick, slots, panels, stack):
    offsets, chans = stack.shape[0], stack.shape[1]
    chunk = max(d for d in range(1, 7) if offsets % d == 0)
    whole = pl.BlockSpec(memory_space=pltpu.VMEM)
    return pl.pallas_call(
        functools.partial(corr_kernel, pick),
        out_shape=jax.ShapeDtypeStruct(stack.shape, jnp.float32),
        grid_spec=pltpu.PrefetchScalarGridSpec(
            num_scalar_prefetch=1,
            grid=(offsets // chunk,),
            in_specs=[whole, whole, whole],
            out_specs=pl.BlockSpec((chunk, chans, chans, LAGS), lambda i, s: (i, 0, 0, 0)),
            scratch_shapes=[pltpu.VMEM((chunk * chans * chans, panels.shape[2]), jnp.bfloat16)],
        ),
        compiler_params=pltpu.CompilerParams(vmem_limit_bytes=CORR_VMEM),
        name="correlate",
    )(slots, panels, jnp.asarray(lag_table()), stack)


def gather_all(own, slots, stack):
    panels = lax.all_gather(own, "row", axis=0)
    return correlate(lambda j: j, slots, panels, stack)


def place(panel_count):
    me = lax.axis_index("row")
    return me, me // 2, lax.rem(me, 2), lax.rem(me // 2, 2)


def first_hop(panel_count):
    me, chip, core, odd = place(panel_count)
    a = jnp.where(core == 0, chip + 1 - 2 * odd, chip + 2)
    b = jnp.where(core == 0, chip - 1 + 4 * odd, chip + 3 - 2 * odd)
    return a, b


def pair_panels(panel_count):
    me, chip, core, odd = place(panel_count)
    return [(0, me, True), (1, me + 1 - 2 * core, True)]


def near_panels(panel_count):
    me, chip, core, odd = place(panel_count)
    a, b = first_hop(panel_count)
    pairs = [(2 * i + t, 2 * c + (core if t == 0 else 1 - core), True) for i, c in enumerate((a, b)) for t in range(2)]
    for i, here in ((0, odd == 1), (2, odd == 0)):
        pairs[i] = (i, pairs[i][1], (core == 1) | jnp.logical_not(here))
    return pairs + [(4, me + 8, True)]


def swapped_panels(panel_count):
    me, chip, core, odd = place(panel_count)
    found = []
    for t in range(2):
        ahead = jnp.where(core == 0, chip + 2, chip + 1 + 2 * odd)
        found.append((2 * odd * core + t, 2 * ahead + (1 - core if t == 0 else core), True))
    for t in range(2):
        ahead = 2 * (chip + 3 - 2 * odd) + 1 - t
        wanted = True if t == 0 else core == 0
        found.append((jnp.where(core == 0, 2 + t, 4), jnp.where(core == 0, ahead, 2 * chip + 8), wanted))
    return found


def products(which, panel_count, own, panels_ref, table, chans, cross, keep):
    found = which(panel_count)
    for start in range(0, len(found), 2):
        some = found[start : start + 2]
        for j, (at, panel, wanted) in enumerate(some):
            cross_tile(own, panels_ref[at].astype(jnp.float32), chans, cross, start + j)
        rows = slice(start * chans * chans, (start + len(some)) * chans * chans)
        full = jnp.dot(cross[rows], table, preferred_element_type=jnp.float32)
        scale = (1.0 / math.sqrt(BINS)) / jnp.maximum(full[:, COLS - 1 :], 1.0)
        keep(start, (full * scale).reshape(len(some), chans * chans, COLS))


def early_kernel(panel_count, which, pair_ref, panels_ref, table_ref, out_ref, cross):
    own = pair_ref[0].astype(jnp.float32)

    def keep(start, corr):
        out_ref[start : start + corr.shape[0]] = corr

    products(which, panel_count, own, panels_ref, table_ref[...], own.shape[0] // SEGS, cross, keep)


def early(which, count, panel_count, chans, pair, panels, table):
    whole = pl.BlockSpec(memory_space=pltpu.VMEM)
    rows = count * chans * chans
    return pl.pallas_call(
        functools.partial(early_kernel, panel_count, which),
        out_shape=jax.ShapeDtypeStruct((count, chans * chans, COLS), jnp.float32),
        in_specs=[whole] * 3,
        out_specs=whole,
        scratch_shapes=[pltpu.VMEM((rows, 2 * LANES), jnp.bfloat16)],
        compiler_params=pltpu.CompilerParams(vmem_limit_bytes=CORR_VMEM),
        cost_estimate=pl.CostEstimate(flops=4 * rows * LANES * COLS, bytes_accessed=4 * rows * COLS, transcendentals=0),
        name=which.__name__,
    )(pair, panels, table)


def last_kernel(panel_count, lists, slots_any, pair_ref, panels_ref, table_ref, stack_ref, *refs):
    done_refs = refs[: len(lists) - 1]
    out_ref, slots_ref, cross, result, sem = refs[len(lists) - 1 :]
    offsets, chans = stack_ref.shape[0], stack_ref.shape[1]
    fetch_slots = pltpu.make_async_copy(slots_any, slots_ref, sem.at[sem.shape[0] - 1])
    fetch_slots.start()
    own = pair_ref[0].astype(jnp.float32)
    copies = []

    def only(wanted, act):
        if wanted is True:
            act()
        else:
            pl.when(wanted)(act)

    def finish(found, corr):
        for j, (at, panel, wanted) in enumerate(found):
            panel = lax.rem(panel + panel_count, panel_count)
            slot = jnp.int32(0)
            for o in range(1, offsets):
                slot = jnp.where(slots_ref[0, o] == panel, o, slot)
            n = len(copies)
            result[n] = stack_ref[slot] + corr[j][:, :LAGS].reshape(chans, chans, LAGS)
            copy = pltpu.make_async_copy(result.at[n], out_ref.at[slot], sem.at[n])
            copies.append((wanted, copy))
            only(wanted, copy.start)

    found = lists[-1](panel_count)

    def keep(start, corr):
        if start == 0:
            fetch_slots.wait()
            for which, done in zip(lists, done_refs):
                finish(which(panel_count), done)
        finish(found[start : start + corr.shape[0]], corr)

    products(lists[-1], panel_count, own, panels_ref, table_ref[...], chans, cross, keep)
    for wanted, copy in copies:
        only(wanted, copy.wait)


def last(lists, counts, panel_count, slots, pair, panels, table, stack, *done):
    offsets, chans = stack.shape[0], stack.shape[1]
    whole = pl.BlockSpec(memory_space=pltpu.VMEM)
    rows = counts[-1] * chans * chans
    return pl.pallas_call(
        functools.partial(last_kernel, panel_count, lists),
        out_shape=jax.ShapeDtypeStruct(stack.shape, jnp.float32),
        in_specs=[whole] * (5 + len(done)),
        out_specs=pl.BlockSpec(memory_space=pltpu.HBM),
        scratch_shapes=[
            pltpu.SMEM(slots.shape, jnp.int32),
            pltpu.VMEM((rows, 2 * LANES), jnp.bfloat16),
            pltpu.VMEM((sum(counts), chans, chans, LAGS), jnp.float32),
            pltpu.SemaphoreType.DMA((sum(counts) + 1,)),
        ],
        compiler_params=pltpu.CompilerParams(vmem_limit_bytes=CORR_VMEM),
        cost_estimate=pl.CostEstimate(flops=4 * rows * LANES * COLS, bytes_accessed=4 * rows * COLS, transcendentals=0),
        name=lists[-1].__name__,
    )(slots, pair, panels, table, stack, *done)


def gather_near(own, slots, stack, panel_count):
    chips = panel_count // 2
    def swap(array):
        return lax.ppermute(array, "row", [(i ^ 1, i) for i in range(panel_count)])

    def fetch(array, even, odd):
        ahead = [even, odd]
        moves = []
        for i in range(panel_count):
            c = i // 2
            moves.append((2 * ((c + ahead[i % 2][c % 2]) % chips) + i % 2, i))
        return lax.ppermute(array, "row", moves)

    table = jnp.asarray(lag_table())
    twice = jnp.stack([own, own])
    pair = lax.optimization_barrier(lax.dynamic_update_slice(twice, swap(own)[None], (1, 0, 0)))
    near = fetch(pair, (1, -1), (2, 2))
    next_near = fetch(pair, (-1, 3), (3, 1))
    far = fetch(pair[0], (4, 4), (4, 4))
    chans = stack.shape[1]
    first = early(pair_panels, 2, panel_count, chans, pair, pair, table)
    near, next_near, far, first = lax.optimization_barrier((near, next_near, far, first))
    five = jnp.concatenate([near, next_near, far[None]], axis=0)
    swapped = swap(five)
    second = early(near_panels, 5, panel_count, chans, pair, five, table)
    lists = (pair_panels, near_panels, swapped_panels)
    return last(lists, (2, 5, 4), panel_count, slots, pair, swapped, table, stack, first, second)


def shards(traces, valid_mask, pair_table, stack_in):
    own = whiten(traces, valid_mask)
    panel_count = lax.axis_size("row")
    if pair_table.shape[1] == 10 and panel_count >= 12 and panel_count % 4 == 0:
        return gather_near(own, pair_table, stack_in[0], panel_count)[None]
    return gather_all(own, pair_table, stack_in[0])[None]


def solution(mesh):
    in_specs = (
        P(("parts", "row"), None, None),
        P(("parts", "row"), None),
        P(("parts", "row"), None),
        P(("parts", "row"), None, None, None, None),
    )
    out_specs = P(("parts", "row"), None, None, None, None)
    return jax.shard_map(shards, mesh=mesh, in_specs=in_specs, out_specs=out_specs, check_vma=False)
```

```python
import functools
import math

import jax
import jax.numpy as jnp
import ml_dtypes
import numpy as np
from jax import lax
from jax.experimental import pallas as pl
from jax.experimental.pallas import tpu as pltpu
from jax.sharding import PartitionSpec as P

SAMPLES = 12000
FLO = 6
BINS = 595
SEGS = 2
HALF = 40
LAGS = 401
EPS = 1e-06
WHITEN_VMEM = 60 << 20
CORR_VMEM = 24 << 20

SPLIT = 20
FOLD = SAMPLES // SPLIT
LANES = 640
RUN = 32
COLS = 512


def bin_at(lane):
    residue = lane // 128 + 5 * (lane % 128 // RUN)
    return residue + SPLIT * (residue < FLO) + SPLIT * (lane % RUN)


BIN_OF = bin_at(np.arange(LANES))
USED = BIN_OF < FLO + BINS
GROUPS = ((1, 4), (2, 3), (0,))


def bf16(a):
    return np.asarray(a, np.float32).astype(ml_dtypes.bfloat16)


def fold_table():
    q = (np.arange(FOLD)[:, None] * BIN_OF[None, :]) % SAMPLES
    angle = 2.0 * np.pi * q / SAMPLES
    cos = np.where(USED, np.cos(angle), 0.0).reshape(FOLD, 5, 1, 128)
    sin = np.where(USED, -np.sin(angle), 0.0).reshape(FOLD, 5, 1, 128)
    table = np.concatenate([cos, sin], axis=2)
    order = [group for some in GROUPS for group in some]
    return bf16(table[:, order].reshape(FOLD, 5 * 256))


def lag_table():
    tau = np.arange(LAGS) - (LAGS - 1) // 2
    q = (BIN_OF[:, None] * tau[None, :]) % SAMPLES
    angle = 2.0 * np.pi * q / SAMPLES
    table = np.zeros((2 * LANES, COLS), np.float64)
    table[:LANES, :LAGS] = np.where(USED[:, None], np.cos(angle), 0.0)
    table[LANES:, :LAGS] = np.where(USED[:, None], -np.sin(angle), 0.0)
    table[LANES - 1, COLS - 1] = 1.0
    return bf16(table)


def cosine(n, of):
    return math.cos(2.0 * math.pi * n / of)


def sine(n, of):
    return math.sin(2.0 * math.pi * n / of)


def ten_point(s):
    e = [s[n] + s[n + 5] for n in range(5)]
    d = [s[n] - s[n + 5] for n in range(5)]
    c1, c2, s1, s2 = cosine(1, 10), cosine(2, 10), sine(1, 10), sine(2, 10)
    e14, e23, f14, f23 = e[1] + e[4], e[2] + e[3], e[1] - e[4], e[2] - e[3]
    d14, d23, g14, g23 = d[1] + d[4], d[2] + d[3], d[1] - d[4], d[2] - d[3]
    y0 = (e[0] + e14 + e23, None)
    y2 = (e[0] + c2 * e14 - c1 * e23, s2 * f14 + s1 * f23)
    y4 = (e[0] - c1 * e14 + c2 * e23, s1 * f14 - s2 * f23)
    y1 = (d[0] + c1 * g14 + c2 * g23, s1 * d14 + s2 * d23)
    y3 = (d[0] - c2 * g14 - c1 * g23, s2 * d14 - s1 * d23)
    y5 = (d[0] - g14 + g23, None)
    return [y0, y1, y2, y3, y4, y5]


def twenty_point(s):
    y = [None] * 11
    y[0::2] = ten_point([s[n] + s[n + 10] for n in range(10)])
    d = [s[n] - s[n + 10] for n in range(10)]
    g1, g2, g3, g4 = (d[n] - d[10 - n] for n in range(1, 5))
    h1, h2, h3, h4 = (d[n] + d[10 - n] for n in range(1, 5))
    for k, turn in ((1, d[5]), (3, -d[5])):
        even = d[0] + cosine(2 * k, 20) * g2 + cosine(4 * k, 20) * g4
        odd = cosine(k, 20) * g1 + cosine(3 * k, 20) * g3
        even_sin = sine(2 * k, 20) * h2 + sine(4 * k, 20) * h4
        odd_sin = sine(k, 20) * h1 + sine(3 * k, 20) * h3 + turn
        y[k] = (even + odd, odd_sin + even_sin)
        y[10 - k] = (even - odd, odd_sin - even_sin)
    y[5] = (d[0] - g2 + g4, h1 - h3 + d[5])
    return y


def hi_lo(y):
    hi = y.astype(jnp.bfloat16)
    return [hi, (y - hi.astype(jnp.float32)).astype(jnp.bfloat16)]


def whiten_kernel(x_hbm, mask_hbm, table_hbm, out_ref, x_buf, mask_buf, table, near, sem):
    chans, minutes, samples = x_buf.shape
    rows = chans * minutes
    starts = (0, 512, 1024, 1280)
    fetch_x = pltpu.make_async_copy(x_hbm, x_buf, sem.at[0])
    fetch_mask = pltpu.make_async_copy(mask_hbm, mask_buf, sem.at[1])
    fetch_table = [
        pltpu.make_async_copy(table_hbm.at[:, pl.ds(a, b - a)], table.at[:, pl.ds(a, b - a)], sem.at[2 + i])
        for i, (a, b) in enumerate(zip(starts, starts[1:]))
    ]
    for copy in [fetch_x, fetch_mask] + fetch_table:
        copy.start()

    down = bin_at(lax.broadcasted_iota(jnp.int32, (LANES, 128), 0))
    down = jnp.where(down < FLO + BINS, down, -SAMPLES)
    lanes = bin_at(lax.broadcasted_iota(jnp.int32, (8, LANES), 1))
    for group in range(5):
        across = jnp.broadcast_to(lanes[:1, group * 128 : (group + 1) * 128], (LANES, 128))
        close = (jnp.abs(down - across) <= HALF) & (across < FLO + BINS)
        near[:, group * 128 : (group + 1) * 128] = jnp.where(close, 1.0, 0.0).astype(jnp.bfloat16)
    bins = lanes[:1]
    count = jnp.minimum(bins + HALF, FLO + BINS - 1) - jnp.maximum(bins - HALF, FLO) + 1
    inverse = 1.0 / jnp.maximum(count, 1).astype(jnp.float32)

    fetch_x.wait()
    x = jnp.swapaxes(x_buf[...], 0, 1).reshape(rows, samples)
    y = twenty_point([x[:, FOLD * n : FOLD * (n + 1)].astype(jnp.float32) for n in range(SPLIT)])
    run = lax.broadcasted_iota(jnp.int32, (rows, 128), 1) // RUN
    for copy in [fetch_mask] + fetch_table:
        copy.wait()
    real = [None] * 5
    imag = [None] * 5
    for part, groups in enumerate(GROUPS):
        wanted = sorted({min(k, SPLIT - k) for g in groups for k in range(g, SPLIT, 5)})
        pieces = [(k, i) for k in wanted for i in range(2) if y[k][i] is not None]
        halves = [hi_lo(y[k][i]) for k, i in pieces]
        left = jnp.concatenate([half[j] for j in range(2) for half in halves], axis=0)
        at = starts[part]
        full = jnp.dot(left, table[:, at : starts[part + 1]], preferred_element_type=jnp.float32)
        got = {
            p: full[rows * i : rows * (i + 1)] + full[rows * (len(pieces) + i) : rows * (len(pieces) + i + 1)]
            for i, p in enumerate(pieces)
        }
        for place, group in enumerate(groups):
            cos = slice(place * 256, place * 256 + 128)
            sin = slice(place * 256 + 128, place * 256 + 256)
            re = im = None
            for q in range(4):
                k = group + 5 * q
                same = min(k, SPLIT - k)
                a = got[(same, 0)]
                r, i = a[:, cos], a[:, sin]
                if (same, 1) in got:
                    b = got[(same, 1)]
                    if k == same:
                        r, i = r + b[:, sin], i - b[:, cos]
                    else:
                        r, i = r - b[:, sin], i + b[:, cos]
                re = r if re is None else jnp.where(run == q, r, re)
                im = i if im is None else jnp.where(run == q, i, im)
            real[group], imag[group] = re, im
    re = jnp.concatenate(real, axis=1)
    im = jnp.concatenate(imag, axis=1)
    power = re * re + im * im
    hi, mid = hi_lo(power)
    low = (power - hi.astype(jnp.float32) - mid.astype(jnp.float32)).astype(jnp.bfloat16)
    sums = jnp.dot(jnp.concatenate([hi, mid, low], axis=0), near[...], preferred_element_type=jnp.float32)
    smooth = (sums[:rows] + sums[rows : 2 * rows] + sums[2 * rows :]) * inverse
    mask = mask_buf[...].astype(jnp.float32)
    spread = jnp.concatenate([jnp.broadcast_to(mask[m : m + 1], (chans, chans)) for m in range(minutes)], axis=0)
    own = lax.broadcasted_iota(jnp.int32, (rows, chans), 0) % chans
    other = lax.broadcasted_iota(jnp.int32, (rows, chans), 1)
    flags = jnp.sum(jnp.where(own == other, spread, 0.0), axis=1, keepdims=True)
    factor = flags * lax.rsqrt(smooth + EPS)
    last = lax.broadcasted_iota(jnp.int32, (rows, LANES), 1) == LANES - 1
    out_ref[:, :LANES] = (re * factor).astype(jnp.bfloat16)
    out_ref[:, LANES:] = jnp.where(last, flags, im * factor).astype(jnp.bfloat16)


def whiten(traces, valid_mask):
    chans, minutes, samples = traces.shape
    rows = chans * minutes
    anywhere = pl.BlockSpec(memory_space=pltpu.HBM)
    return pl.pallas_call(
        whiten_kernel,
        out_shape=pltpu.VMEM((rows, 2 * LANES), jnp.bfloat16),
        in_specs=[anywhere] * 3,
        out_specs=pl.BlockSpec(memory_space=pltpu.VMEM),
        scratch_shapes=[
            pltpu.VMEM((chans, minutes, samples), jnp.bfloat16),
            pltpu.VMEM((minutes, chans), jnp.int32),
            pltpu.VMEM((FOLD, 5 * 256), jnp.bfloat16),
            pltpu.VMEM((LANES, LANES), jnp.bfloat16),
            pltpu.SemaphoreType.DMA((5,)),
        ],
        compiler_params=pltpu.CompilerParams(vmem_limit_bytes=WHITEN_VMEM),
        name="whiten",
    )(traces, valid_mask.T, jnp.asarray(fold_table()))


def cross_tile(own, part, chans, cross, j):
    minutes = own.shape[0] // chans
    for a in range(0, chans, 2):
        both_re, both_im = [], []
        for channel in (a, a + 1):
            re = im = None
            for m in range(minutes):
                row = m * chans + channel
                o_re, o_im = own[row : row + 1, :LANES], own[row : row + 1, LANES:]
                p_re = part[m * chans : (m + 1) * chans, :LANES]
                p_im = part[m * chans : (m + 1) * chans, LANES:]
                r = o_re * p_re + o_im * p_im
                i = o_im * p_re - o_re * p_im
                re = r if re is None else re + r
                im = i if im is None else im + i
            both_re.append(re)
            both_im.append(im)
        rows = slice((j * chans + a) * chans, (j * chans + a + 2) * chans)
        cross[rows, :LANES] = jnp.concatenate(both_re, axis=0).astype(jnp.bfloat16)
        cross[rows, LANES:] = jnp.concatenate(both_im, axis=0).astype(jnp.bfloat16)


def lag_product(cross, table, shape):
    full = jnp.dot(cross, table, preferred_element_type=jnp.float32)
    scale = (1.0 / math.sqrt(BINS)) / jnp.maximum(full[:, COLS - 1 :], 1.0)
    return (full * scale)[:, :LAGS].reshape(shape)


def corr_kernel(pick, slots_ref, panels_ref, lag_ref, stack_ref, out_ref, cross):
    step = pl.program_id(0)
    count, chans = out_ref.shape[0], out_ref.shape[1]
    own = panels_ref[pick(lax.axis_index("row"))].astype(jnp.float32)
    for j in range(count):
        part = panels_ref[pick(slots_ref[0, step * count + j])].astype(jnp.float32)
        cross_tile(own, part, chans, cross, j)
    corr = lag_product(cross[...], lag_ref[...], out_ref.shape)
    out_ref[...] = stack_ref[pl.ds(step * count, count)] + corr


def correlate(pick, slots, panels, stack):
    offsets, chans = stack.shape[0], stack.shape[1]
    chunk = max(d for d in range(1, 7) if offsets % d == 0)
    whole = pl.BlockSpec(memory_space=pltpu.VMEM)
    return pl.pallas_call(
        functools.partial(corr_kernel, pick),
        out_shape=jax.ShapeDtypeStruct(stack.shape, jnp.float32),
        grid_spec=pltpu.PrefetchScalarGridSpec(
            num_scalar_prefetch=1,
            grid=(offsets // chunk,),
            in_specs=[whole, whole, whole],
            out_specs=pl.BlockSpec((chunk, chans, chans, LAGS), lambda i, s: (i, 0, 0, 0)),
            scratch_shapes=[pltpu.VMEM((chunk * chans * chans, panels.shape[2]), jnp.bfloat16)],
        ),
        compiler_params=pltpu.CompilerParams(vmem_limit_bytes=CORR_VMEM),
        name="correlate",
    )(slots, panels, jnp.asarray(lag_table()), stack)


def gather_all(own, slots, stack):
    panels = lax.all_gather(own, "row", axis=0)
    return correlate(lambda j: j, slots, panels, stack)


def place(panel_count):
    me = lax.axis_index("row")
    return me, me // 2, lax.rem(me, 2), lax.rem(me // 2, 2)


def first_hop(panel_count):
    me, chip, core, odd = place(panel_count)
    a = jnp.where(core == 0, chip + 1 - 2 * odd, chip + 2)
    b = jnp.where(core == 0, chip - 1 + 4 * odd, chip + 3 - 2 * odd)
    return a, b


def pair_panels(panel_count):
    me, chip, core, odd = place(panel_count)
    return [(0, me, True), (1, me + 1 - 2 * core, True)]


def near_panels(panel_count):
    me, chip, core, odd = place(panel_count)
    a, b = first_hop(panel_count)
    pairs = [(2 * i + t, 2 * c + (core if t == 0 else 1 - core), True) for i, c in enumerate((a, b)) for t in range(2)]
    for i, here in ((0, odd == 1), (2, odd == 0)):
        pairs[i] = (i, pairs[i][1], (core == 1) | jnp.logical_not(here))
    return pairs + [(4, me + 8, True)]


def swapped_panels(panel_count):
    me, chip, core, odd = place(panel_count)
    found = []
    for t in range(2):
        ahead = jnp.where(core == 0, chip + 2, chip + 1 + 2 * odd)
        found.append((t, 2 * ahead + (1 - core if t == 0 else core), True))
    for t in range(2):
        ahead = 2 * (chip + 3 - 2 * odd) + 1 - t
        wanted = True if t == 0 else core == 0
        found.append((2 + t, jnp.where(core == 0, ahead, 2 * chip + 8), wanted))
    return found


def products(which, panel_count, own, panels_ref, table, chans, cross, keep):
    found = which(panel_count)
    for start in range(0, len(found), 2):
        some = found[start : start + 2]
        for j, (at, panel, wanted) in enumerate(some):
            cross_tile(own, panels_ref[at].astype(jnp.float32), chans, cross, start + j)
        rows = slice(start * chans * chans, (start + len(some)) * chans * chans)
        full = jnp.dot(cross[rows], table, preferred_element_type=jnp.float32)
        scale = (1.0 / math.sqrt(BINS)) / jnp.maximum(full[:, COLS - 1 :], 1.0)
        keep(start, (full * scale).reshape(len(some), chans * chans, COLS))


def early_kernel(panel_count, which, pair_ref, panels_ref, table_ref, out_ref, cross):
    own = pair_ref[0].astype(jnp.float32)

    def keep(start, corr):
        out_ref[start : start + corr.shape[0]] = corr

    products(which, panel_count, own, panels_ref, table_ref[...], own.shape[0] // SEGS, cross, keep)


def early(which, count, panel_count, chans, pair, panels, table):
    whole = pl.BlockSpec(memory_space=pltpu.VMEM)
    rows = count * chans * chans
    return pl.pallas_call(
        functools.partial(early_kernel, panel_count, which),
        out_shape=jax.ShapeDtypeStruct((count, chans * chans, COLS), jnp.float32),
        in_specs=[whole] * 3,
        out_specs=whole,
        scratch_shapes=[pltpu.VMEM((rows, 2 * LANES), jnp.bfloat16)],
        compiler_params=pltpu.CompilerParams(vmem_limit_bytes=CORR_VMEM),
        cost_estimate=pl.CostEstimate(flops=4 * rows * LANES * COLS, bytes_accessed=4 * rows * COLS, transcendentals=0),
        name=which.__name__,
    )(pair, panels, table)


def last_kernel(panel_count, lists, slots_any, pair_ref, panels_ref, table_ref, stack_ref, *refs):
    done_refs = refs[: len(lists) - 1]
    out_ref, slots_ref, cross, result, sem = refs[len(lists) - 1 :]
    offsets, chans = stack_ref.shape[0], stack_ref.shape[1]
    fetch_slots = pltpu.make_async_copy(slots_any, slots_ref, sem.at[sem.shape[0] - 1])
    fetch_slots.start()
    own = pair_ref[0].astype(jnp.float32)
    copies = []

    def only(wanted, act):
        if wanted is True:
            act()
        else:
            pl.when(wanted)(act)

    def finish(found, corr):
        for j, (at, panel, wanted) in enumerate(found):
            panel = lax.rem(panel + panel_count, panel_count)
            slot = jnp.int32(0)
            for o in range(1, offsets):
                slot = jnp.where(slots_ref[0, o] == panel, o, slot)
            n = len(copies)
            result[n] = stack_ref[slot] + corr[j][:, :LAGS].reshape(chans, chans, LAGS)
            copy = pltpu.make_async_copy(result.at[n], out_ref.at[slot], sem.at[n])
            copies.append((wanted, copy))
            only(wanted, copy.start)

    found = lists[-1](panel_count)

    def keep(start, corr):
        if start == 0:
            fetch_slots.wait()
            for which, done in zip(lists, done_refs):
                finish(which(panel_count), done)
        finish(found[start : start + corr.shape[0]], corr)

    products(lists[-1], panel_count, own, panels_ref, table_ref[...], chans, cross, keep)
    for wanted, copy in copies:
        only(wanted, copy.wait)


def last(lists, counts, panel_count, slots, pair, panels, table, stack, *done):
    offsets, chans = stack.shape[0], stack.shape[1]
    whole = pl.BlockSpec(memory_space=pltpu.VMEM)
    rows = counts[-1] * chans * chans
    return pl.pallas_call(
        functools.partial(last_kernel, panel_count, lists),
        out_shape=jax.ShapeDtypeStruct(stack.shape, jnp.float32),
        in_specs=[whole] * (5 + len(done)),
        out_specs=pl.BlockSpec(memory_space=pltpu.HBM),
        scratch_shapes=[
            pltpu.SMEM(slots.shape, jnp.int32),
            pltpu.VMEM((rows, 2 * LANES), jnp.bfloat16),
            pltpu.VMEM((sum(counts), chans, chans, LAGS), jnp.float32),
            pltpu.SemaphoreType.DMA((sum(counts) + 1,)),
        ],
        compiler_params=pltpu.CompilerParams(vmem_limit_bytes=CORR_VMEM),
        cost_estimate=pl.CostEstimate(flops=4 * rows * LANES * COLS, bytes_accessed=4 * rows * COLS, transcendentals=0),
        name=lists[-1].__name__,
    )(slots, pair, panels, table, stack, *done)


def gather_near(own, slots, stack, panel_count):
    chips = panel_count // 2
    def swap(array):
        return lax.ppermute(array, "row", [(i ^ 1, i) for i in range(panel_count)])

    def fetch(array, even, odd):
        ahead = [even, odd]
        moves = []
        for i in range(panel_count):
            c = i // 2
            moves.append((2 * ((c + ahead[i % 2][c % 2]) % chips) + i % 2, i))
        return lax.ppermute(array, "row", moves)

    table = jnp.asarray(lag_table())
    twice = jnp.stack([own, own])
    pair = lax.optimization_barrier(lax.dynamic_update_slice(twice, swap(own)[None], (1, 0, 0)))
    near = fetch(pair, (1, -1), (2, 2))
    next_near = fetch(pair, (-1, 3), (3, 1))
    far = fetch(pair[0], (4, 4), (4, 4))
    chans = stack.shape[1]
    first = early(pair_panels, 2, panel_count, chans, pair, pair, table)
    near, next_near, far, first = lax.optimization_barrier((near, next_near, far, first))
    five = jnp.concatenate([near, next_near, far[None]], axis=0)
    me, chip, core, odd = place(panel_count)
    low = jnp.where((core == 0) & (odd == 1), next_near, near)
    high = jnp.where(core == 0, far[None], next_near)
    swapped = swap(jnp.concatenate([low, high], axis=0))
    second = early(near_panels, 5, panel_count, chans, pair, five, table)
    lists = (pair_panels, near_panels, swapped_panels)
    return last(lists, (2, 5, 4), panel_count, slots, pair, swapped, table, stack, first, second)


def shards(traces, valid_mask, pair_table, stack_in):
    own = whiten(traces, valid_mask)
    panel_count = lax.axis_size("row")
    if pair_table.shape[1] == 10 and panel_count >= 12 and panel_count % 4 == 0:
        return gather_near(own, pair_table, stack_in[0], panel_count)[None]
    return gather_all(own, pair_table, stack_in[0])[None]


def solution(mesh):
    in_specs = (
        P(("parts", "row"), None, None),
        P(("parts", "row"), None),
        P(("parts", "row"), None),
        P(("parts", "row"), None, None, None, None),
    )
    out_specs = P(("parts", "row"), None, None, None, None)
    return jax.shard_map(shards, mesh=mesh, in_specs=in_specs, out_specs=out_specs, check_vma=False)
```

```python
import functools
import math

import jax
import jax.numpy as jnp
import ml_dtypes
import numpy as np
from jax import lax
from jax.experimental import pallas as pl
from jax.experimental.pallas import tpu as pltpu
from jax.sharding import PartitionSpec as P

SAMPLES = 12000
FLO = 6
BINS = 595
SEGS = 2
HALF = 40
LAGS = 401
EPS = 1e-06
WHITEN_VMEM = 60 << 20
CORR_VMEM = 24 << 20

SPLIT = 20
FOLD = SAMPLES // SPLIT
LANES = 640
RUN = 32
COLS = 512


def bin_at(lane):
    residue = lane // 128 + 5 * (lane % 128 // RUN)
    return residue + SPLIT * (residue < FLO) + SPLIT * (lane % RUN)


BIN_OF = bin_at(np.arange(LANES))
USED = BIN_OF < FLO + BINS
GROUPS = ((1, 4), (2, 3), (0,))


def bf16(a):
    return np.asarray(a, np.float32).astype(ml_dtypes.bfloat16)


def fold_table():
    q = (np.arange(FOLD)[:, None] * BIN_OF[None, :]) % SAMPLES
    angle = 2.0 * np.pi * q / SAMPLES
    cos = np.where(USED, np.cos(angle), 0.0).reshape(FOLD, 5, 1, 128)
    sin = np.where(USED, -np.sin(angle), 0.0).reshape(FOLD, 5, 1, 128)
    table = np.concatenate([cos, sin], axis=2)
    order = [group for some in GROUPS for group in some]
    return bf16(table[:, order].reshape(FOLD, 5 * 256))


def lag_table():
    tau = np.arange(LAGS) - (LAGS - 1) // 2
    q = (BIN_OF[:, None] * tau[None, :]) % SAMPLES
    angle = 2.0 * np.pi * q / SAMPLES
    table = np.zeros((2 * LANES, COLS), np.float64)
    table[:LANES, :LAGS] = np.where(USED[:, None], np.cos(angle), 0.0)
    table[LANES:, :LAGS] = np.where(USED[:, None], -np.sin(angle), 0.0)
    table[LANES - 1, COLS - 1] = 1.0
    return bf16(table)


def cosine(n, of):
    return math.cos(2.0 * math.pi * n / of)


def sine(n, of):
    return math.sin(2.0 * math.pi * n / of)


def ten_point(s):
    e = [s[n] + s[n + 5] for n in range(5)]
    d = [s[n] - s[n + 5] for n in range(5)]
    c1, c2, s1, s2 = cosine(1, 10), cosine(2, 10), sine(1, 10), sine(2, 10)
    e14, e23, f14, f23 = e[1] + e[4], e[2] + e[3], e[1] - e[4], e[2] - e[3]
    d14, d23, g14, g23 = d[1] + d[4], d[2] + d[3], d[1] - d[4], d[2] - d[3]
    y0 = (e[0] + e14 + e23, None)
    y2 = (e[0] + c2 * e14 - c1 * e23, s2 * f14 + s1 * f23)
    y4 = (e[0] - c1 * e14 + c2 * e23, s1 * f14 - s2 * f23)
    y1 = (d[0] + c1 * g14 + c2 * g23, s1 * d14 + s2 * d23)
    y3 = (d[0] - c2 * g14 - c1 * g23, s2 * d14 - s1 * d23)
    y5 = (d[0] - g14 + g23, None)
    return [y0, y1, y2, y3, y4, y5]


def twenty_point(s):
    y = [None] * 11
    y[0::2] = ten_point([s[n] + s[n + 10] for n in range(10)])
    d = [s[n] - s[n + 10] for n in range(10)]
    g1, g2, g3, g4 = (d[n] - d[10 - n] for n in range(1, 5))
    h1, h2, h3, h4 = (d[n] + d[10 - n] for n in range(1, 5))
    for k, turn in ((1, d[5]), (3, -d[5])):
        even = d[0] + cosine(2 * k, 20) * g2 + cosine(4 * k, 20) * g4
        odd = cosine(k, 20) * g1 + cosine(3 * k, 20) * g3
        even_sin = sine(2 * k, 20) * h2 + sine(4 * k, 20) * h4
        odd_sin = sine(k, 20) * h1 + sine(3 * k, 20) * h3 + turn
        y[k] = (even + odd, odd_sin + even_sin)
        y[10 - k] = (even - odd, odd_sin - even_sin)
    y[5] = (d[0] - g2 + g4, h1 - h3 + d[5])
    return y


def hi_lo(y):
    hi = y.astype(jnp.bfloat16)
    return [hi, (y - hi.astype(jnp.float32)).astype(jnp.bfloat16)]


def whiten_kernel(x_hbm, mask_hbm, table_hbm, out_ref, x_buf, mask_buf, table, near, sem):
    chans, minutes, samples = x_buf.shape
    rows = chans * minutes
    starts = (0, 512, 1024, 1280)
    fetch_x = pltpu.make_async_copy(x_hbm, x_buf, sem.at[0])
    fetch_mask = pltpu.make_async_copy(mask_hbm, mask_buf, sem.at[1])
    fetch_table = [
        pltpu.make_async_copy(table_hbm.at[:, pl.ds(a, b - a)], table.at[:, pl.ds(a, b - a)], sem.at[2 + i])
        for i, (a, b) in enumerate(zip(starts, starts[1:]))
    ]
    for copy in [fetch_x, fetch_mask] + fetch_table:
        copy.start()

    down = bin_at(lax.broadcasted_iota(jnp.int32, (LANES, 128), 0))
    down = jnp.where(down < FLO + BINS, down, -SAMPLES)
    lanes = bin_at(lax.broadcasted_iota(jnp.int32, (8, LANES), 1))
    for group in range(5):
        across = jnp.broadcast_to(lanes[:1, group * 128 : (group + 1) * 128], (LANES, 128))
        close = (jnp.abs(down - across) <= HALF) & (across < FLO + BINS)
        near[:, group * 128 : (group + 1) * 128] = jnp.where(close, 1.0, 0.0).astype(jnp.bfloat16)
    bins = lanes[:1]
    count = jnp.minimum(bins + HALF, FLO + BINS - 1) - jnp.maximum(bins - HALF, FLO) + 1
    inverse = 1.0 / jnp.maximum(count, 1).astype(jnp.float32)

    fetch_x.wait()
    x = jnp.swapaxes(x_buf[...], 0, 1).reshape(rows, samples)
    y = twenty_point([x[:, FOLD * n : FOLD * (n + 1)].astype(jnp.float32) for n in range(SPLIT)])
    run = lax.broadcasted_iota(jnp.int32, (rows, 128), 1) // RUN
    for copy in [fetch_mask] + fetch_table:
        copy.wait()
    real = [None] * 5
    imag = [None] * 5
    for part, groups in enumerate(GROUPS):
        wanted = sorted({min(k, SPLIT - k) for g in groups for k in range(g, SPLIT, 5)})
        pieces = [(k, i) for k in wanted for i in range(2) if y[k][i] is not None]
        halves = [hi_lo(y[k][i]) for k, i in pieces]
        left = jnp.concatenate([half[j] for j in range(2) for half in halves], axis=0)
        at = starts[part]
        full = jnp.dot(left, table[:, at : starts[part + 1]], preferred_element_type=jnp.float32)
        got = {
            p: full[rows * i : rows * (i + 1)] + full[rows * (len(pieces) + i) : rows * (len(pieces) + i + 1)]
            for i, p in enumerate(pieces)
        }
        for place, group in enumerate(groups):
            cos = slice(place * 256, place * 256 + 128)
            sin = slice(place * 256 + 128, place * 256 + 256)
            re = im = None
            for q in range(4):
                k = group + 5 * q
                same = min(k, SPLIT - k)
                a = got[(same, 0)]
                r, i = a[:, cos], a[:, sin]
                if (same, 1) in got:
                    b = got[(same, 1)]
                    if k == same:
                        r, i = r + b[:, sin], i - b[:, cos]
                    else:
                        r, i = r - b[:, sin], i + b[:, cos]
                re = r if re is None else jnp.where(run == q, r, re)
                im = i if im is None else jnp.where(run == q, i, im)
            real[group], imag[group] = re, im
    re = jnp.concatenate(real, axis=1)
    im = jnp.concatenate(imag, axis=1)
    power = re * re + im * im
    hi, mid = hi_lo(power)
    low = (power - hi.astype(jnp.float32) - mid.astype(jnp.float32)).astype(jnp.bfloat16)
    sums = jnp.dot(jnp.concatenate([hi, mid, low], axis=0), near[...], preferred_element_type=jnp.float32)
    smooth = (sums[:rows] + sums[rows : 2 * rows] + sums[2 * rows :]) * inverse
    mask = mask_buf[...].astype(jnp.float32)
    spread = jnp.concatenate([jnp.broadcast_to(mask[m : m + 1], (chans, chans)) for m in range(minutes)], axis=0)
    own = lax.broadcasted_iota(jnp.int32, (rows, chans), 0) % chans
    other = lax.broadcasted_iota(jnp.int32, (rows, chans), 1)
    flags = jnp.sum(jnp.where(own == other, spread, 0.0), axis=1, keepdims=True)
    factor = flags * lax.rsqrt(smooth + EPS)
    last = lax.broadcasted_iota(jnp.int32, (rows, LANES), 1) == LANES - 1
    out_ref[:, :LANES] = (re * factor).astype(jnp.bfloat16)
    out_ref[:, LANES:] = jnp.where(last, flags, im * factor).astype(jnp.bfloat16)


def whiten(traces, valid_mask):
    chans, minutes, samples = traces.shape
    rows = chans * minutes
    anywhere = pl.BlockSpec(memory_space=pltpu.HBM)
    return pl.pallas_call(
        whiten_kernel,
        out_shape=pltpu.VMEM((rows, 2 * LANES), jnp.bfloat16),
        in_specs=[anywhere] * 3,
        out_specs=pl.BlockSpec(memory_space=pltpu.VMEM),
        scratch_shapes=[
            pltpu.VMEM((chans, minutes, samples), jnp.bfloat16),
            pltpu.VMEM((minutes, chans), jnp.int32),
            pltpu.VMEM((FOLD, 5 * 256), jnp.bfloat16),
            pltpu.VMEM((LANES, LANES), jnp.bfloat16),
            pltpu.SemaphoreType.DMA((5,)),
        ],
        compiler_params=pltpu.CompilerParams(vmem_limit_bytes=WHITEN_VMEM),
        name="whiten",
    )(traces, valid_mask.T, jnp.asarray(fold_table()))


def cross_tile(own, part, chans, cross, j):
    minutes = own.shape[0] // chans
    for a in range(0, chans, 2):
        both_re, both_im = [], []
        for channel in (a, a + 1):
            re = im = None
            for m in range(minutes):
                row = m * chans + channel
                o_re, o_im = own[row : row + 1, :LANES], own[row : row + 1, LANES:]
                p_re = part[m * chans : (m + 1) * chans, :LANES]
                p_im = part[m * chans : (m + 1) * chans, LANES:]
                r = o_re * p_re + o_im * p_im
                i = o_im * p_re - o_re * p_im
                re = r if re is None else re + r
                im = i if im is None else im + i
            both_re.append(re)
            both_im.append(im)
        rows = slice((j * chans + a) * chans, (j * chans + a + 2) * chans)
        cross[rows, :LANES] = jnp.concatenate(both_re, axis=0).astype(jnp.bfloat16)
        cross[rows, LANES:] = jnp.concatenate(both_im, axis=0).astype(jnp.bfloat16)


def lag_product(cross, table, shape):
    full = jnp.dot(cross, table, preferred_element_type=jnp.float32)
    scale = (1.0 / math.sqrt(BINS)) / jnp.maximum(full[:, COLS - 1 :], 1.0)
    return (full * scale)[:, :LAGS].reshape(shape)


def corr_kernel(pick, slots_ref, panels_ref, lag_ref, stack_ref, out_ref, cross):
    step = pl.program_id(0)
    count, chans = out_ref.shape[0], out_ref.shape[1]
    own = panels_ref[pick(lax.axis_index("row"))].astype(jnp.float32)
    for j in range(count):
        part = panels_ref[pick(slots_ref[0, step * count + j])].astype(jnp.float32)
        cross_tile(own, part, chans, cross, j)
    corr = lag_product(cross[...], lag_ref[...], out_ref.shape)
    out_ref[...] = stack_ref[pl.ds(step * count, count)] + corr


def correlate(pick, slots, panels, stack):
    offsets, chans = stack.shape[0], stack.shape[1]
    chunk = max(d for d in range(1, 7) if offsets % d == 0)
    whole = pl.BlockSpec(memory_space=pltpu.VMEM)
    return pl.pallas_call(
        functools.partial(corr_kernel, pick),
        out_shape=jax.ShapeDtypeStruct(stack.shape, jnp.float32),
        grid_spec=pltpu.PrefetchScalarGridSpec(
            num_scalar_prefetch=1,
            grid=(offsets // chunk,),
            in_specs=[whole, whole, whole],
            out_specs=pl.BlockSpec((chunk, chans, chans, LAGS), lambda i, s: (i, 0, 0, 0)),
            scratch_shapes=[pltpu.VMEM((chunk * chans * chans, panels.shape[2]), jnp.bfloat16)],
        ),
        compiler_params=pltpu.CompilerParams(vmem_limit_bytes=CORR_VMEM),
        name="correlate",
    )(slots, panels, jnp.asarray(lag_table()), stack)


def gather_all(own, slots, stack):
    panels = lax.all_gather(own, "row", axis=0)
    return correlate(lambda j: j, slots, panels, stack)


def place(panel_count):
    me = lax.axis_index("row")
    return me, me // 2, lax.rem(me, 2), lax.rem(me // 2, 2)


def first_hop(panel_count):
    me, chip, core, odd = place(panel_count)
    a = jnp.where(core == 0, chip + 1 - 2 * odd, chip + 2)
    b = jnp.where(core == 0, chip - 1 + 4 * odd, chip + 3 - 2 * odd)
    return a, b


def pair_panels(panel_count):
    me, chip, core, odd = place(panel_count)
    return [(0, me, True), (1, me + 1 - 2 * core, True)]


def near_panels(panel_count):
    me, chip, core, odd = place(panel_count)
    a, b = first_hop(panel_count)
    pairs = [(2 * i + t, 2 * c + (core if t == 0 else 1 - core), True) for i, c in enumerate((a, b)) for t in range(2)]
    for i, here in ((0, odd == 1), (2, odd == 0)):
        pairs[i] = (i, pairs[i][1], (core == 1) | jnp.logical_not(here))
    return pairs + [(4, me + 8, True)]


def swapped_panels(panel_count):
    me, chip, core, odd = place(panel_count)
    found = []
    for t in range(2):
        ahead = jnp.where(core == 0, chip + 2, chip + 1 + 2 * odd)
        found.append((t, 2 * ahead + (1 - core if t == 0 else core), True))
    for t in range(2):
        ahead = 2 * (chip + 3 - 2 * odd) + 1 - t
        wanted = True if t == 0 else core == 0
        found.append((2 + t, jnp.where(core == 0, ahead, 2 * chip + 8), wanted))
    return found


def products(which, panel_count, own, panels_ref, table, chans, cross, keep):
    found = which(panel_count)
    for start in range(0, len(found), 2):
        some = found[start : start + 2]
        for j, (at, panel, wanted) in enumerate(some):
            cross_tile(own, panels_ref[at].astype(jnp.float32), chans, cross, start + j)
        rows = slice(start * chans * chans, (start + len(some)) * chans * chans)
        full = jnp.dot(cross[rows], table, preferred_element_type=jnp.float32)
        scale = (1.0 / math.sqrt(BINS)) / jnp.maximum(full[:, COLS - 1 :], 1.0)
        keep(start, (full * scale).reshape(len(some), chans * chans, COLS))


def early_kernel(panel_count, which, pair_ref, panels_ref, table_ref, *refs):
    out_ref, cross = refs[-2:]
    own = pair_ref[0].astype(jnp.float32)

    def keep(start, corr):
        out_ref[start : start + corr.shape[0]] = corr

    products(which, panel_count, own, panels_ref, table_ref[...], own.shape[0] // SEGS, cross, keep)


def early(which, count, panel_count, chans, pair, panels, table, *held):
    whole = pl.BlockSpec(memory_space=pltpu.VMEM)
    rows = count * chans * chans
    return pl.pallas_call(
        functools.partial(early_kernel, panel_count, which),
        out_shape=jax.ShapeDtypeStruct((count, chans * chans, COLS), jnp.float32),
        in_specs=[whole] * (3 + len(held)),
        out_specs=whole,
        scratch_shapes=[pltpu.VMEM((rows, 2 * LANES), jnp.bfloat16)],
        compiler_params=pltpu.CompilerParams(vmem_limit_bytes=CORR_VMEM),
        cost_estimate=pl.CostEstimate(flops=4 * rows * LANES * COLS, bytes_accessed=4 * rows * COLS, transcendentals=0),
        name=which.__name__,
    )(pair, panels, table, *held)


def last_kernel(panel_count, lists, slots_any, pair_ref, panels_ref, table_ref, stack_ref, *refs):
    done_refs = refs[: len(lists) - 1]
    out_ref, slots_ref, cross, result, sem = refs[len(lists) - 1 :]
    offsets, chans = stack_ref.shape[0], stack_ref.shape[1]
    fetch_slots = pltpu.make_async_copy(slots_any, slots_ref, sem.at[sem.shape[0] - 1])
    fetch_slots.start()
    own = pair_ref[0].astype(jnp.float32)
    copies = []

    def only(wanted, act):
        if wanted is True:
            act()
        else:
            pl.when(wanted)(act)

    def finish(found, corr):
        for j, (at, panel, wanted) in enumerate(found):
            panel = lax.rem(panel + panel_count, panel_count)
            slot = jnp.int32(0)
            for o in range(1, offsets):
                slot = jnp.where(slots_ref[0, o] == panel, o, slot)
            n = len(copies)
            result[n] = stack_ref[slot] + corr[j][:, :LAGS].reshape(chans, chans, LAGS)
            copy = pltpu.make_async_copy(result.at[n], out_ref.at[slot], sem.at[n])
            copies.append((wanted, copy))
            only(wanted, copy.start)

    found = lists[-1](panel_count)

    def keep(start, corr):
        if start == 0:
            fetch_slots.wait()
            for which, done in zip(lists, done_refs):
                finish(which(panel_count), done)
        finish(found[start : start + corr.shape[0]], corr)

    products(lists[-1], panel_count, own, panels_ref, table_ref[...], chans, cross, keep)
    for wanted, copy in copies:
        only(wanted, copy.wait)


def last(lists, counts, panel_count, slots, pair, panels, table, stack, *done):
    offsets, chans = stack.shape[0], stack.shape[1]
    whole = pl.BlockSpec(memory_space=pltpu.VMEM)
    rows = counts[-1] * chans * chans
    return pl.pallas_call(
        functools.partial(last_kernel, panel_count, lists),
        out_shape=jax.ShapeDtypeStruct(stack.shape, jnp.float32),
        in_specs=[whole] * (5 + len(done)),
        out_specs=pl.BlockSpec(memory_space=pltpu.HBM),
        scratch_shapes=[
            pltpu.SMEM(slots.shape, jnp.int32),
            pltpu.VMEM((rows, 2 * LANES), jnp.bfloat16),
            pltpu.VMEM((sum(counts), chans, chans, LAGS), jnp.float32),
            pltpu.SemaphoreType.DMA((sum(counts) + 1,)),
        ],
        compiler_params=pltpu.CompilerParams(vmem_limit_bytes=CORR_VMEM),
        cost_estimate=pl.CostEstimate(flops=4 * rows * LANES * COLS, bytes_accessed=4 * rows * COLS, transcendentals=0),
        name=lists[-1].__name__,
    )(slots, pair, panels, table, stack, *done)


def gather_near(own, slots, stack, panel_count):
    chips = panel_count // 2
    def swap(array):
        return lax.ppermute(array, "row", [(i ^ 1, i) for i in range(panel_count)])

    def fetch(array, even, odd):
        ahead = [even, odd]
        moves = []
        for i in range(panel_count):
            c = i // 2
            moves.append((2 * ((c + ahead[i % 2][c % 2]) % chips) + i % 2, i))
        return lax.ppermute(array, "row", moves)

    table = jnp.asarray(lag_table())
    twice = jnp.stack([own, own])
    pair = lax.optimization_barrier(lax.dynamic_update_slice(twice, swap(own)[None], (1, 0, 0)))
    near = fetch(pair, (1, -1), (2, 2))
    next_near = fetch(pair, (-1, 3), (3, 1))
    far = fetch(pair[0], (4, 4), (4, 4))
    chans = stack.shape[1]
    first = early(pair_panels, 2, panel_count, chans, pair, pair, table)
    near, next_near, far, first = lax.optimization_barrier((near, next_near, far, first))
    five = jnp.concatenate([near, next_near, far[None]], axis=0)
    me, chip, core, odd = place(panel_count)
    low = jnp.where((core == 0) & (odd == 1), next_near, near)
    high = jnp.where(core == 0, far[None], next_near)
    swapped = swap(jnp.concatenate([low, high], axis=0))
    second = early(near_panels, 5, panel_count, chans, pair, five, table, stack)
    lists = (pair_panels, near_panels, swapped_panels)
    return last(lists, (2, 5, 4), panel_count, slots, pair, swapped, table, stack, first, second)


def shards(traces, valid_mask, pair_table, stack_in):
    own = whiten(traces, valid_mask)
    panel_count = lax.axis_size("row")
    if pair_table.shape[1] == 10 and panel_count >= 12 and panel_count % 4 == 0:
        return gather_near(own, pair_table, stack_in[0], panel_count)[None]
    return gather_all(own, pair_table, stack_in[0])[None]


def solution(mesh):
    in_specs = (
        P(("parts", "row"), None, None),
        P(("parts", "row"), None),
        P(("parts", "row"), None),
        P(("parts", "row"), None, None, None, None),
    )
    out_specs = P(("parts", "row"), None, None, None, None)
    return jax.shard_map(shards, mesh=mesh, in_specs=in_specs, out_specs=out_specs, check_vma=False)
```

```python
import functools
import math

import jax
import jax.numpy as jnp
import ml_dtypes
import numpy as np
from jax import lax
from jax.experimental import pallas as pl
from jax.experimental.pallas import tpu as pltpu
from jax.sharding import PartitionSpec as P

SAMPLES = 12000
FLO = 6
BINS = 595
SEGS = 2
HALF = 40
LAGS = 401
EPS = 1e-06
WHITEN_VMEM = 60 << 20
CORR_VMEM = 24 << 20
TOGETHER = 5

SPLIT = 20
FOLD = SAMPLES // SPLIT
LANES = 640
RUN = 32
COLS = 512


def bin_at(lane):
    residue = lane // 128 + 5 * (lane % 128 // RUN)
    return residue + SPLIT * (residue < FLO) + SPLIT * (lane % RUN)


BIN_OF = bin_at(np.arange(LANES))
USED = BIN_OF < FLO + BINS
GROUPS = ((1, 4), (2, 3), (0,))


def bf16(a):
    return np.asarray(a, np.float32).astype(ml_dtypes.bfloat16)


def fold_table():
    q = (np.arange(FOLD)[:, None] * BIN_OF[None, :]) % SAMPLES
    angle = 2.0 * np.pi * q / SAMPLES
    cos = np.where(USED, np.cos(angle), 0.0).reshape(FOLD, 5, 1, 128)
    sin = np.where(USED, -np.sin(angle), 0.0).reshape(FOLD, 5, 1, 128)
    table = np.concatenate([cos, sin], axis=2)
    order = [group for some in GROUPS for group in some]
    return bf16(table[:, order].reshape(FOLD, 5 * 256))


def lag_table():
    tau = np.arange(LAGS) - (LAGS - 1) // 2
    q = (BIN_OF[:, None] * tau[None, :]) % SAMPLES
    angle = 2.0 * np.pi * q / SAMPLES
    table = np.zeros((2 * LANES, COLS), np.float64)
    table[:LANES, :LAGS] = np.where(USED[:, None], np.cos(angle), 0.0)
    table[LANES:, :LAGS] = np.where(USED[:, None], -np.sin(angle), 0.0)
    table[LANES - 1, COLS - 1] = 1.0
    return bf16(table)


def cosine(n, of):
    return math.cos(2.0 * math.pi * n / of)


def sine(n, of):
    return math.sin(2.0 * math.pi * n / of)


def ten_point(s):
    e = [s[n] + s[n + 5] for n in range(5)]
    d = [s[n] - s[n + 5] for n in range(5)]
    c1, c2, s1, s2 = cosine(1, 10), cosine(2, 10), sine(1, 10), sine(2, 10)
    e14, e23, f14, f23 = e[1] + e[4], e[2] + e[3], e[1] - e[4], e[2] - e[3]
    d14, d23, g14, g23 = d[1] + d[4], d[2] + d[3], d[1] - d[4], d[2] - d[3]
    y0 = (e[0] + e14 + e23, None)
    y2 = (e[0] + c2 * e14 - c1 * e23, s2 * f14 + s1 * f23)
    y4 = (e[0] - c1 * e14 + c2 * e23, s1 * f14 - s2 * f23)
    y1 = (d[0] + c1 * g14 + c2 * g23, s1 * d14 + s2 * d23)
    y3 = (d[0] - c2 * g14 - c1 * g23, s2 * d14 - s1 * d23)
    y5 = (d[0] - g14 + g23, None)
    return [y0, y1, y2, y3, y4, y5]


def twenty_point(s):
    y = [None] * 11
    y[0::2] = ten_point([s[n] + s[n + 10] for n in range(10)])
    d = [s[n] - s[n + 10] for n in range(10)]
    g1, g2, g3, g4 = (d[n] - d[10 - n] for n in range(1, 5))
    h1, h2, h3, h4 = (d[n] + d[10 - n] for n in range(1, 5))
    for k, turn in ((1, d[5]), (3, -d[5])):
        even = d[0] + cosine(2 * k, 20) * g2 + cosine(4 * k, 20) * g4
        odd = cosine(k, 20) * g1 + cosine(3 * k, 20) * g3
        even_sin = sine(2 * k, 20) * h2 + sine(4 * k, 20) * h4
        odd_sin = sine(k, 20) * h1 + sine(3 * k, 20) * h3 + turn
        y[k] = (even + odd, odd_sin + even_sin)
        y[10 - k] = (even - odd, odd_sin - even_sin)
    y[5] = (d[0] - g2 + g4, h1 - h3 + d[5])
    return y


def hi_lo(y):
    hi = y.astype(jnp.bfloat16)
    return [hi, (y - hi.astype(jnp.float32)).astype(jnp.bfloat16)]


def whiten_kernel(x_hbm, mask_hbm, table_hbm, out_ref, x_buf, mask_buf, table, near, sem):
    chans, minutes, samples = x_buf.shape
    rows = chans * minutes
    starts = (0, 512, 1024, 1280)
    fetch_x = pltpu.make_async_copy(x_hbm, x_buf, sem.at[0])
    fetch_mask = pltpu.make_async_copy(mask_hbm, mask_buf, sem.at[1])
    fetch_table = [
        pltpu.make_async_copy(table_hbm.at[:, pl.ds(a, b - a)], table.at[:, pl.ds(a, b - a)], sem.at[2 + i])
        for i, (a, b) in enumerate(zip(starts, starts[1:]))
    ]
    for copy in [fetch_x, fetch_mask] + fetch_table:
        copy.start()

    down = bin_at(lax.broadcasted_iota(jnp.int32, (LANES, 128), 0))
    down = jnp.where(down < FLO + BINS, down, -SAMPLES)
    lanes = bin_at(lax.broadcasted_iota(jnp.int32, (8, LANES), 1))
    for group in range(5):
        across = jnp.broadcast_to(lanes[:1, group * 128 : (group + 1) * 128], (LANES, 128))
        close = (jnp.abs(down - across) <= HALF) & (across < FLO + BINS)
        near[:, group * 128 : (group + 1) * 128] = jnp.where(close, 1.0, 0.0).astype(jnp.bfloat16)
    bins = lanes[:1]
    count = jnp.minimum(bins + HALF, FLO + BINS - 1) - jnp.maximum(bins - HALF, FLO) + 1
    inverse = 1.0 / jnp.maximum(count, 1).astype(jnp.float32)

    fetch_x.wait()
    x = jnp.swapaxes(x_buf[...], 0, 1).reshape(rows, samples)
    y = twenty_point([x[:, FOLD * n : FOLD * (n + 1)].astype(jnp.float32) for n in range(SPLIT)])
    run = lax.broadcasted_iota(jnp.int32, (rows, 128), 1) // RUN
    for copy in [fetch_mask] + fetch_table:
        copy.wait()
    real = [None] * 5
    imag = [None] * 5
    for part, groups in enumerate(GROUPS):
        wanted = sorted({min(k, SPLIT - k) for g in groups for k in range(g, SPLIT, 5)})
        pieces = [(k, i) for k in wanted for i in range(2) if y[k][i] is not None]
        halves = [hi_lo(y[k][i]) for k, i in pieces]
        left = jnp.concatenate([half[j] for j in range(2) for half in halves], axis=0)
        at = starts[part]
        full = jnp.dot(left, table[:, at : starts[part + 1]], preferred_element_type=jnp.float32)
        got = {
            p: full[rows * i : rows * (i + 1)] + full[rows * (len(pieces) + i) : rows * (len(pieces) + i + 1)]
            for i, p in enumerate(pieces)
        }
        for place, group in enumerate(groups):
            cos = slice(place * 256, place * 256 + 128)
            sin = slice(place * 256 + 128, place * 256 + 256)
            re = im = None
            for q in range(4):
                k = group + 5 * q
                same = min(k, SPLIT - k)
                a = got[(same, 0)]
                r, i = a[:, cos], a[:, sin]
                if (same, 1) in got:
                    b = got[(same, 1)]
                    if k == same:
                        r, i = r + b[:, sin], i - b[:, cos]
                    else:
                        r, i = r - b[:, sin], i + b[:, cos]
                re = r if re is None else jnp.where(run == q, r, re)
                im = i if im is None else jnp.where(run == q, i, im)
            real[group], imag[group] = re, im
    re = jnp.concatenate(real, axis=1)
    im = jnp.concatenate(imag, axis=1)
    power = re * re + im * im
    hi, mid = hi_lo(power)
    low = (power - hi.astype(jnp.float32) - mid.astype(jnp.float32)).astype(jnp.bfloat16)
    sums = jnp.dot(jnp.concatenate([hi, mid, low], axis=0), near[...], preferred_element_type=jnp.float32)
    smooth = (sums[:rows] + sums[rows : 2 * rows] + sums[2 * rows :]) * inverse
    mask = mask_buf[...].astype(jnp.float32)
    spread = jnp.concatenate([jnp.broadcast_to(mask[m : m + 1], (chans, chans)) for m in range(minutes)], axis=0)
    own = lax.broadcasted_iota(jnp.int32, (rows, chans), 0) % chans
    other = lax.broadcasted_iota(jnp.int32, (rows, chans), 1)
    flags = jnp.sum(jnp.where(own == other, spread, 0.0), axis=1, keepdims=True)
    factor = flags * lax.rsqrt(smooth + EPS)
    last = lax.broadcasted_iota(jnp.int32, (rows, LANES), 1) == LANES - 1
    out_ref[:, :LANES] = (re * factor).astype(jnp.bfloat16)
    out_ref[:, LANES:] = jnp.where(last, flags, im * factor).astype(jnp.bfloat16)


def whiten(traces, valid_mask):
    chans, minutes, samples = traces.shape
    rows = chans * minutes
    anywhere = pl.BlockSpec(memory_space=pltpu.HBM)
    return pl.pallas_call(
        whiten_kernel,
        out_shape=pltpu.VMEM((rows, 2 * LANES), jnp.bfloat16),
        in_specs=[anywhere] * 3,
        out_specs=pl.BlockSpec(memory_space=pltpu.VMEM),
        scratch_shapes=[
            pltpu.VMEM((chans, minutes, samples), jnp.bfloat16),
            pltpu.VMEM((minutes, chans), jnp.int32),
            pltpu.VMEM((FOLD, 5 * 256), jnp.bfloat16),
            pltpu.VMEM((LANES, LANES), jnp.bfloat16),
            pltpu.SemaphoreType.DMA((5,)),
        ],
        compiler_params=pltpu.CompilerParams(vmem_limit_bytes=WHITEN_VMEM),
        name="whiten",
    )(traces, valid_mask.T, jnp.asarray(fold_table()))


def cross_tile(own, part, chans, cross, j):
    minutes = own.shape[0] // chans
    for a in range(0, chans, 2):
        both_re, both_im = [], []
        for channel in (a, a + 1):
            re = im = None
            for m in range(minutes):
                row = m * chans + channel
                o_re, o_im = own[row : row + 1, :LANES], own[row : row + 1, LANES:]
                p_re = part[m * chans : (m + 1) * chans, :LANES]
                p_im = part[m * chans : (m + 1) * chans, LANES:]
                r = o_re * p_re + o_im * p_im
                i = o_im * p_re - o_re * p_im
                re = r if re is None else re + r
                im = i if im is None else im + i
            both_re.append(re)
            both_im.append(im)
        rows = slice((j * chans + a) * chans, (j * chans + a + 2) * chans)
        cross[rows, :LANES] = jnp.concatenate(both_re, axis=0).astype(jnp.bfloat16)
        cross[rows, LANES:] = jnp.concatenate(both_im, axis=0).astype(jnp.bfloat16)


def lag_product(cross, table, shape):
    full = jnp.dot(cross, table, preferred_element_type=jnp.float32)
    scale = (1.0 / math.sqrt(BINS)) / jnp.maximum(full[:, COLS - 1 :], 1.0)
    return (full * scale)[:, :LAGS].reshape(shape)


def corr_kernel(pick, slots_ref, panels_ref, lag_ref, stack_ref, out_ref, cross):
    step = pl.program_id(0)
    count, chans = out_ref.shape[0], out_ref.shape[1]
    own = panels_ref[pick(lax.axis_index("row"))].astype(jnp.float32)
    for j in range(count):
        part = panels_ref[pick(slots_ref[0, step * count + j])].astype(jnp.float32)
        cross_tile(own, part, chans, cross, j)
    corr = lag_product(cross[...], lag_ref[...], out_ref.shape)
    out_ref[...] = stack_ref[pl.ds(step * count, count)] + corr


def correlate(pick, slots, panels, stack):
    offsets, chans = stack.shape[0], stack.shape[1]
    chunk = max(d for d in range(1, 7) if offsets % d == 0)
    whole = pl.BlockSpec(memory_space=pltpu.VMEM)
    return pl.pallas_call(
        functools.partial(corr_kernel, pick),
        out_shape=jax.ShapeDtypeStruct(stack.shape, jnp.float32),
        grid_spec=pltpu.PrefetchScalarGridSpec(
            num_scalar_prefetch=1,
            grid=(offsets // chunk,),
            in_specs=[whole, whole, whole],
            out_specs=pl.BlockSpec((chunk, chans, chans, LAGS), lambda i, s: (i, 0, 0, 0)),
            scratch_shapes=[pltpu.VMEM((chunk * chans * chans, panels.shape[2]), jnp.bfloat16)],
        ),
        compiler_params=pltpu.CompilerParams(vmem_limit_bytes=CORR_VMEM),
        name="correlate",
    )(slots, panels, jnp.asarray(lag_table()), stack)


def gather_all(own, slots, stack):
    panels = lax.all_gather(own, "row", axis=0)
    return correlate(lambda j: j, slots, panels, stack)


def place(panel_count):
    me = lax.axis_index("row")
    return me, me // 2, lax.rem(me, 2), lax.rem(me // 2, 2)


def first_hop(panel_count):
    me, chip, core, odd = place(panel_count)
    a = jnp.where(core == 0, chip + 1 - 2 * odd, chip + 2)
    b = jnp.where(core == 0, chip - 1 + 4 * odd, chip + 3 - 2 * odd)
    return a, b


def pair_panels(panel_count):
    me, chip, core, odd = place(panel_count)
    return [(0, me, True), (1, me + 1 - 2 * core, True)]


def near_panels(panel_count):
    me, chip, core, odd = place(panel_count)
    a, b = first_hop(panel_count)
    pairs = [(2 * i + t, 2 * c + (core if t == 0 else 1 - core), True) for i, c in enumerate((a, b)) for t in range(2)]
    for i, here in ((0, odd == 1), (2, odd == 0)):
        pairs[i] = (i, pairs[i][1], (core == 1) | jnp.logical_not(here))
    return pairs + [(4, me + 8, True)]


def swapped_panels(panel_count):
    me, chip, core, odd = place(panel_count)
    found = []
    for t in range(2):
        ahead = jnp.where(core == 0, chip + 2, chip + 1 + 2 * odd)
        found.append((t, 2 * ahead + (1 - core if t == 0 else core), True))
    for t in range(2):
        ahead = 2 * (chip + 3 - 2 * odd) + 1 - t
        wanted = True if t == 0 else core == 0
        found.append((2 + t, jnp.where(core == 0, ahead, 2 * chip + 8), wanted))
    return found


def products(which, panel_count, own, panels_ref, table, chans, cross, keep):
    found = which(panel_count)
    for start in range(0, len(found), TOGETHER):
        some = found[start : start + TOGETHER]
        for j, (at, panel, wanted) in enumerate(some):
            cross_tile(own, panels_ref[at].astype(jnp.float32), chans, cross, start + j)
        rows = slice(start * chans * chans, (start + len(some)) * chans * chans)
        full = jnp.dot(cross[rows], table, preferred_element_type=jnp.float32)
        scale = (1.0 / math.sqrt(BINS)) / jnp.maximum(full[:, COLS - 1 :], 1.0)
        keep(start, (full * scale).reshape(len(some), chans * chans, COLS))


def early_kernel(panel_count, which, pair_ref, panels_ref, table_ref, *refs):
    out_ref, cross = refs[-2:]
    own = pair_ref[0].astype(jnp.float32)

    def keep(start, corr):
        out_ref[start : start + corr.shape[0]] = corr

    products(which, panel_count, own, panels_ref, table_ref[...], own.shape[0] // SEGS, cross, keep)


def early(which, count, panel_count, chans, pair, panels, table, *held):
    whole = pl.BlockSpec(memory_space=pltpu.VMEM)
    rows = count * chans * chans
    return pl.pallas_call(
        functools.partial(early_kernel, panel_count, which),
        out_shape=jax.ShapeDtypeStruct((count, chans * chans, COLS), jnp.float32),
        in_specs=[whole] * (3 + len(held)),
        out_specs=whole,
        scratch_shapes=[pltpu.VMEM((rows, 2 * LANES), jnp.bfloat16)],
        compiler_params=pltpu.CompilerParams(vmem_limit_bytes=CORR_VMEM),
        cost_estimate=pl.CostEstimate(flops=4 * rows * LANES * COLS, bytes_accessed=4 * rows * COLS, transcendentals=0),
        name=which.__name__,
    )(pair, panels, table, *held)


def last_kernel(panel_count, lists, slots_any, pair_ref, panels_ref, table_ref, stack_ref, *refs):
    done_refs = refs[: len(lists) - 1]
    out_ref, slots_ref, cross, result, sem = refs[len(lists) - 1 :]
    offsets, chans = stack_ref.shape[0], stack_ref.shape[1]
    fetch_slots = pltpu.make_async_copy(slots_any, slots_ref, sem.at[sem.shape[0] - 1])
    fetch_slots.start()
    own = pair_ref[0].astype(jnp.float32)
    copies = []

    def only(wanted, act):
        if wanted is True:
            act()
        else:
            pl.when(wanted)(act)

    def finish(found, corr):
        for j, (at, panel, wanted) in enumerate(found):
            panel = lax.rem(panel + panel_count, panel_count)
            slot = jnp.int32(0)
            for o in range(1, offsets):
                slot = jnp.where(slots_ref[0, o] == panel, o, slot)
            n = len(copies)
            result[n] = stack_ref[slot] + corr[j][:, :LAGS].reshape(chans, chans, LAGS)
            copy = pltpu.make_async_copy(result.at[n], out_ref.at[slot], sem.at[n])
            copies.append((wanted, copy))
            only(wanted, copy.start)

    found = lists[-1](panel_count)

    def keep(start, corr):
        if start == 0:
            fetch_slots.wait()
            for which, done in zip(lists, done_refs):
                finish(which(panel_count), done)
        finish(found[start : start + corr.shape[0]], corr)

    products(lists[-1], panel_count, own, panels_ref, table_ref[...], chans, cross, keep)
    for wanted, copy in copies:
        only(wanted, copy.wait)


def last(lists, counts, panel_count, slots, pair, panels, table, stack, *done):
    offsets, chans = stack.shape[0], stack.shape[1]
    whole = pl.BlockSpec(memory_space=pltpu.VMEM)
    rows = counts[-1] * chans * chans
    return pl.pallas_call(
        functools.partial(last_kernel, panel_count, lists),
        out_shape=jax.ShapeDtypeStruct(stack.shape, jnp.float32),
        in_specs=[whole] * (5 + len(done)),
        out_specs=pl.BlockSpec(memory_space=pltpu.HBM),
        scratch_shapes=[
            pltpu.SMEM(slots.shape, jnp.int32),
            pltpu.VMEM((rows, 2 * LANES), jnp.bfloat16),
            pltpu.VMEM((sum(counts), chans, chans, LAGS), jnp.float32),
            pltpu.SemaphoreType.DMA((sum(counts) + 1,)),
        ],
        compiler_params=pltpu.CompilerParams(vmem_limit_bytes=CORR_VMEM),
        cost_estimate=pl.CostEstimate(flops=4 * rows * LANES * COLS, bytes_accessed=4 * rows * COLS, transcendentals=0),
        name=lists[-1].__name__,
    )(slots, pair, panels, table, stack, *done)


def gather_near(own, slots, stack, panel_count):
    chips = panel_count // 2
    def swap(array):
        return lax.ppermute(array, "row", [(i ^ 1, i) for i in range(panel_count)])

    def fetch(array, even, odd):
        ahead = [even, odd]
        moves = []
        for i in range(panel_count):
            c = i // 2
            moves.append((2 * ((c + ahead[i % 2][c % 2]) % chips) + i % 2, i))
        return lax.ppermute(array, "row", moves)

    table = jnp.asarray(lag_table())
    twice = jnp.stack([own, own])
    pair = lax.optimization_barrier(lax.dynamic_update_slice(twice, swap(own)[None], (1, 0, 0)))
    near = fetch(pair, (1, -1), (2, 2))
    next_near = fetch(pair, (-1, 3), (3, 1))
    far = fetch(pair[0], (4, 4), (4, 4))
    chans = stack.shape[1]
    first = early(pair_panels, 2, panel_count, chans, pair, pair, table)
    near, next_near, far, first = lax.optimization_barrier((near, next_near, far, first))
    five = jnp.concatenate([near, next_near, far[None]], axis=0)
    me, chip, core, odd = place(panel_count)
    low = jnp.where((core == 0) & (odd == 1), next_near, near)
    high = jnp.where(core == 0, far[None], next_near)
    swapped = swap(jnp.concatenate([low, high], axis=0))
    second = early(near_panels, 5, panel_count, chans, pair, five, table, stack)
    lists = (pair_panels, near_panels, swapped_panels)
    return last(lists, (2, 5, 4), panel_count, slots, pair, swapped, table, stack, first, second)


def shards(traces, valid_mask, pair_table, stack_in):
    own = whiten(traces, valid_mask)
    panel_count = lax.axis_size("row")
    if pair_table.shape[1] == 10 and panel_count >= 12 and panel_count % 4 == 0:
        return gather_near(own, pair_table, stack_in[0], panel_count)[None]
    return gather_all(own, pair_table, stack_in[0])[None]


def solution(mesh):
    in_specs = (
        P(("parts", "row"), None, None),
        P(("parts", "row"), None),
        P(("parts", "row"), None),
        P(("parts", "row"), None, None, None, None),
    )
    out_specs = P(("parts", "row"), None, None, None, None)
    return jax.shard_map(shards, mesh=mesh, in_specs=in_specs, out_specs=out_specs, check_vma=False)
```

```python
import functools
import math

import jax
import jax.numpy as jnp
import ml_dtypes
import numpy as np
from jax import lax
from jax.experimental import pallas as pl
from jax.experimental.pallas import tpu as pltpu
from jax.sharding import PartitionSpec as P

SAMPLES = 12000
FLO = 6
BINS = 595
SEGS = 2
HALF = 40
LAGS = 401
EPS = 1e-06
WHITEN_VMEM = 60 << 20
CORR_VMEM = 24 << 20
TOGETHER = 5

SPLIT = 20
FOLD = SAMPLES // SPLIT
LANES = 640
RUN = 32
COLS = 512


def bin_at(lane):
    residue = lane // 128 + 5 * (lane % 128 // RUN)
    return residue + SPLIT * (residue < FLO) + SPLIT * (lane % RUN)


BIN_OF = bin_at(np.arange(LANES))
USED = BIN_OF < FLO + BINS
GROUPS = ((1, 4), (2, 3), (0,))


def bf16(a):
    return np.asarray(a, np.float32).astype(ml_dtypes.bfloat16)


def fold_table():
    q = (np.arange(FOLD)[:, None] * BIN_OF[None, :]) % SAMPLES
    angle = 2.0 * np.pi * q / SAMPLES
    cos = np.where(USED, np.cos(angle), 0.0).reshape(FOLD, 5, 1, 128)
    sin = np.where(USED, -np.sin(angle), 0.0).reshape(FOLD, 5, 1, 128)
    table = np.concatenate([cos, sin], axis=2)
    order = [group for some in GROUPS for group in some]
    return bf16(table[:, order].reshape(FOLD, 5 * 256))


def lag_table():
    tau = np.arange(LAGS) - (LAGS - 1) // 2
    q = (BIN_OF[:, None] * tau[None, :]) % SAMPLES
    angle = 2.0 * np.pi * q / SAMPLES
    table = np.zeros((2 * LANES, COLS), np.float64)
    table[:LANES, :LAGS] = np.where(USED[:, None], np.cos(angle), 0.0)
    table[LANES:, :LAGS] = np.where(USED[:, None], -np.sin(angle), 0.0)
    table[LANES - 1, COLS - 1] = 1.0
    return bf16(table)


def cosine(n, of):
    return math.cos(2.0 * math.pi * n / of)


def sine(n, of):
    return math.sin(2.0 * math.pi * n / of)


def ten_point(s):
    e = [s[n] + s[n + 5] for n in range(5)]
    d = [s[n] - s[n + 5] for n in range(5)]
    c1, c2, s1, s2 = cosine(1, 10), cosine(2, 10), sine(1, 10), sine(2, 10)
    e14, e23, f14, f23 = e[1] + e[4], e[2] + e[3], e[1] - e[4], e[2] - e[3]
    d14, d23, g14, g23 = d[1] + d[4], d[2] + d[3], d[1] - d[4], d[2] - d[3]
    y0 = (e[0] + e14 + e23, None)
    y2 = (e[0] + c2 * e14 - c1 * e23, s2 * f14 + s1 * f23)
    y4 = (e[0] - c1 * e14 + c2 * e23, s1 * f14 - s2 * f23)
    y1 = (d[0] + c1 * g14 + c2 * g23, s1 * d14 + s2 * d23)
    y3 = (d[0] - c2 * g14 - c1 * g23, s2 * d14 - s1 * d23)
    y5 = (d[0] - g14 + g23, None)
    return [y0, y1, y2, y3, y4, y5]


def twenty_point(s):
    y = [None] * 11
    y[0::2] = ten_point([s[n] + s[n + 10] for n in range(10)])
    d = [s[n] - s[n + 10] for n in range(10)]
    g1, g2, g3, g4 = (d[n] - d[10 - n] for n in range(1, 5))
    h1, h2, h3, h4 = (d[n] + d[10 - n] for n in range(1, 5))
    for k, turn in ((1, d[5]), (3, -d[5])):
        even = d[0] + cosine(2 * k, 20) * g2 + cosine(4 * k, 20) * g4
        odd = cosine(k, 20) * g1 + cosine(3 * k, 20) * g3
        even_sin = sine(2 * k, 20) * h2 + sine(4 * k, 20) * h4
        odd_sin = sine(k, 20) * h1 + sine(3 * k, 20) * h3 + turn
        y[k] = (even + odd, odd_sin + even_sin)
        y[10 - k] = (even - odd, odd_sin - even_sin)
    y[5] = (d[0] - g2 + g4, h1 - h3 + d[5])
    return y


def hi_lo(y):
    hi = y.astype(jnp.bfloat16)
    return [hi, (y - hi.astype(jnp.float32)).astype(jnp.bfloat16)]


def whiten_kernel(x_hbm, mask_hbm, table_hbm, out_ref, x_buf, mask_buf, table, near, sem):
    chans, minutes, samples = x_buf.shape
    rows = chans * minutes
    starts = (0, 512, 1024, 1280)
    fetch_x = pltpu.make_async_copy(x_hbm, x_buf, sem.at[0])
    fetch_mask = pltpu.make_async_copy(mask_hbm, mask_buf, sem.at[1])
    fetch_table = [
        pltpu.make_async_copy(table_hbm.at[:, pl.ds(a, b - a)], table.at[:, pl.ds(a, b - a)], sem.at[2 + i])
        for i, (a, b) in enumerate(zip(starts, starts[1:]))
    ]
    for copy in [fetch_x, fetch_mask] + fetch_table:
        copy.start()

    down = bin_at(lax.broadcasted_iota(jnp.int32, (LANES, 128), 0))
    down = jnp.where(down < FLO + BINS, down, -SAMPLES)
    lanes = bin_at(lax.broadcasted_iota(jnp.int32, (8, LANES), 1))
    for group in range(5):
        across = jnp.broadcast_to(lanes[:1, group * 128 : (group + 1) * 128], (LANES, 128))
        close = (jnp.abs(down - across) <= HALF) & (across < FLO + BINS)
        near[:, group * 128 : (group + 1) * 128] = jnp.where(close, 1.0, 0.0).astype(jnp.bfloat16)
    bins = lanes[:1]
    count = jnp.minimum(bins + HALF, FLO + BINS - 1) - jnp.maximum(bins - HALF, FLO) + 1
    inverse = 1.0 / jnp.maximum(count, 1).astype(jnp.float32)

    fetch_x.wait()
    x = jnp.swapaxes(x_buf[...], 0, 1).reshape(rows, samples)
    y = twenty_point([x[:, FOLD * n : FOLD * (n + 1)].astype(jnp.float32) for n in range(SPLIT)])
    run = lax.broadcasted_iota(jnp.int32, (rows, 128), 1) // RUN
    for copy in [fetch_mask] + fetch_table:
        copy.wait()
    real = [None] * 5
    imag = [None] * 5
    for part, groups in enumerate(GROUPS):
        wanted = sorted({min(k, SPLIT - k) for g in groups for k in range(g, SPLIT, 5)})
        pieces = [(k, i) for k in wanted for i in range(2) if y[k][i] is not None]
        halves = [hi_lo(y[k][i]) for k, i in pieces]
        left = jnp.concatenate([half[j] for j in range(2) for half in halves], axis=0)
        at = starts[part]
        full = jnp.dot(left, table[:, at : starts[part + 1]], preferred_element_type=jnp.float32)
        got = {
            p: full[rows * i : rows * (i + 1)] + full[rows * (len(pieces) + i) : rows * (len(pieces) + i + 1)]
            for i, p in enumerate(pieces)
        }
        for place, group in enumerate(groups):
            cos = slice(place * 256, place * 256 + 128)
            sin = slice(place * 256 + 128, place * 256 + 256)
            re = im = None
            for q in range(4):
                k = group + 5 * q
                same = min(k, SPLIT - k)
                a = got[(same, 0)]
                r, i = a[:, cos], a[:, sin]
                if (same, 1) in got:
                    b = got[(same, 1)]
                    if k == same:
                        r, i = r + b[:, sin], i - b[:, cos]
                    else:
                        r, i = r - b[:, sin], i + b[:, cos]
                re = r if re is None else jnp.where(run == q, r, re)
                im = i if im is None else jnp.where(run == q, i, im)
            real[group], imag[group] = re, im
    re = jnp.concatenate(real, axis=1)
    im = jnp.concatenate(imag, axis=1)
    power = re * re + im * im
    hi, mid = hi_lo(power)
    low = (power - hi.astype(jnp.float32) - mid.astype(jnp.float32)).astype(jnp.bfloat16)
    sums = jnp.dot(jnp.concatenate([hi, mid, low], axis=0), near[...], preferred_element_type=jnp.float32)
    smooth = (sums[:rows] + sums[rows : 2 * rows] + sums[2 * rows :]) * inverse
    mask = mask_buf[...].astype(jnp.float32)
    spread = jnp.concatenate([jnp.broadcast_to(mask[m : m + 1], (chans, chans)) for m in range(minutes)], axis=0)
    own = lax.broadcasted_iota(jnp.int32, (rows, chans), 0) % chans
    other = lax.broadcasted_iota(jnp.int32, (rows, chans), 1)
    flags = jnp.sum(jnp.where(own == other, spread, 0.0), axis=1, keepdims=True)
    factor = flags * lax.rsqrt(smooth + EPS)
    last = lax.broadcasted_iota(jnp.int32, (rows, LANES), 1) == LANES - 1
    out_ref[:, :LANES] = (re * factor).astype(jnp.bfloat16)
    out_ref[:, LANES:] = jnp.where(last, flags, im * factor).astype(jnp.bfloat16)


def whiten(traces, valid_mask):
    chans, minutes, samples = traces.shape
    rows = chans * minutes
    anywhere = pl.BlockSpec(memory_space=pltpu.HBM)
    return pl.pallas_call(
        whiten_kernel,
        out_shape=pltpu.VMEM((rows, 2 * LANES), jnp.bfloat16),
        in_specs=[anywhere] * 3,
        out_specs=pl.BlockSpec(memory_space=pltpu.VMEM),
        scratch_shapes=[
            pltpu.VMEM((chans, minutes, samples), jnp.bfloat16),
            pltpu.VMEM((minutes, chans), jnp.int32),
            pltpu.VMEM((FOLD, 5 * 256), jnp.bfloat16),
            pltpu.VMEM((LANES, LANES), jnp.bfloat16),
            pltpu.SemaphoreType.DMA((5,)),
        ],
        compiler_params=pltpu.CompilerParams(vmem_limit_bytes=WHITEN_VMEM),
        name="whiten",
    )(traces, valid_mask.T, jnp.asarray(fold_table()))


def cross_tile(own, part, chans, cross, j):
    minutes = own.shape[0] // chans
    for a in range(0, chans, 2):
        both_re, both_im = [], []
        for channel in (a, a + 1):
            re = im = None
            for m in range(minutes):
                row = m * chans + channel
                o_re, o_im = own[row : row + 1, :LANES], own[row : row + 1, LANES:]
                p_re = part[m * chans : (m + 1) * chans, :LANES]
                p_im = part[m * chans : (m + 1) * chans, LANES:]
                r = o_re * p_re + o_im * p_im
                i = o_im * p_re - o_re * p_im
                re = r if re is None else re + r
                im = i if im is None else im + i
            both_re.append(re)
            both_im.append(im)
        rows = slice((j * chans + a) * chans, (j * chans + a + 2) * chans)
        cross[rows, :LANES] = jnp.concatenate(both_re, axis=0).astype(jnp.bfloat16)
        cross[rows, LANES:] = jnp.concatenate(both_im, axis=0).astype(jnp.bfloat16)


def lag_product(cross, table, shape):
    full = jnp.dot(cross, table, preferred_element_type=jnp.float32)
    scale = (1.0 / math.sqrt(BINS)) / jnp.maximum(full[:, COLS - 1 :], 1.0)
    return (full * scale)[:, :LAGS].reshape(shape)


def corr_kernel(pick, slots_ref, panels_ref, lag_ref, stack_ref, out_ref, cross):
    step = pl.program_id(0)
    count, chans = out_ref.shape[0], out_ref.shape[1]
    own = panels_ref[pick(lax.axis_index("row"))].astype(jnp.float32)
    for j in range(count):
        part = panels_ref[pick(slots_ref[0, step * count + j])].astype(jnp.float32)
        cross_tile(own, part, chans, cross, j)
    corr = lag_product(cross[...], lag_ref[...], out_ref.shape)
    out_ref[...] = stack_ref[pl.ds(step * count, count)] + corr


def correlate(pick, slots, panels, stack):
    offsets, chans = stack.shape[0], stack.shape[1]
    chunk = max(d for d in range(1, 7) if offsets % d == 0)
    whole = pl.BlockSpec(memory_space=pltpu.VMEM)
    return pl.pallas_call(
        functools.partial(corr_kernel, pick),
        out_shape=jax.ShapeDtypeStruct(stack.shape, jnp.float32),
        grid_spec=pltpu.PrefetchScalarGridSpec(
            num_scalar_prefetch=1,
            grid=(offsets // chunk,),
            in_specs=[whole, whole, whole],
            out_specs=pl.BlockSpec((chunk, chans, chans, LAGS), lambda i, s: (i, 0, 0, 0)),
            scratch_shapes=[pltpu.VMEM((chunk * chans * chans, panels.shape[2]), jnp.bfloat16)],
        ),
        compiler_params=pltpu.CompilerParams(vmem_limit_bytes=CORR_VMEM),
        name="correlate",
    )(slots, panels, jnp.asarray(lag_table()), stack)


def gather_all(own, slots, stack):
    panels = lax.all_gather(own, "row", axis=0)
    return correlate(lambda j: j, slots, panels, stack)


def place(panel_count):
    me = lax.axis_index("row")
    return me, me // 2, lax.rem(me, 2), lax.rem(me // 2, 2)


def first_hop(panel_count):
    me, chip, core, odd = place(panel_count)
    a = jnp.where(core == 0, chip + 1 - 2 * odd, chip + 2)
    b = jnp.where(core == 0, chip - 1 + 4 * odd, chip + 3 - 2 * odd)
    return a, b


def pair_panels(panel_count):
    me, chip, core, odd = place(panel_count)
    return [(0, me, True), (1, me + 1 - 2 * core, True)]


def near_panels(panel_count):
    me, chip, core, odd = place(panel_count)
    a, b = first_hop(panel_count)
    pairs = [(2 * i + t, 2 * c + (core if t == 0 else 1 - core), True) for i, c in enumerate((a, b)) for t in range(2)]
    for i, here in ((0, odd == 1), (2, odd == 0)):
        pairs[i] = (i, pairs[i][1], (core == 1) | jnp.logical_not(here))
    return pairs + [(4, me + 8, True)]


def swapped_panels(panel_count):
    me, chip, core, odd = place(panel_count)
    found = []
    for t in range(2):
        ahead = jnp.where(core == 0, chip + 2, chip + 1 + 2 * odd)
        found.append((t, 2 * ahead + (1 - core if t == 0 else core), True))
    for t in range(2):
        ahead = 2 * (chip + 3 - 2 * odd) + 1 - t
        wanted = True if t == 0 else core == 0
        found.append((2 + t, jnp.where(core == 0, ahead, 2 * chip + 8), wanted))
    return found


def products(which, panel_count, own, panels_ref, table, chans, cross, keep):
    found = which(panel_count)
    for start in range(0, len(found), TOGETHER):
        some = found[start : start + TOGETHER]
        for j, (at, panel, wanted) in enumerate(some):
            cross_tile(own, panels_ref[at].astype(jnp.float32), chans, cross, start + j)
        rows = slice(start * chans * chans, (start + len(some)) * chans * chans)
        full = jnp.dot(cross[rows], table, preferred_element_type=jnp.float32)
        scale = (1.0 / math.sqrt(BINS)) / jnp.maximum(full[:, COLS - 1 :], 1.0)
        keep(start, (full * scale).reshape(len(some), chans * chans, COLS))


def early_kernel(panel_count, which, pair_ref, panels_ref, table_ref, *refs):
    out_ref, cross = refs[-2:]
    own = pair_ref[0].astype(jnp.float32)

    def keep(start, corr):
        out_ref[start : start + corr.shape[0]] = corr

    products(which, panel_count, own, panels_ref, table_ref[...], own.shape[0] // SEGS, cross, keep)


def early(which, count, panel_count, chans, pair, panels, table, *held):
    whole = pl.BlockSpec(memory_space=pltpu.VMEM)
    rows = count * chans * chans
    return pl.pallas_call(
        functools.partial(early_kernel, panel_count, which),
        out_shape=jax.ShapeDtypeStruct((count, chans * chans, COLS), jnp.float32),
        in_specs=[whole] * (3 + len(held)),
        out_specs=whole,
        scratch_shapes=[pltpu.VMEM((rows, 2 * LANES), jnp.bfloat16)],
        compiler_params=pltpu.CompilerParams(vmem_limit_bytes=CORR_VMEM),
        cost_estimate=pl.CostEstimate(flops=4 * rows * LANES * COLS, bytes_accessed=4 * rows * COLS, transcendentals=0),
        name=which.__name__,
    )(pair, panels, table, *held)


def last_kernel(panel_count, lists, slots_any, pair_ref, panels_ref, table_ref, stack_ref, *refs):
    done_refs = refs[: len(lists) - 1]
    out_ref, slots_ref, cross, result, sem = refs[len(lists) - 1 :]
    offsets, chans = stack_ref.shape[0], stack_ref.shape[1]
    fetch_slots = pltpu.make_async_copy(slots_any, slots_ref, sem.at[sem.shape[0] - 1])
    fetch_slots.start()
    own = pair_ref[0].astype(jnp.float32)
    copies = []

    def only(wanted, act):
        if wanted is True:
            act()
        else:
            pl.when(wanted)(act)

    def finish(found, corr):
        for j, (at, panel, wanted) in enumerate(found):
            panel = lax.rem(panel + panel_count, panel_count)
            slot = jnp.int32(0)
            for o in range(1, offsets):
                slot = jnp.where(slots_ref[0, o] == panel, o, slot)
            n = len(copies)
            result[n] = stack_ref[slot] + corr[j][:, :LAGS].reshape(chans, chans, LAGS)
            copy = pltpu.make_async_copy(result.at[n], out_ref.at[slot], sem.at[n])
            copies.append((wanted, copy))
            only(wanted, copy.start)

    found = lists[-1](panel_count)

    def keep(start, corr):
        if start == 0:
            fetch_slots.wait()
            for which, done in zip(lists, done_refs):
                finish(which(panel_count), done)
        finish(found[start : start + corr.shape[0]], corr)

    products(lists[-1], panel_count, own, panels_ref, table_ref[...], chans, cross, keep)
    for wanted, copy in copies:
        only(wanted, copy.wait)


def last(lists, counts, panel_count, slots, pair, panels, table, stack, *done):
    offsets, chans = stack.shape[0], stack.shape[1]
    whole = pl.BlockSpec(memory_space=pltpu.VMEM)
    rows = counts[-1] * chans * chans
    return pl.pallas_call(
        functools.partial(last_kernel, panel_count, lists),
        out_shape=jax.ShapeDtypeStruct(stack.shape, jnp.float32),
        in_specs=[whole] * (5 + len(done)),
        out_specs=pl.BlockSpec(memory_space=pltpu.HBM),
        scratch_shapes=[
            pltpu.SMEM(slots.shape, jnp.int32),
            pltpu.VMEM((rows, 2 * LANES), jnp.bfloat16),
            pltpu.VMEM((sum(counts), chans, chans, LAGS), jnp.float32),
            pltpu.SemaphoreType.DMA((sum(counts) + 1,)),
        ],
        compiler_params=pltpu.CompilerParams(vmem_limit_bytes=CORR_VMEM),
        cost_estimate=pl.CostEstimate(flops=4 * rows * LANES * COLS, bytes_accessed=4 * rows * COLS, transcendentals=0),
        name=lists[-1].__name__,
    )(slots, pair, panels, table, stack, *done)


def gather_near(own, slots, stack, panel_count):
    chips = panel_count // 2
    def swap(array):
        return lax.ppermute(array, "row", [(i ^ 1, i) for i in range(panel_count)])

    def fetch(array, even, odd):
        ahead = [even, odd]
        moves = []
        for i in range(panel_count):
            c = i // 2
            moves.append((2 * ((c + ahead[i % 2][c % 2]) % chips) + i % 2, i))
        return lax.ppermute(array, "row", moves)

    table = jnp.asarray(lag_table())
    twice = jnp.stack([own, own])
    pair, own = lax.optimization_barrier((lax.dynamic_update_slice(twice, swap(own)[None], (1, 0, 0)), own))
    near = fetch(pair, (1, -1), (2, 2))
    next_near = fetch(pair, (-1, 3), (3, 1))
    far = fetch(own, (4, 4), (4, 4))
    chans = stack.shape[1]
    first = early(pair_panels, 2, panel_count, chans, pair, pair, table)
    near, next_near, far, first = lax.optimization_barrier((near, next_near, far, first))
    five = jnp.concatenate([near, next_near, far[None]], axis=0)
    me, chip, core, odd = place(panel_count)
    low = jnp.where((core == 0) & (odd == 1), next_near, near)
    high = jnp.where(core == 0, far[None], next_near)
    swapped = swap(jnp.concatenate([low, high], axis=0))
    second = early(near_panels, 5, panel_count, chans, pair, five, table, stack)
    lists = (pair_panels, near_panels, swapped_panels)
    return last(lists, (2, 5, 4), panel_count, slots, pair, swapped, table, stack, first, second)


def shards(traces, valid_mask, pair_table, stack_in):
    own = whiten(traces, valid_mask)
    panel_count = lax.axis_size("row")
    if pair_table.shape[1] == 10 and panel_count >= 12 and panel_count % 4 == 0:
        return gather_near(own, pair_table, stack_in[0], panel_count)[None]
    return gather_all(own, pair_table, stack_in[0])[None]


def solution(mesh):
    in_specs = (
        P(("parts", "row"), None, None),
        P(("parts", "row"), None),
        P(("parts", "row"), None),
        P(("parts", "row"), None, None, None, None),
    )
    out_specs = P(("parts", "row"), None, None, None, None)
    return jax.shard_map(shards, mesh=mesh, in_specs=in_specs, out_specs=out_specs, check_vma=False)
```
